512 devices in a mesh: ex: 64 (over y, z_hi, core), feat: 8 (over x, z_lo).
Axes of the slice: x: 4, y: 8, z: 8 (z_hi: 4, z_lo: 2; z = z_hi * 2 + z_lo), core: 2. Of those that a mesh axis runs over, the one named last changes fastest.
Arguments:
- proj_inputs: bfloat16 [2, 2048, 24, 2048], P(None, 'ex', None, 'feat'), may hold values from -6 to 6
- out_cotangent: bfloat16 [2, 2048, 24, 4096], P(None, 'ex', None, 'feat'), may hold values from -200 to 200
- seq_lengths: int32 [2048], P('ex'), may hold values from 6 to 24, as said below
- frozen_adapter: bfloat16 [2, 128, 2048], P(None, None, 'feat'), may hold values from -0.125 to 0.125
- left_factor: bfloat16 [2, 512, 4096], P(None, None, 'feat'), may hold values from -0.09375 to 0.09375
- right_factor: bfloat16 [2, 128, 16], replicated, may hold values from -0.5 to 0.5
- valid_grads: bfloat16 [256, 8192], P('ex', 'feat'), may hold values from -200 to 200
Outputs:
- scores: float32 [2048, 256], P('ex')
The draws below stay inside these ranges and needn't reach their ends.
Inputs may be any that keep to these rules, and one draw needn't show every extreme that they name: Tokens at positions below seq_lengths are live; in every aligned block of 32 examples one example has all 24 tokens live and one has the fewest allowed.
All inputs are finite; a program needn't handle non-finite values.
Results may differ from the reference program's by a relative error of at most 0.0037.
Values may be sent and summed in bfloat16 or wider, within the bound.
No kernel may reach another device: no remote copies, remote signals or barrier semaphores. Data moves between devices by JAX's collectives and lax.ppermute only.
A program may use at most 64 MiB of HBM per device.

```python
import math
import jax
import jax.numpy as jnp
from jax import lax

D = 4096
HW = 2048
R = 128
KL = 512
KR = 16
LAYERS = 2
NV = 256
SEQ = 24
EXG = 32
EXAMPLES = 2048
N_EX = 64


def spread_factor(key, shape, lowest, highest):
    return jnp.exp(jax.random.uniform(key, shape, jnp.float32, math.log(lowest), math.log(highest)))


def rough_values(key, shape):
    return jnp.clip(jax.random.normal(jax.random.fold_in(key, 13), shape, jnp.float32), -6.0, 6.0)


def draw_out_cotangent(key, part):
    shape = (LAYERS, EXAMPLES, SEQ, D)
    base = rough_values(jax.random.fold_in(key, 1), shape)
    row_scale = spread_factor(jax.random.fold_in(key, 2), (LAYERS, EXAMPLES, 1, 1), 1.0, 10.0)
    column_scale = spread_factor(jax.random.fold_in(key, 3), (LAYERS, 1, 1, D), 0.3, 3.0)
    return (base * row_scale * column_scale).astype(jnp.bfloat16)


def draw_valid_grads(key, part):
    shape = (NV, KL * KR)
    base = rough_values(jax.random.fold_in(key, 4), shape)
    row_scale = spread_factor(jax.random.fold_in(key, 5), (NV, 1), 1.0, 10.0)
    column_scale = spread_factor(jax.random.fold_in(key, 6), (1, KL * KR), 0.3, 3.0)
    return (base * row_scale * column_scale).astype(jnp.bfloat16)


def draw_seq_lengths(key, part):
    shortest = max(1, SEQ // 4)
    blocks = EXAMPLES // EXG
    sampled = jax.random.randint(jax.random.fold_in(key, 7), (EXAMPLES,), shortest, SEQ + 1, dtype=jnp.int32)
    chosen = jax.random.randint(jax.random.fold_in(key, 8), (blocks,), 0, EXG, dtype=jnp.int32)
    position = jnp.arange(EXAMPLES, dtype=jnp.int32)
    within = position % EXG
    picked = jnp.repeat(chosen, EXG)
    sampled = jnp.where(within == picked, SEQ, sampled)
    return jnp.where(within == (picked + 1) % EXG, shortest, sampled).astype(jnp.int32)


def level_of(stream_key, dims, pieces, least, high):
    factor_of = 1.0
    for dim, parts in pieces:
        heights = jax.random.uniform(jax.random.fold_in(jax.random.fold_in(stream_key, 6), dim), (parts,), jnp.float32, least / len(pieces), high / len(pieces))
        factor_of = factor_of * jnp.repeat(jnp.exp(heights), dims[dim] // parts).reshape((-1,) + (1,) * (len(dims) - 1 - dim))
    return factor_of


def gaussian(rng, shape, scale, limit, cuts=(), kind=jnp.bfloat16):
    result = jax.random.normal(rng, shape, jnp.float32) * scale
    if len(cuts) > 0:
        result = level_of(rng, shape, cuts, -0.22, 0.18) * result
    return jnp.clip(result, min=-limit, max=limit).astype(kind)


def setup_inputs(seed: int = 0) -> dict:
    keys = jax.random.split(jax.random.key(seed), 8)
    proj_inputs = gaussian(keys[0], (LAYERS, EXAMPLES, SEQ, HW), 1.0, 6.0, ((1, 64), (3, 8)))
    out_cotangent = draw_out_cotangent(jax.random.fold_in(keys[7], 71), 0)
    seq_lengths = draw_seq_lengths(jax.random.fold_in(keys[7], 71), 0)
    frozen_adapter = gaussian(keys[3], (LAYERS, R, HW), HW ** -0.5, 0.125, ((2, 8),))
    left_factor = gaussian(keys[4], (LAYERS, KL, D), D ** -0.5, 0.09375, ((2, 8),))
    right_factor = gaussian(keys[5], (LAYERS, R, KR), R ** -0.5, 0.5)
    valid_grads = draw_valid_grads(jax.random.fold_in(keys[7], 71), 0)
    return {"proj_inputs": proj_inputs, "out_cotangent": out_cotangent, "seq_lengths": seq_lengths, "frozen_adapter": frozen_adapter, "left_factor": left_factor, "right_factor": right_factor, "valid_grads": valid_grads}


def reference(proj_inputs, out_cotangent, seq_lengths, frozen_adapter, left_factor, right_factor, valid_grads):
    highest = lax.Precision.HIGHEST
    adapter_wide = frozen_adapter.astype(jnp.float32)
    right_wide = right_factor.astype(jnp.float32)
    left_wide = left_factor.astype(jnp.float32)
    position = jnp.arange(SEQ, dtype=jnp.int32)

    def one_group(group):
        first_row = (group * EXG).astype(jnp.int32)
        inputs_group = lax.dynamic_slice_in_dim(proj_inputs, first_row, EXG, 1).astype(jnp.float32)
        cotan_group = lax.dynamic_slice_in_dim(out_cotangent, first_row, EXG, 1).astype(jnp.float32)
        length_group = lax.dynamic_slice_in_dim(seq_lengths, first_row, EXG, 0)
        live_tokens = (position[None, :] < length_group[:, None]).astype(jnp.float32)
        adapted = jnp.einsum('lesh,lrh->lesr', inputs_group, adapter_wide, precision=highest)
        right_rows = jnp.einsum('lesr,lrb->lesb', adapted, right_wide, precision=highest)
        right_rows = (right_rows * live_tokens[None, :, :, None]).astype(jnp.bfloat16)
        left_rows = jnp.einsum('lkd,lesd->lkes', left_wide, cotan_group, precision=highest)
        projected = jnp.einsum('lkes,lesb->ekb', left_rows, right_rows.astype(jnp.float32), precision=highest)
        return projected.reshape(EXG, KL * KR)
    projected = lax.map(one_group, jnp.arange(N_EX, dtype=jnp.int32)).reshape(EXAMPLES, KL * KR)
    train_norm = jnp.sqrt(lax.optimization_barrier(jnp.sum(projected * projected, axis=1)) + 1e-06)
    valid_wide = valid_grads.astype(jnp.float32)
    valid_norm = jnp.sqrt(lax.optimization_barrier(jnp.sum(valid_wide * valid_wide, axis=1)) + 1e-06)
    rounded = projected.astype(jnp.bfloat16)
    products = jnp.dot(rounded, valid_grads.T, preferred_element_type=jnp.float32)
    return math.sqrt(KL * KR) * products / (train_norm[:, None] * valid_norm[None, :])
```

```python
import math

import jax
import jax.numpy as jnp
from jax import lax
from jax.experimental import pallas as pl
from jax.experimental.pallas import tpu as pltpu
from jax.sharding import PartitionSpec as P

F32 = jnp.float32
BF16 = jnp.bfloat16
GROUP = 4
NT = (((1,), (1,)), ((), ()))
NN = (((1,), (0,)), ((), ()))
TN = (((0,), (0,)), ((), ()))


def dot(a, b, dims):
    return lax.dot_general(a, b, dims, preferred_element_type=F32)


def split(x):
    high = x.astype(BF16)
    return high, (x - high.astype(F32)).astype(BF16)


def call(kernel, out_shape, flops, bytes_accessed, name, scratch=(), smem=0, args=()):
    specs = [pl.BlockSpec(memory_space=pltpu.SMEM)] * smem
    specs += [pl.BlockSpec(memory_space=pltpu.VMEM)] * (len(args) - smem)
    return pl.pallas_call(
        kernel,
        out_shape=out_shape,
        in_specs=specs,
        out_specs=jax.tree.map(lambda _: pl.BlockSpec(memory_space=pltpu.VMEM), out_shape),
        scratch_shapes=list(scratch),
        cost_estimate=pl.CostEstimate(flops=flops, bytes_accessed=bytes_accessed, transcendentals=0),
        name=name,
    )(*args)


def right_kernel(x_ref, a_ref, r_ref, out_ref):
    peers = out_ref.shape[0]
    layers = x_ref.shape[0]
    proj = r_ref.shape[2]
    for l in range(layers):
        mix = dot(r_ref[l], a_ref[l], TN)
        high, low = split(mix)
        both = jnp.concatenate([high, low], axis=0)
        rows = dot(both, x_ref[l], NT)
        rows = (rows[:proj] + rows[proj:]).astype(BF16)
        for p in range(peers):
            out_ref[p, l * proj:(l + 1) * proj, :] = rows


def left_kernel(c_ref, l_ref, high_ref, low_ref):
    layers, tokens, _ = c_ref.shape
    step = 256
    for l in range(layers):
        for t in range(0, tokens, step):
            high, low = split(dot(c_ref[l, t:t + step, :], l_ref[l], NT))
            high_ref[l, t:t + step, :] = high
            low_ref[l, t:t + step, :] = low


def project_kernel(seq_ref, rr_ref, high_ref, low_ref, out_ref):
    peers, two_proj, tokens = rr_ref.shape
    layers, _, kl = high_ref.shape
    proj = two_proj // layers
    half = proj // 2
    owned = kl // peers
    examples = seq_ref.shape[0]
    seq = tokens // examples
    span = GROUP * seq
    width = 2 * 128
    total = rr_ref[0].astype(F32)
    for p in range(1, peers):
        total = total + rr_ref[p].astype(F32)
    first = total[:proj]
    second = total[proj:]
    lane = lax.broadcasted_iota(jnp.int32, (proj, width), 1)
    out_lane = lax.broadcasted_iota(jnp.int32, (GROUP * half, 128), 1)
    for g in range(examples // GROUP):
        x0 = first if g == 0 else pltpu.roll(first, (tokens - g * span) % tokens, 1)
        x1 = pltpu.roll(second, (tokens + span - g * span) % tokens, 1)
        x0, x1 = x0[:, :width], x1[:, :width]
        blocks = []
        for i in range(GROUP):
            start = i * seq
            stop = start + seq_ref[g * GROUP + i]
            mask0 = (lane >= start) & (lane < stop)
            mask1 = (lane >= start + span) & (lane < stop + span)
            blocks.append(jnp.where(mask0, x0, jnp.where(mask1, x1, 0.0)))
        spread = jnp.concatenate(blocks, axis=0)
        high, low = split(spread)
        both = jnp.concatenate([high, low], axis=0)[:, :layers * span]
        high = high[:, :layers * span]
        t = g * span
        left_high = jnp.concatenate([high_ref[l, t:t + span, :] for l in range(layers)], axis=0)
        left_low = jnp.concatenate([low_ref[l, t:t + span, :] for l in range(layers)], axis=0)
        rows = GROUP * proj
        part = dot(both, left_high, NN)
        part = part[:rows] + part[rows:] + dot(high, left_low, NN)
        part = part.reshape(GROUP, 2, half, kl)
        even = part[:, 0].reshape(GROUP * half, kl)
        odd = part[:, 1].reshape(GROUP * half, kl)
        for p in range(peers):
            tile = (p * owned) // 128 * 128
            e = even[:, tile:tile + 128]
            o = odd[:, tile:tile + 128]
            if (p * owned) % 128 == 0:
                o = pltpu.roll(o, 64, 1)
            else:
                e = pltpu.roll(e, 64, 1)
            both_k = jnp.where(out_lane < 64, e, o)
            r = g * GROUP * half
            out_ref[p, r:r + GROUP * half, :] = both_k.astype(BF16)


def product_kernel(part_ref, valid_ref, squares_ref, out_ref, sum_ref):
    peers, rows, _ = part_ref.shape
    valid_count = valid_ref.shape[0]
    examples = rows // 8
    total = part_ref[0].astype(F32)
    for p in range(1, peers):
        total = total + part_ref[p].astype(F32)
    sum_ref[...] = total
    squares = jnp.sum((total * total).reshape(examples, 8, 128), axis=1)
    squares = jnp.sum(squares, axis=1, keepdims=True)
    row = lax.broadcasted_iota(jnp.int32, (examples, valid_count), 0)
    column = lax.broadcasted_iota(jnp.int32, (examples, valid_count), 1)
    train = jnp.sum(jnp.where(row == column, squares, 0.0), axis=0, keepdims=True)
    acc = jnp.zeros((2 * examples, valid_count), F32)
    for b in range(8):
        block = sum_ref[pl.ds(b, examples, stride=8), :]
        high, low = split(block)
        both = jnp.concatenate([high, low], axis=0)
        acc = acc + dot(both, valid_ref[:, b * 128:(b + 1) * 128], NT)
    products = acc[:examples] + acc[examples:]
    tail_row = lax.broadcasted_iota(jnp.int32, (8, valid_count), 0)
    tail = jnp.where(tail_row == 0, squares_ref[...], jnp.where(tail_row == 1, train, 0.0))
    for p in range(peers):
        out_ref[p, :examples, :] = products
        out_ref[p, examples:, :] = tail


def score_kernel(scaling, part_ref, out_ref):
    peers = part_ref.shape[0]
    examples, valid_count = out_ref.shape
    total = part_ref[0]
    for p in range(1, peers):
        total = total + part_ref[p]
    products = total[:examples]
    valid = jnp.sqrt(total[examples:examples + 1] + 1e-06)
    row = lax.broadcasted_iota(jnp.int32, (examples, valid_count), 0)
    column = lax.broadcasted_iota(jnp.int32, (examples, valid_count), 1)
    train = jnp.where(row == column, total[examples + 1:examples + 2], 0.0)
    train = jnp.sqrt(jnp.sum(train, axis=1, keepdims=True) + 1e-06)
    out_ref[...] = scaling * products / (train * valid)


def body(proj_inputs, out_cotangent, seq_lengths, frozen_adapter, left_factor, right_factor, valid_grads):
    layers, examples, seq, inputs = proj_inputs.shape
    width = out_cotangent.shape[3]
    peers = lax.axis_size("feat")
    groups = lax.axis_size("ex")
    proj = right_factor.shape[2]
    kl = left_factor.shape[1]
    tokens = examples * seq
    owned = kl // peers
    valid_count = valid_grads.shape[0] * groups
    scaling = math.sqrt(kl * proj)

    own_valid = valid_grads.reshape(-1, owned, 2, 8).transpose(0, 3, 2, 1).reshape(1, -1, owned * proj)
    own_valid = jnp.broadcast_to(own_valid, (groups,) + own_valid.shape[1:])
    valid = lax.all_to_all(own_valid, "ex", 0, 0, tiled=True).reshape(valid_count, owned * proj)
    valid_wide = valid.astype(F32)
    valid_squares = jnp.sum(valid_wide * valid_wide, axis=1)[None, :]

    right_parts = call(
        right_kernel,
        jax.ShapeDtypeStruct((peers, layers * proj, tokens), BF16),
        2 * layers * tokens * inputs * 256,
        proj_inputs.size * 2,
        "right_rows",
        args=(proj_inputs.reshape(layers, tokens, inputs), frozen_adapter, right_factor),
    )
    right_parts = lax.all_to_all(right_parts, "feat", 0, 0, tiled=True)

    left_shape = jax.ShapeDtypeStruct((layers, tokens, kl), BF16)
    left_high, left_low = call(
        left_kernel,
        (left_shape, left_shape),
        2 * layers * tokens * width * kl,
        (out_cotangent.size + left_factor.size) * 2 + layers * tokens * kl * 4,
        "left_rows",
        args=(out_cotangent.reshape(layers, tokens, width), left_factor),
    )
    parts = call(
        project_kernel,
        jax.ShapeDtypeStruct((peers, examples * 8, 128), BF16),
        2 * layers * tokens * kl * 256,
        layers * tokens * kl * 4,
        "project",
        smem=1,
        args=(seq_lengths, right_parts, left_high, left_low),
    )
    parts = lax.all_to_all(parts, "feat", 0, 0, tiled=True)
    products = call(
        product_kernel,
        jax.ShapeDtypeStruct((peers, examples + 8, valid_count), F32),
        4 * examples * valid_count * owned * proj,
        parts.size * 2 + valid.size * 2,
        "products",
        scratch=(pltpu.VMEM((examples * 8, 128), F32),),
        args=(parts, valid, valid_squares),
    )
    products = lax.all_to_all(products, "feat", 0, 0, tiled=True)

    def score(part_ref, out_ref):
        score_kernel(scaling, part_ref, out_ref)

    return call(
        score,
        jax.ShapeDtypeStruct((examples, valid_count), F32),
        examples * valid_count * 16,
        products.size * 4,
        "scores",
        args=(products,),
    )


def solution(mesh):
    return jax.shard_map(
        body,
        mesh=mesh,
        in_specs=(
            P(None, "ex", None, "feat"),
            P(None, "ex", None, "feat"),
            P("ex"),
            P(None, None, "feat"),
            P(None, None, "feat"),
            P(),
            P("ex", "feat"),
        ),
        out_specs=P("ex", None),
        check_vma=False,
    )
```

```python
import math

import jax
import jax.numpy as jnp
from jax import lax
from jax.experimental import pallas as pl
from jax.experimental.pallas import tpu as pltpu
from jax.sharding import PartitionSpec as P

F32 = jnp.float32
BF16 = jnp.bfloat16
VMEM_LIMIT = 24 << 20
GROUP = 4
NT = (((1,), (1,)), ((), ()))
NN = (((1,), (0,)), ((), ()))
TN = (((0,), (0,)), ((), ()))


def dot(a, b, dims):
    return lax.dot_general(a, b, dims, preferred_element_type=F32)


def split(x):
    high = x.astype(BF16)
    return high, (x - high.astype(F32)).astype(BF16)


def on_chip(x):
    return pltpu.with_memory_space_constraint(x, pltpu.VMEM)


def call(kernel, out_shape, flops, bytes_accessed, name, scratch=(), smem=0, args=()):
    specs = [pl.BlockSpec(memory_space=pltpu.SMEM)] * smem
    specs += [pl.BlockSpec(memory_space=pltpu.VMEM)] * (len(args) - smem)
    return pl.pallas_call(
        kernel,
        out_shape=out_shape,
        in_specs=specs,
        out_specs=jax.tree.map(
            lambda _: pl.BlockSpec(memory_space=pltpu.VMEM), out_shape, is_leaf=lambda x: hasattr(x, "shape")
        ),
        scratch_shapes=list(scratch),
        cost_estimate=pl.CostEstimate(flops=flops, bytes_accessed=bytes_accessed, transcendentals=0),
        compiler_params=pltpu.CompilerParams(vmem_limit_bytes=VMEM_LIMIT),
        name=name,
    )(*args)


def right_kernel(x_ref, a_ref, r_ref, out_ref):
    peers = out_ref.shape[0]
    layers = x_ref.shape[0]
    proj = r_ref.shape[1]
    for l in range(layers):
        mix = dot(r_ref[l], a_ref[l], NN)
        high, low = split(mix)
        both = jnp.concatenate([high, low], axis=0)
        rows = dot(both, x_ref[l], NT)
        rows = (rows[:proj] + rows[proj:]).astype(BF16)
        for p in range(peers):
            out_ref[p, l * proj:(l + 1) * proj, :] = rows


def left_kernel(c_ref, l_ref, high_ref, low_ref):
    layers, tokens, _ = c_ref.shape
    step = 256
    for l in range(layers):
        for t in range(0, tokens, step):
            high, low = split(dot(c_ref[l, t:t + step, :], l_ref[l], NT))
            high_ref[l, t:t + step, :] = high
            low_ref[l, t:t + step, :] = low


def project_kernel(seq_ref, rr_ref, high_ref, low_ref, out_ref):
    peers, two_proj, tokens = rr_ref.shape
    layers, _, kl = high_ref.shape
    proj = two_proj // layers
    half = proj // 2
    owned = kl // peers
    examples = seq_ref.shape[0]
    seq = tokens // examples
    span = GROUP * seq
    width = 2 * 128
    total = rr_ref[0].astype(F32)
    for p in range(1, peers):
        total = total + rr_ref[p].astype(F32)
    first = total[:proj]
    second = total[proj:]
    lane = lax.broadcasted_iota(jnp.int32, (proj, width), 1)
    out_lane = lax.broadcasted_iota(jnp.int32, (GROUP * half, 128), 1)
    for g in range(examples // GROUP):
        x0 = first if g == 0 else pltpu.roll(first, (tokens - g * span) % tokens, 1)
        x1 = pltpu.roll(second, (tokens + span - g * span) % tokens, 1)
        x0, x1 = x0[:, :width], x1[:, :width]
        blocks = []
        for i in range(GROUP):
            start = i * seq
            stop = start + seq_ref[g * GROUP + i]
            mask0 = (lane >= start) & (lane < stop)
            mask1 = (lane >= start + span) & (lane < stop + span)
            blocks.append(jnp.where(mask0, x0, jnp.where(mask1, x1, 0.0)))
        spread = jnp.concatenate(blocks, axis=0)
        high, low = split(spread)
        both = jnp.concatenate([high, low], axis=0)[:, :layers * span]
        high = high[:, :layers * span]
        t = g * span
        left_high = jnp.concatenate([high_ref[l, t:t + span, :] for l in range(layers)], axis=0)
        left_low = jnp.concatenate([low_ref[l, t:t + span, :] for l in range(layers)], axis=0)
        rows = GROUP * proj
        part = dot(both, left_high, NN)
        part = part[:rows] + part[rows:] + dot(high, left_low, NN)
        part = part.reshape(GROUP, 2, half, kl)
        even = part[:, 0].reshape(GROUP * half, kl)
        odd = part[:, 1].reshape(GROUP * half, kl)
        for p in range(peers):
            tile = (p * owned) // 128 * 128
            e = even[:, tile:tile + 128]
            o = odd[:, tile:tile + 128]
            if (p * owned) % 128 == 0:
                o = pltpu.roll(o, 64, 1)
            else:
                e = pltpu.roll(e, 64, 1)
            both_k = jnp.where(out_lane < 64, e, o)
            r = g * GROUP * half
            out_ref[p, r:r + GROUP * half, :] = both_k.astype(BF16)


def product_kernel(part_ref, valid_ref, out_ref, sum_ref):
    peers, rows, _ = part_ref.shape
    valid_count = valid_ref.shape[0]
    examples = rows // 8
    total = part_ref[0].astype(F32)
    for p in range(1, peers):
        total = total + part_ref[p].astype(F32)
    sum_ref[...] = total
    squares = jnp.sum((total * total).reshape(examples, 8, 128), axis=1)
    squares = jnp.sum(squares, axis=1, keepdims=True)
    row = lax.broadcasted_iota(jnp.int32, (examples, valid_count), 0)
    column = lax.broadcasted_iota(jnp.int32, (examples, valid_count), 1)
    train = jnp.sum(jnp.where(row == column, squares, 0.0), axis=0, keepdims=True)
    acc = jnp.zeros((2 * examples, valid_count), F32)
    valid_squares = jnp.zeros((valid_count, 128), F32)
    for b in range(8):
        block = sum_ref[pl.ds(b, examples, stride=8), :]
        high, low = split(block)
        both = jnp.concatenate([high, low], axis=0)
        valid = valid_ref[:, b * 128:(b + 1) * 128]
        valid_squares = valid_squares + valid * valid
        acc = acc + dot(both, valid.astype(BF16), NT)
    products = acc[:examples] + acc[examples:]
    valid_squares = jnp.sum(valid_squares.T, axis=0, keepdims=True)
    tail_row = lax.broadcasted_iota(jnp.int32, (8, valid_count), 0)
    tail = jnp.where(tail_row == 0, valid_squares, jnp.where(tail_row == 1, train, 0.0))
    for p in range(peers):
        out_ref[p, :examples, :] = products
        out_ref[p, examples:, :] = tail


def score_kernel(scaling, part_ref, out_ref):
    peers = part_ref.shape[0]
    examples, valid_count = out_ref.shape
    total = part_ref[0]
    for p in range(1, peers):
        total = total + part_ref[p]
    products = total[:examples]
    valid = jnp.sqrt(total[examples:examples + 1] + 1e-06)
    row = lax.broadcasted_iota(jnp.int32, (examples, valid_count), 0)
    column = lax.broadcasted_iota(jnp.int32, (examples, valid_count), 1)
    train = jnp.where(row == column, total[examples + 1:examples + 2], 0.0)
    train = jnp.sqrt(jnp.sum(train, axis=1, keepdims=True) + 1e-06)
    out_ref[...] = scaling * products / (train * valid)


def body(proj_inputs, out_cotangent, seq_lengths, frozen_adapter, left_factor, right_factor, valid_grads):
    layers, examples, seq, inputs = proj_inputs.shape
    width = out_cotangent.shape[3]
    peers = lax.axis_size("feat")
    groups = lax.axis_size("ex")
    proj = right_factor.shape[2]
    kl = left_factor.shape[1]
    tokens = examples * seq
    owned = kl // peers
    valid_count = valid_grads.shape[0] * groups
    scaling = math.sqrt(kl * proj)

    own_valid = valid_grads.reshape(-1, owned, 2, 8).transpose(0, 3, 2, 1).reshape(1, -1, owned * proj)
    valid = lax.all_gather(lax.optimization_barrier(own_valid.astype(F32))[0], "ex", axis=0, tiled=True)

    right_parts = call(
        right_kernel,
        pltpu.VMEM((peers, layers * proj, tokens), BF16),
        2 * layers * tokens * inputs * 256,
        proj_inputs.size * 2,
        "right_rows",
        args=(proj_inputs.reshape(layers, tokens, inputs), frozen_adapter, right_factor.swapaxes(1, 2)),
    )
    right_parts = lax.all_to_all(right_parts, "feat", 0, 0, tiled=True)

    left_shape = pltpu.VMEM((layers, tokens, kl), BF16)
    left_high, left_low = call(
        left_kernel,
        (left_shape, left_shape),
        2 * layers * tokens * width * kl,
        (out_cotangent.size + left_factor.size) * 2 + layers * tokens * kl * 4,
        "left_rows",
        args=(out_cotangent.reshape(layers, tokens, width), left_factor),
    )
    parts = call(
        project_kernel,
        pltpu.VMEM((peers, examples * 8, 128), BF16),
        2 * layers * tokens * kl * 256,
        layers * tokens * kl * 4,
        "project",
        smem=1,
        args=(seq_lengths, on_chip(right_parts), on_chip(left_high), on_chip(left_low)),
    )
    parts = lax.all_to_all(parts, "feat", 0, 0, tiled=True)
    products = call(
        product_kernel,
        pltpu.VMEM((peers, examples + 8, valid_count), F32),
        4 * examples * valid_count * owned * proj,
        parts.size * 2 + valid.size * 2,
        "products",
        scratch=(pltpu.VMEM((examples * 8, 128), F32),),
        args=(on_chip(parts), on_chip(valid)),
    )
    products = lax.all_to_all(products, "feat", 0, 0, tiled=True)

    def score(part_ref, out_ref):
        score_kernel(scaling, part_ref, out_ref)

    return call(
        score,
        jax.ShapeDtypeStruct((examples, valid_count), F32),
        examples * valid_count * 16,
        products.size * 4,
        "scores",
        args=(on_chip(products),),
    )


def solution(mesh):
    return jax.shard_map(
        body,
        mesh=mesh,
        in_specs=(
            P(None, "ex", None, "feat"),
            P(None, "ex", None, "feat"),
            P("ex"),
            P(None, None, "feat"),
            P(None, None, "feat"),
            P(),
            P("ex", "feat"),
        ),
        out_specs=P("ex", None),
        check_vma=False,
    )
```

```python
import math

import jax
import jax.numpy as jnp
from jax import lax
from jax.experimental import pallas as pl
from jax.experimental.pallas import tpu as pltpu
from jax.sharding import PartitionSpec as P


F32 = jnp.float32
BF16 = jnp.bfloat16
VMEM_LIMIT = 24 << 20
GROUP = 4
NT = (((1,), (1,)), ((), ()))
NN = (((1,), (0,)), ((), ()))


def dot(a, b, dims):
    return lax.dot_general(a, b, dims, preferred_element_type=F32)


def split(x):
    high = x.astype(BF16)
    return high, (x - high.astype(F32)).astype(BF16)


def on_chip(x):
    return pltpu.with_memory_space_constraint(x, pltpu.VMEM)


def off_chip(x):
    return pltpu.with_memory_space_constraint(x, pltpu.HBM)


def call(kernel, out_shape, flops, bytes_accessed, scratch=(), smem=0, args=()):
    specs = [pl.BlockSpec(memory_space=pltpu.SMEM)] * smem
    specs += [pl.BlockSpec(memory_space=pltpu.VMEM)] * (len(args) - smem)
    return pl.pallas_call(
        kernel,
        out_shape=out_shape,
        in_specs=specs,
        out_specs=jax.tree.map(
            lambda _: pl.BlockSpec(memory_space=pltpu.VMEM), out_shape, is_leaf=lambda x: hasattr(x, "shape")
        ),
        scratch_shapes=list(scratch),
        cost_estimate=pl.CostEstimate(flops=flops, bytes_accessed=bytes_accessed, transcendentals=0),
        compiler_params=pltpu.CompilerParams(vmem_limit_bytes=VMEM_LIMIT),
    )(*args)


def right_kernel(x_ref, a_ref, r_ref, out_ref):
    peers = out_ref.shape[0]
    layers = x_ref.shape[0]
    proj = r_ref.shape[1]
    for l in range(layers):
        mix = dot(r_ref[l], a_ref[l], NN)
        high, low = split(mix)
        both = jnp.concatenate([high, low], axis=0)
        rows = dot(both, x_ref[l], NT)
        rows = (rows[:proj] + rows[proj:]).astype(BF16)
        for p in range(peers):
            out_ref[p, l * proj:(l + 1) * proj, :] = rows


def left_kernel(c_ref, l_ref, high_ref, low_ref):
    layers, tokens, _ = c_ref.shape
    step = 256
    for l in range(layers):
        for t in range(0, tokens, step):
            high, low = split(dot(c_ref[l, t:t + step, :], l_ref[l], NT))
            high_ref[l, t:t + step, :] = high
            low_ref[l, t:t + step, :] = low


def project_kernel(seq_ref, rr_ref, high_ref, low_ref, out_ref):
    peers, two_proj, tokens = rr_ref.shape
    layers, _, kl = high_ref.shape
    proj = two_proj // layers
    half = proj // 2
    owned = kl // peers
    examples = seq_ref.shape[0]
    seq = tokens // examples
    span = GROUP * seq
    width = 2 * 128
    total = rr_ref[0].astype(F32)
    for p in range(1, peers):
        total = total + rr_ref[p].astype(F32)
    first = total[:proj]
    second = total[proj:]
    lane = lax.broadcasted_iota(jnp.int32, (proj, width), 1)
    out_lane = lax.broadcasted_iota(jnp.int32, (GROUP * half, 128), 1)
    for g in range(examples // GROUP):
        x0 = first if g == 0 else pltpu.roll(first, (tokens - g * span) % tokens, 1)
        x1 = pltpu.roll(second, (tokens + span - g * span) % tokens, 1)
        x0, x1 = x0[:, :width], x1[:, :width]
        blocks = []
        for i in range(GROUP):
            start = i * seq
            stop = start + seq_ref[g * GROUP + i]
            mask0 = (lane >= start) & (lane < stop)
            mask1 = (lane >= start + span) & (lane < stop + span)
            blocks.append(jnp.where(mask0, x0, jnp.where(mask1, x1, 0.0)))
        spread = jnp.concatenate(blocks, axis=0)
        high, low = split(spread)
        both = jnp.concatenate([high, low], axis=0)[:, :layers * span]
        high = high[:, :layers * span]
        t = g * span
        left_high = jnp.concatenate([high_ref[l, t:t + span, :] for l in range(layers)], axis=0)
        left_low = jnp.concatenate([low_ref[l, t:t + span, :] for l in range(layers)], axis=0)
        rows = GROUP * proj
        part = dot(both, left_high, NN)
        part = part[:rows] + part[rows:] + dot(high, left_low, NN)
        part = part.reshape(GROUP, 2, half, kl)
        even = part[:, 0].reshape(GROUP * half, kl)
        odd = part[:, 1].reshape(GROUP * half, kl)
        for p in range(peers):
            tile = (p * owned) // 128 * 128
            e = even[:, tile:tile + 128]
            o = odd[:, tile:tile + 128]
            if (p * owned) % 128 == 0:
                o = pltpu.roll(o, 64, 1)
            else:
                e = pltpu.roll(e, 64, 1)
            both_k = jnp.where(out_lane < 64, e, o)
            r = g * GROUP * half
            out_ref[p, r:r + GROUP * half, :] = both_k.astype(BF16)


def valid_kernel(own_ref, held_ref, other_ref, out_ref, squares_ref):
    half = held_ref.shape[0]
    count = 2 * half
    lane = lax.broadcasted_iota(jnp.int32, (8, count), 1)
    relative = ((lane >> 7) & 1) | (((lane >> 6) & 1) << 1) | (((lane >> 5) & 1) << 2)
    group = (relative ^ own_ref[0]) & 7
    index = (((lane >> 2) & 7) << 5) | (group << 2) | (lane & 3)
    row = lax.broadcasted_iota(jnp.int32, (count, count), 0)
    order = (row == jnp.broadcast_to(index[:1], (count, count))).astype(F32).astype(BF16)
    squares = jnp.zeros((count, 128), F32)
    for b in range(8):
        lanes = slice(b * 128, (b + 1) * 128)
        rows = dot(order[:, :half], held_ref[:, lanes], NN) + dot(order[:, half:], other_ref[:, lanes], NN)
        squares = squares + rows * rows
        out_ref[:, lanes] = rows.astype(BF16)
    squares_ref[...] = jnp.sum(squares.T, axis=0, keepdims=True)


def product_kernel(part_ref, valid_ref, squares_ref, out_ref, sum_ref):
    peers, rows, _ = part_ref.shape
    valid_count = valid_ref.shape[0]
    examples = rows // 8
    total = part_ref[0].astype(F32)
    for p in range(1, peers):
        total = total + part_ref[p].astype(F32)
    sum_ref[...] = total
    squares = jnp.sum((total * total).reshape(examples, 8, 128), axis=1)
    squares = jnp.sum(squares, axis=1, keepdims=True)
    row = lax.broadcasted_iota(jnp.int32, (examples, valid_count), 0)
    column = lax.broadcasted_iota(jnp.int32, (examples, valid_count), 1)
    train = jnp.sum(jnp.where(row == column, squares, 0.0), axis=0, keepdims=True)
    acc = jnp.zeros((2 * examples, valid_count), F32)
    for b in range(8):
        block = sum_ref[pl.ds(b, examples, stride=8), :]
        high, low = split(block)
        both = jnp.concatenate([high, low], axis=0)
        acc = acc + dot(both, valid_ref[:, b * 128:(b + 1) * 128], NT)
    products = acc[:examples] + acc[examples:]
    tail_row = lax.broadcasted_iota(jnp.int32, (8, valid_count), 0)
    tail = jnp.where(tail_row == 0, squares_ref[...], jnp.where(tail_row == 1, train, 0.0))
    for p in range(peers):
        out_ref[p, :examples, :] = products
        out_ref[p, examples:, :] = tail


def score_kernel(scaling, part_ref, out_ref):
    peers = part_ref.shape[0]
    examples, valid_count = out_ref.shape
    total = part_ref[0]
    for p in range(1, peers):
        total = total + part_ref[p]
    products = total[:examples]
    valid = jnp.sqrt(total[examples:examples + 1] + 1e-06)
    row = lax.broadcasted_iota(jnp.int32, (examples, valid_count), 0)
    column = lax.broadcasted_iota(jnp.int32, (examples, valid_count), 1)
    train = jnp.where(row == column, total[examples + 1:examples + 2], 0.0)
    train = jnp.sqrt(jnp.sum(train, axis=1, keepdims=True) + 1e-06)
    out_ref[...] = scaling * products / (train * valid)


def scores_of(proj_inputs, out_cotangent, seq_lengths, frozen_adapter, left_factor, right_factor, valid_grads):
    layers, examples, seq, inputs = proj_inputs.shape
    width = out_cotangent.shape[3]
    peers = lax.axis_size("feat")
    groups = lax.axis_size("ex")
    proj = right_factor.shape[2]
    kl = left_factor.shape[1]
    tokens = examples * seq
    owned = kl // peers
    valid_count = valid_grads.shape[0] * groups
    scaling = math.sqrt(kl * proj)
    mesh_y = 8
    inner = groups // mesh_y

    own_valid = valid_grads.reshape(-1, owned, 2, 8).transpose(0, 3, 2, 1).reshape(1, -1, owned * proj)
    far = [[y * inner + j for y in range(mesh_y)] for j in range(inner)]
    own_valid = jnp.broadcast_to(own_valid, (mesh_y,) + own_valid.shape[1:])
    held = lax.all_to_all(own_valid, "ex", 0, 0, tiled=True, axis_index_groups=far)
    held = held.reshape(-1, owned * proj)
    for bit in (4, 2, 1):
        other = lax.ppermute(held, "ex", [(i, i ^ bit) for i in range(groups)])
        if bit > 1:
            held = jnp.concatenate([held, other], axis=0)
    own_group = jnp.full((1,), lax.axis_index("ex"), jnp.int32)
    valid, valid_squares = call(
        valid_kernel,
        (
            pltpu.VMEM((valid_count, owned * proj), BF16),
            pltpu.VMEM((1, valid_count), F32),
        ),
        2 * valid_count * valid_count * owned * proj,
        2 * valid_count * owned * proj * 2,
        smem=1,
        args=(own_group, on_chip(held), on_chip(other)),
    )

    right_parts = call(
        right_kernel,
        pltpu.VMEM((peers, layers * proj, tokens), BF16),
        2 * layers * tokens * inputs * 256,
        proj_inputs.size * 2,
        args=(off_chip(proj_inputs.reshape(layers, tokens, inputs)), off_chip(frozen_adapter), off_chip(right_factor.swapaxes(1, 2))),
    )
    right_parts = lax.all_to_all(right_parts, "feat", 0, 0, tiled=True)

    left_shape = pltpu.VMEM((layers, tokens, kl), BF16)
    left_high, left_low = call(
        left_kernel,
        (left_shape, left_shape),
        2 * layers * tokens * width * kl,
        (out_cotangent.size + left_factor.size) * 2 + layers * tokens * kl * 4,
        args=(off_chip(out_cotangent.reshape(layers, tokens, width)), off_chip(left_factor)),
    )
    parts = call(
        project_kernel,
        pltpu.VMEM((peers, examples * 8, 128), BF16),
        2 * layers * tokens * kl * 256,
        layers * tokens * kl * 4,
        smem=1,
        args=(seq_lengths, on_chip(right_parts), on_chip(left_high), on_chip(left_low)),
    )
    parts = lax.all_to_all(parts, "feat", 0, 0, tiled=True)
    products = call(
        product_kernel,
        pltpu.VMEM((peers, examples + 8, valid_count), F32),
        4 * examples * valid_count * owned * proj,
        parts.size * 2 + valid.size * 2,
        scratch=(pltpu.VMEM((examples * 8, 128), F32),),
        args=(on_chip(parts), on_chip(valid), on_chip(valid_squares)),
    )
    products = lax.all_to_all(products, "feat", 0, 0, tiled=True)

    def score(part_ref, out_ref):
        score_kernel(scaling, part_ref, out_ref)

    return call(
        score,
        jax.ShapeDtypeStruct((examples, valid_count), F32),
        examples * valid_count * 16,
        products.size * 4,
        args=(on_chip(products),),
    )


def solution(mesh):
    return jax.shard_map(
        scores_of,
        mesh=mesh,
        in_specs=(
            P(None, "ex", None, "feat"),
            P(None, "ex", None, "feat"),
            P("ex"),
            P(None, None, "feat"),
            P(None, None, "feat"),
            P(),
            P("ex", "feat"),
        ),
        out_specs=P("ex", None),
        check_vma=False,
    )
```

```python
import math

import jax
import jax.numpy as jnp
from jax import lax
from jax.experimental import pallas as pl
from jax.experimental.pallas import tpu as pltpu
from jax.sharding import PartitionSpec as P


F32 = jnp.float32
BF16 = jnp.bfloat16
VMEM_LIMIT = 24 << 20
LEFT_STEP = 256
GROUP = 4
NT = (((1,), (1,)), ((), ()))
NN = (((1,), (0,)), ((), ()))


def dot(a, b, dims):
    return lax.dot_general(a, b, dims, preferred_element_type=F32)


def split(x):
    high = x.astype(BF16)
    return high, (x - high.astype(F32)).astype(BF16)


def on_chip(x):
    return pltpu.with_memory_space_constraint(x, pltpu.VMEM)


def off_chip(x):
    return pltpu.with_memory_space_constraint(x, pltpu.HBM)


def staged(arrays):
    return tuple(pltpu.VMEM(x.shape, x.dtype) for x in arrays)


def call(kernel, out_shape, flops, bytes_accessed, scratch=(), smem=0, args=(), hbm=False):
    specs = [pl.BlockSpec(memory_space=pltpu.SMEM)] * smem
    specs += [pl.BlockSpec(memory_space=pltpu.HBM if hbm else pltpu.VMEM)] * (len(args) - smem)
    return pl.pallas_call(
        kernel,
        out_shape=out_shape,
        in_specs=specs,
        out_specs=jax.tree.map(
            lambda _: pl.BlockSpec(memory_space=pltpu.VMEM), out_shape, is_leaf=lambda x: hasattr(x, "shape")
        ),
        scratch_shapes=list(scratch),
        cost_estimate=pl.CostEstimate(flops=flops, bytes_accessed=bytes_accessed, transcendentals=0),
        compiler_params=pltpu.CompilerParams(vmem_limit_bytes=VMEM_LIMIT),
    )(*args)


def right_kernel(x_hbm, a_hbm, r_hbm, out_ref, x_ref, a_ref, r_ref, sems):
    peers = out_ref.shape[0]
    layers = x_ref.shape[0]
    proj = r_ref.shape[1]
    small = [
        pltpu.make_async_copy(r_hbm, r_ref, sems.at[0]),
        pltpu.make_async_copy(a_hbm, a_ref, sems.at[1]),
    ]
    inputs = [pltpu.make_async_copy(x_hbm.at[l], x_ref.at[l], sems.at[2 + l]) for l in range(layers)]
    for copy in small + inputs:
        copy.start()
    for copy in small:
        copy.wait()
    mixes = []
    for l in range(layers):
        high, low = split(dot(r_ref[l], a_ref[l], NN))
        mixes.append(jnp.concatenate([high, low], axis=0))
    for l in range(layers):
        inputs[l].wait()
        rows = dot(mixes[l], x_ref[l], NT)
        rows = (rows[:proj] + rows[proj:]).astype(BF16)
        for p in range(peers):
            out_ref[p, l * proj:(l + 1) * proj, :] = rows


def left_kernel(c_hbm, l_hbm, high_ref, low_ref, c_ref, l_ref, sems):
    layers, tokens, _ = c_ref.shape
    step = LEFT_STEP
    factors, pieces = [], []
    for l in range(layers):
        factors.append(pltpu.make_async_copy(l_hbm.at[l], l_ref.at[l], sems.at[l]))
        factors[-1].start()
        for t in range(0, tokens, step):
            rows = pl.ds(t, step)
            copy = pltpu.make_async_copy(c_hbm.at[l, rows], c_ref.at[l, rows], sems.at[layers + len(pieces)])
            copy.start()
            pieces.append((l, t, copy))
    for l, t, copy in pieces:
        if t == 0:
            factors[l].wait()
        copy.wait()
        high, low = split(dot(c_ref[l, t:t + step, :], l_ref[l], NT))
        high_ref[l, t:t + step, :] = high
        low_ref[l, t:t + step, :] = low


def project_kernel(seq_ref, rr_ref, high_ref, low_ref, out_ref):
    peers, two_proj, tokens = rr_ref.shape
    layers, _, kl = high_ref.shape
    proj = two_proj // layers
    half = proj // 2
    owned = kl // peers
    examples = seq_ref.shape[0]
    seq = tokens // examples
    span = GROUP * seq
    width = 2 * 128
    total = rr_ref[0].astype(F32)
    for p in range(1, peers):
        total = total + rr_ref[p].astype(F32)
    first = total[:proj]
    second = total[proj:]
    lane = lax.broadcasted_iota(jnp.int32, (proj, width), 1)
    out_lane = lax.broadcasted_iota(jnp.int32, (GROUP * half, 128), 1)
    for g in range(examples // GROUP):
        x0 = first if g == 0 else pltpu.roll(first, (tokens - g * span) % tokens, 1)
        x1 = pltpu.roll(second, (tokens + span - g * span) % tokens, 1)
        x0, x1 = x0[:, :width], x1[:, :width]
        blocks = []
        for i in range(GROUP):
            start = i * seq
            stop = start + seq_ref[g * GROUP + i]
            mask0 = (lane >= start) & (lane < stop)
            mask1 = (lane >= start + span) & (lane < stop + span)
            blocks.append(jnp.where(mask0, x0, jnp.where(mask1, x1, 0.0)))
        spread = jnp.concatenate(blocks, axis=0)
        high, low = split(spread)
        both = jnp.concatenate([high, low], axis=0)[:, :layers * span]
        high = high[:, :layers * span]
        t = g * span
        left_high = jnp.concatenate([high_ref[l, t:t + span, :] for l in range(layers)], axis=0)
        left_low = jnp.concatenate([low_ref[l, t:t + span, :] for l in range(layers)], axis=0)
        rows = GROUP * proj
        part = dot(both, left_high, NN)
        part = part[:rows] + part[rows:] + dot(high, left_low, NN)
        part = part.reshape(GROUP, 2, half, kl)
        even = part[:, 0].reshape(GROUP * half, kl)
        odd = part[:, 1].reshape(GROUP * half, kl)
        for p in range(peers):
            tile = (p * owned) // 128 * 128
            e = even[:, tile:tile + 128]
            o = odd[:, tile:tile + 128]
            if (p * owned) % 128 == 0:
                o = pltpu.roll(o, 64, 1)
            else:
                e = pltpu.roll(e, 64, 1)
            both_k = jnp.where(out_lane < 64, e, o)
            r = g * GROUP * half
            out_ref[p, r:r + GROUP * half, :] = both_k.astype(BF16)


def join_kernel(*refs):
    rows = refs[0].shape[0]
    for n, ref in enumerate(refs[:-1]):
        refs[-1][n * rows:(n + 1) * rows, :] = ref[...]


def valid_kernel(own_ref, *refs):
    pieces, other_ref, out_ref, squares_ref = refs[:-3], refs[-3], refs[-2], refs[-1]
    half = other_ref.shape[0]
    count = 2 * half
    lane = lax.broadcasted_iota(jnp.int32, (8, count), 1)
    group = (((lane >> 7) & 1) | (((lane >> 5) & 3) << 1)) ^ own_ref[0]
    index = (((lane >> 2) & 7) << 5) | ((group & 7) << 2) | (lane & 3)
    row = lax.broadcasted_iota(jnp.int32, (count, count), 0)
    order = (row == jnp.broadcast_to(index[:1], (count, count))).astype(F32).astype(BF16)
    squares = jnp.zeros((count, 128), F32)
    for b in range(8):
        lanes = slice(b * 128, (b + 1) * 128)
        held = jnp.concatenate([ref[:, lanes] for ref in (*pieces, other_ref)], axis=0)
        rows = dot(order, held, NN)
        squares = squares + rows * rows
        out_ref[:, lanes] = rows.astype(BF16)
    squares_ref[...] = jnp.sum(squares.T, axis=0, keepdims=True)


def product_kernel(part_ref, valid_ref, squares_ref, out_ref, sum_ref):
    peers, rows, _ = part_ref.shape
    valid_count = valid_ref.shape[0]
    examples = rows // 8
    total = part_ref[0].astype(F32)
    for p in range(1, peers):
        total = total + part_ref[p].astype(F32)
    sum_ref[...] = total
    squares = jnp.sum((total * total).reshape(examples, 8, 128), axis=1)
    squares = jnp.sum(squares, axis=1, keepdims=True)
    row = lax.broadcasted_iota(jnp.int32, (examples, valid_count), 0)
    column = lax.broadcasted_iota(jnp.int32, (examples, valid_count), 1)
    train = jnp.sum(jnp.where(row == column, squares, 0.0), axis=0, keepdims=True)
    acc = jnp.zeros((2 * examples, valid_count), F32)
    for b in range(8):
        block = sum_ref[pl.ds(b, examples, stride=8), :]
        high, low = split(block)
        both = jnp.concatenate([high, low], axis=0)
        acc = acc + dot(both, valid_ref[:, b * 128:(b + 1) * 128], NT)
    products = acc[:examples] + acc[examples:]
    tail_row = lax.broadcasted_iota(jnp.int32, (8, valid_count), 0)
    tail = jnp.where(tail_row == 0, squares_ref[...], jnp.where(tail_row == 1, train, 0.0))
    for p in range(peers):
        out_ref[p, :examples, :] = products
        out_ref[p, examples:, :] = tail


def score_kernel(scaling, part_ref, out_ref):
    peers = part_ref.shape[0]
    examples, valid_count = out_ref.shape
    total = part_ref[0]
    for p in range(1, peers):
        total = total + part_ref[p]
    products = total[:examples]
    valid = jnp.sqrt(total[examples:examples + 1] + 1e-06)
    row = lax.broadcasted_iota(jnp.int32, (examples, valid_count), 0)
    column = lax.broadcasted_iota(jnp.int32, (examples, valid_count), 1)
    train = jnp.where(row == column, total[examples + 1:examples + 2], 0.0)
    train = jnp.sqrt(jnp.sum(train, axis=1, keepdims=True) + 1e-06)
    out_ref[...] = scaling * products / (train * valid)


def scores_of(proj_inputs, out_cotangent, seq_lengths, frozen_adapter, left_factor, right_factor, valid_grads):
    layers, examples, seq, inputs = proj_inputs.shape
    width = out_cotangent.shape[3]
    peers = lax.axis_size("feat")
    groups = lax.axis_size("ex")
    proj = right_factor.shape[2]
    kl = left_factor.shape[1]
    tokens = examples * seq
    owned = kl // peers
    valid_count = valid_grads.shape[0] * groups
    scaling = math.sqrt(kl * proj)
    mesh_y = 8
    inner = groups // mesh_y

    own_valid = valid_grads.reshape(-1, owned, 2, 8).transpose(0, 3, 2, 1).reshape(1, -1, owned * proj)
    far = [[y * inner + j for y in range(mesh_y)] for j in range(inner)]
    own_valid = jnp.broadcast_to(own_valid, (mesh_y,) + own_valid.shape[1:])
    held = lax.all_to_all(own_valid, "ex", 0, 0, tiled=True, axis_index_groups=far)
    held = held.reshape(-1, owned * proj)
    pieces = [held]
    for bit in (2, 4, 6):
        pieces.append(lax.ppermute(held, "ex", [(i, i ^ bit) for i in range(groups)]))
    pieces = [on_chip(piece) for piece in pieces]
    half = call(
        join_kernel,
        jax.ShapeDtypeStruct((valid_count // 2, owned * proj), BF16),
        0,
        2 * valid_count * owned * proj,
        args=pieces,
    )
    other = lax.ppermute(half, "ex", [(i, i ^ 1) for i in range(groups)])
    own_group = jnp.full((1,), lax.axis_index("ex"), jnp.int32)
    valid, valid_squares = call(
        valid_kernel,
        (
            pltpu.VMEM((valid_count, owned * proj), BF16),
            pltpu.VMEM((1, valid_count), F32),
        ),
        2 * valid_count * valid_count * owned * proj,
        2 * valid_count * owned * proj * 2,
        smem=1,
        args=(own_group, *pieces, on_chip(other)),
    )

    right_in = (proj_inputs.reshape(layers, tokens, inputs), frozen_adapter, right_factor.swapaxes(1, 2))
    right_parts = call(
        right_kernel,
        pltpu.VMEM((peers, layers * proj, tokens), BF16),
        2 * layers * tokens * inputs * 256,
        proj_inputs.size * 2,
        scratch=(*staged(right_in), pltpu.SemaphoreType.DMA((2 + layers,))),
        args=tuple(off_chip(x) for x in right_in),
        hbm=True,
    )
    right_parts = lax.all_to_all(right_parts, "feat", 0, 0, tiled=True)

    left_shape = pltpu.VMEM((layers, tokens, kl), BF16)
    left_in = (out_cotangent.reshape(layers, tokens, width), left_factor)
    left_high, left_low = call(
        left_kernel,
        (left_shape, left_shape),
        2 * layers * tokens * width * kl,
        (out_cotangent.size + left_factor.size) * 2 + layers * tokens * kl * 4,
        scratch=(*staged(left_in), pltpu.SemaphoreType.DMA((layers + layers * tokens // LEFT_STEP,))),
        args=tuple(off_chip(x) for x in left_in),
        hbm=True,
    )
    parts = call(
        project_kernel,
        pltpu.VMEM((peers, examples * 8, 128), BF16),
        2 * layers * tokens * kl * 256,
        layers * tokens * kl * 4,
        smem=1,
        args=(seq_lengths, on_chip(right_parts), on_chip(left_high), on_chip(left_low)),
    )
    parts = lax.all_to_all(parts, "feat", 0, 0, tiled=True)
    products = call(
        product_kernel,
        pltpu.VMEM((peers, examples + 8, valid_count), F32),
        4 * examples * valid_count * owned * proj,
        parts.size * 2 + valid.size * 2,
        scratch=(pltpu.VMEM((examples * 8, 128), F32),),
        args=(on_chip(parts), on_chip(valid), on_chip(valid_squares)),
    )
    products = lax.all_to_all(products, "feat", 0, 0, tiled=True)

    def score(part_ref, out_ref):
        score_kernel(scaling, part_ref, out_ref)

    return call(
        score,
        jax.ShapeDtypeStruct((examples, valid_count), F32),
        examples * valid_count * 16,
        products.size * 4,
        args=(on_chip(products),),
    )


def solution(mesh):
    return jax.shard_map(
        scores_of,
        mesh=mesh,
        in_specs=(
            P(None, "ex", None, "feat"),
            P(None, "ex", None, "feat"),
            P("ex"),
            P(None, None, "feat"),
            P(None, None, "feat"),
            P(),
            P("ex", "feat"),
        ),
        out_specs=P("ex", None),
        check_vma=False,
    )
```

```python
import math

import jax
import jax.numpy as jnp
from jax import lax
from jax.experimental import pallas as pl
from jax.experimental.pallas import tpu as pltpu
from jax.sharding import PartitionSpec as P


F32 = jnp.float32
BF16 = jnp.bfloat16
VMEM_LIMIT = 24 << 20
LEFT_STEP = 256
GROUP = 4
NT = (((1,), (1,)), ((), ()))
NN = (((1,), (0,)), ((), ()))


def dot(a, b, dims):
    return lax.dot_general(a, b, dims, preferred_element_type=F32)


def split(x):
    high = x.astype(BF16)
    return high, (x - high.astype(F32)).astype(BF16)


def on_chip(x):
    return pltpu.with_memory_space_constraint(x, pltpu.VMEM)


def off_chip(x):
    return pltpu.with_memory_space_constraint(x, pltpu.HBM)


def staged(arrays):
    return tuple(pltpu.VMEM(x.shape, x.dtype) for x in arrays)


def call(kernel, out_shape, flops, bytes_accessed, scratch=(), smem=0, args=(), hbm=False):
    specs = [pl.BlockSpec(memory_space=pltpu.SMEM)] * smem
    specs += [pl.BlockSpec(memory_space=pltpu.HBM if hbm else pltpu.VMEM)] * (len(args) - smem)
    return pl.pallas_call(
        kernel,
        out_shape=out_shape,
        in_specs=specs,
        out_specs=jax.tree.map(
            lambda _: pl.BlockSpec(memory_space=pltpu.VMEM), out_shape, is_leaf=lambda x: hasattr(x, "shape")
        ),
        scratch_shapes=list(scratch),
        cost_estimate=pl.CostEstimate(flops=flops, bytes_accessed=bytes_accessed, transcendentals=0),
        compiler_params=pltpu.CompilerParams(vmem_limit_bytes=VMEM_LIMIT),
    )(*args)


def right_kernel(x_hbm, a_hbm, r_hbm, out_ref, x_ref, a_ref, r_ref, sems):
    peers = out_ref.shape[0]
    layers = x_ref.shape[0]
    proj = r_ref.shape[1]
    small = [
        pltpu.make_async_copy(r_hbm, r_ref, sems.at[0]),
        pltpu.make_async_copy(a_hbm, a_ref, sems.at[1]),
    ]
    inputs = [pltpu.make_async_copy(x_hbm.at[l], x_ref.at[l], sems.at[2 + l]) for l in range(layers)]
    for copy in small + inputs:
        copy.start()
    for copy in small:
        copy.wait()
    mixes = []
    for l in range(layers):
        high, low = split(dot(r_ref[l], a_ref[l], NN))
        mixes.append(jnp.concatenate([high, low], axis=0))
    for l in range(layers):
        inputs[l].wait()
        rows = dot(mixes[l], x_ref[l], NT)
        rows = (rows[:proj] + rows[proj:]).astype(BF16)
        for p in range(peers):
            out_ref[p, l * proj:(l + 1) * proj, :] = rows


def left_kernel(c_hbm, l_hbm, high_ref, low_ref, c_ref, l_ref, sems):
    layers, tokens, _ = c_ref.shape
    step = LEFT_STEP
    factors, pieces = [], []
    for l in range(layers):
        factors.append(pltpu.make_async_copy(l_hbm.at[l], l_ref.at[l], sems.at[l]))
        factors[-1].start()
        for t in range(0, tokens, step):
            rows = pl.ds(t, step)
            copy = pltpu.make_async_copy(c_hbm.at[l, rows], c_ref.at[l, rows], sems.at[layers + len(pieces)])
            copy.start()
            pieces.append((l, t, copy))
    for l, t, copy in pieces:
        if t == 0:
            factors[l].wait()
        copy.wait()
        high, low = split(dot(c_ref[l, t:t + step, :], l_ref[l], NT))
        high_ref[l, t:t + step, :] = high
        low_ref[l, t:t + step, :] = low


def project_kernel(seq_ref, rr_ref, high_ref, low_ref, out_ref):
    peers, two_proj, tokens = rr_ref.shape
    layers, _, kl = high_ref.shape
    proj = two_proj // layers
    half = proj // 2
    owned = kl // peers
    examples = seq_ref.shape[0]
    seq = tokens // examples
    span = GROUP * seq
    width = 2 * 128
    total = rr_ref[0].astype(F32)
    for p in range(1, peers):
        total = total + rr_ref[p].astype(F32)
    first = total[:proj]
    second = total[proj:]
    lane = lax.broadcasted_iota(jnp.int32, (proj, width), 1)
    out_lane = lax.broadcasted_iota(jnp.int32, (GROUP * half, 128), 1)
    for g in range(examples // GROUP):
        x0 = first if g == 0 else pltpu.roll(first, (tokens - g * span) % tokens, 1)
        x1 = pltpu.roll(second, (tokens + span - g * span) % tokens, 1)
        x0, x1 = x0[:, :width], x1[:, :width]
        blocks = []
        for i in range(GROUP):
            start = i * seq
            stop = start + seq_ref[g * GROUP + i]
            mask0 = (lane >= start) & (lane < stop)
            mask1 = (lane >= start + span) & (lane < stop + span)
            blocks.append(jnp.where(mask0, x0, jnp.where(mask1, x1, 0.0)))
        spread = jnp.concatenate(blocks, axis=0)
        high, low = split(spread)
        both = jnp.concatenate([high, low], axis=0)[:, :layers * span]
        high = high[:, :layers * span]
        t = g * span
        left_high = jnp.concatenate([high_ref[l, t:t + span, :] for l in range(layers)], axis=0)
        left_low = jnp.concatenate([low_ref[l, t:t + span, :] for l in range(layers)], axis=0)
        rows = GROUP * proj
        part = dot(both, left_high, NN)
        part = part[:rows] + part[rows:] + dot(high, left_low, NN)
        part = part.reshape(GROUP, 2, half, kl)
        even = part[:, 0].reshape(GROUP * half, kl)
        odd = part[:, 1].reshape(GROUP * half, kl)
        for p in range(peers):
            tile = (p * owned) // 128 * 128
            e = even[:, tile:tile + 128]
            o = odd[:, tile:tile + 128]
            if (p * owned) % 128 == 0:
                o = pltpu.roll(o, 64, 1)
            else:
                e = pltpu.roll(e, 64, 1)
            both_k = jnp.where(out_lane < 64, e, o)
            r = g * GROUP * half
            out_ref[p, r:r + GROUP * half, :] = both_k.astype(BF16)


def valid_kernel(own_ref, half_ref, other_ref, out_ref, squares_ref):
    count = half_ref.shape[0]
    place = lax.broadcasted_iota(jnp.int32, (8, 2 * count), 1)
    core = ((place >> 8) ^ own_ref[0]) & 1
    index = (((place >> 3) & 31) << 3) | (core << 2) | ((place >> 1) & 3)
    row = lax.broadcasted_iota(jnp.int32, (count, 2 * count), 0)
    squares = jnp.zeros((count, 128), F32)
    for h in range(2):
        source = jnp.where((place & 1) == h, index, -1)
        order = (row == jnp.broadcast_to(source[:1], row.shape)).astype(F32).astype(BF16)
        for q in range(4):
            lanes = slice(q * 128, (q + 1) * 128)
            rows = dot(order[:, :count], half_ref[:, lanes], NN) + dot(order[:, count:], other_ref[:, lanes], NN)
            squares = squares + rows * rows
            b = h * 4 + q
            out_ref[:, b * 128:(b + 1) * 128] = rows.astype(BF16)
    squares_ref[...] = jnp.sum(squares.T, axis=0, keepdims=True)


def product_kernel(part_ref, valid_ref, squares_ref, out_ref, sum_ref):
    peers, rows, _ = part_ref.shape
    valid_count = valid_ref.shape[0]
    examples = rows // 8
    total = part_ref[0].astype(F32)
    for p in range(1, peers):
        total = total + part_ref[p].astype(F32)
    sum_ref[...] = total
    squares = jnp.sum((total * total).reshape(examples, 8, 128), axis=1)
    squares = jnp.sum(squares, axis=1, keepdims=True)
    row = lax.broadcasted_iota(jnp.int32, (examples, valid_count), 0)
    column = lax.broadcasted_iota(jnp.int32, (examples, valid_count), 1)
    train = jnp.sum(jnp.where(row == column, squares, 0.0), axis=0, keepdims=True)
    acc = jnp.zeros((2 * examples, valid_count), F32)
    for b in range(8):
        block = sum_ref[pl.ds(b, examples, stride=8), :]
        high, low = split(block)
        both = jnp.concatenate([high, low], axis=0)
        acc = acc + dot(both, valid_ref[:, b * 128:(b + 1) * 128], NT)
    products = acc[:examples] + acc[examples:]
    tail_row = lax.broadcasted_iota(jnp.int32, (8, valid_count), 0)
    tail = jnp.where(tail_row == 0, squares_ref[...], jnp.where(tail_row == 1, train, 0.0))
    for p in range(peers):
        out_ref[p, :examples, :] = products
        out_ref[p, examples:, :] = tail


def score_kernel(scaling, part_ref, out_ref):
    peers = part_ref.shape[0]
    examples, valid_count = out_ref.shape
    total = part_ref[0]
    for p in range(1, peers):
        total = total + part_ref[p]
    products = total[:examples]
    valid = jnp.sqrt(total[examples:examples + 1] + 1e-06)
    row = lax.broadcasted_iota(jnp.int32, (examples, valid_count), 0)
    column = lax.broadcasted_iota(jnp.int32, (examples, valid_count), 1)
    train = jnp.where(row == column, total[examples + 1:examples + 2], 0.0)
    train = jnp.sqrt(jnp.sum(train, axis=1, keepdims=True) + 1e-06)
    out_ref[...] = scaling * products / (train * valid)


def scores_of(proj_inputs, out_cotangent, seq_lengths, frozen_adapter, left_factor, right_factor, valid_grads):
    layers, examples, seq, inputs = proj_inputs.shape
    width = out_cotangent.shape[3]
    peers = lax.axis_size("feat")
    groups = lax.axis_size("ex")
    proj = right_factor.shape[2]
    kl = left_factor.shape[1]
    tokens = examples * seq
    owned = kl // peers
    valid_count = valid_grads.shape[0] * groups
    scaling = math.sqrt(kl * proj)

    own_valid = valid_grads.reshape(-1, owned, 2, 8).transpose(0, 3, 2, 1).reshape(1, -1, owned * proj // 2)
    own_valid = jnp.broadcast_to(own_valid, (groups // 2,) + own_valid.shape[1:])
    same_core = [[i * 2 + c for i in range(groups // 2)] for c in range(2)]
    half = lax.all_to_all(own_valid, "ex", 0, 0, tiled=True, axis_index_groups=same_core)
    half = half.reshape(valid_count, owned * proj // 2)
    other = lax.ppermute(half, "ex", [(i, i ^ 1) for i in range(groups)])
    own_group = jnp.full((1,), lax.axis_index("ex"), jnp.int32)
    valid, valid_squares = call(
        valid_kernel,
        (
            pltpu.VMEM((valid_count, owned * proj), BF16),
            pltpu.VMEM((1, valid_count), F32),
        ),
        2 * valid_count * valid_count * owned * proj,
        2 * valid_count * owned * proj * 2,
        smem=1,
        args=(own_group, on_chip(half), on_chip(other)),
    )

    right_in = (proj_inputs.reshape(layers, tokens, inputs), frozen_adapter, right_factor.swapaxes(1, 2))
    right_parts = call(
        right_kernel,
        pltpu.VMEM((peers, layers * proj, tokens), BF16),
        2 * layers * tokens * inputs * 256,
        proj_inputs.size * 2,
        scratch=(*staged(right_in), pltpu.SemaphoreType.DMA((2 + layers,))),
        args=tuple(off_chip(x) for x in right_in),
        hbm=True,
    )
    right_parts = lax.all_to_all(right_parts, "feat", 0, 0, tiled=True)

    left_shape = pltpu.VMEM((layers, tokens, kl), BF16)
    left_in = (out_cotangent.reshape(layers, tokens, width), left_factor)
    left_high, left_low = call(
        left_kernel,
        (left_shape, left_shape),
        2 * layers * tokens * width * kl,
        (out_cotangent.size + left_factor.size) * 2 + layers * tokens * kl * 4,
        scratch=(*staged(left_in), pltpu.SemaphoreType.DMA((layers + layers * tokens // LEFT_STEP,))),
        args=tuple(off_chip(x) for x in left_in),
        hbm=True,
    )
    parts = call(
        project_kernel,
        pltpu.VMEM((peers, examples * 8, 128), BF16),
        2 * layers * tokens * kl * 256,
        layers * tokens * kl * 4,
        smem=1,
        args=(seq_lengths, on_chip(right_parts), on_chip(left_high), on_chip(left_low)),
    )
    parts = lax.all_to_all(parts, "feat", 0, 0, tiled=True)
    products = call(
        product_kernel,
        pltpu.VMEM((peers, examples + 8, valid_count), F32),
        4 * examples * valid_count * owned * proj,
        parts.size * 2 + valid.size * 2,
        scratch=(pltpu.VMEM((examples * 8, 128), F32),),
        args=(on_chip(parts), on_chip(valid), on_chip(valid_squares)),
    )
    products = lax.all_to_all(products, "feat", 0, 0, tiled=True)

    def score(part_ref, out_ref):
        score_kernel(scaling, part_ref, out_ref)

    return call(
        score,
        jax.ShapeDtypeStruct((examples, valid_count), F32),
        examples * valid_count * 16,
        products.size * 4,
        args=(on_chip(products),),
    )


def solution(mesh):
    return jax.shard_map(
        scores_of,
        mesh=mesh,
        in_specs=(
            P(None, "ex", None, "feat"),
            P(None, "ex", None, "feat"),
            P("ex"),
            P(None, None, "feat"),
            P(None, None, "feat"),
            P(),
            P("ex", "feat"),
        ),
        out_specs=P("ex", None),
        check_vma=False,
    )
```

```python
import math

import jax
import jax.numpy as jnp
from jax import lax
from jax.experimental import pallas as pl
from jax.experimental.pallas import tpu as pltpu
from jax.sharding import PartitionSpec as P


F32 = jnp.float32
BF16 = jnp.bfloat16
VMEM_LIMIT = 24 << 20
LEFT_STEP = 256
GROUP = 4
NT = (((1,), (1,)), ((), ()))
NN = (((1,), (0,)), ((), ()))


def dot(a, b, dims):
    return lax.dot_general(a, b, dims, preferred_element_type=F32)


def split(x):
    high = x.astype(BF16)
    return high, (x - high.astype(F32)).astype(BF16)


def on_chip(x):
    return pltpu.with_memory_space_constraint(x, pltpu.VMEM)


def off_chip(x):
    return pltpu.with_memory_space_constraint(x, pltpu.HBM)


def staged(arrays):
    return tuple(pltpu.VMEM(x.shape, x.dtype) for x in arrays)


def call(kernel, out_shape, flops, bytes_accessed, scratch=(), smem=0, args=(), hbm=False):
    specs = [pl.BlockSpec(memory_space=pltpu.SMEM)] * smem
    specs += [pl.BlockSpec(memory_space=pltpu.HBM if hbm else pltpu.VMEM)] * (len(args) - smem)
    return pl.pallas_call(
        kernel,
        out_shape=out_shape,
        in_specs=specs,
        out_specs=jax.tree.map(
            lambda _: pl.BlockSpec(memory_space=pltpu.VMEM), out_shape, is_leaf=lambda x: hasattr(x, "shape")
        ),
        scratch_shapes=list(scratch),
        cost_estimate=pl.CostEstimate(flops=flops, bytes_accessed=bytes_accessed, transcendentals=0),
        compiler_params=pltpu.CompilerParams(vmem_limit_bytes=VMEM_LIMIT),
    )(*args)


def right_kernel(x_hbm, a_hbm, r_hbm, out_ref, x_ref, a_ref, r_ref, sems):
    peers = out_ref.shape[0]
    layers = x_ref.shape[0]
    proj = r_ref.shape[1]
    small = [
        pltpu.make_async_copy(r_hbm, r_ref, sems.at[0]),
        pltpu.make_async_copy(a_hbm, a_ref, sems.at[1]),
    ]
    inputs = [pltpu.make_async_copy(x_hbm.at[l], x_ref.at[l], sems.at[2 + l]) for l in range(layers)]
    for copy in small + inputs:
        copy.start()
    for copy in small:
        copy.wait()
    mixes = []
    for l in range(layers):
        high, low = split(dot(r_ref[l], a_ref[l], NN))
        mixes.append(jnp.concatenate([high, low], axis=0))
    for l in range(layers):
        inputs[l].wait()
        rows = dot(mixes[l], x_ref[l], NT)
        rows = (rows[:proj] + rows[proj:]).astype(BF16)
        for p in range(peers):
            out_ref[p, l * proj:(l + 1) * proj, :] = rows


def left_kernel(c_hbm, l_hbm, high_ref, low_ref, c_ref, l_ref, sems):
    layers, tokens, _ = c_ref.shape
    step = LEFT_STEP
    factors, pieces = [], []
    for l in range(layers):
        factors.append(pltpu.make_async_copy(l_hbm.at[l], l_ref.at[l], sems.at[l]))
        factors[-1].start()
        for t in range(0, tokens, step):
            rows = pl.ds(t, step)
            copy = pltpu.make_async_copy(c_hbm.at[l, rows], c_ref.at[l, rows], sems.at[layers + len(pieces)])
            copy.start()
            pieces.append((l, t, copy))
    for l, t, copy in pieces:
        if t == 0:
            factors[l].wait()
        copy.wait()
        high, low = split(dot(c_ref[l, t:t + step, :], l_ref[l], NT))
        high_ref[l, t:t + step, :] = high
        low_ref[l, t:t + step, :] = low


def project_kernel(seq_ref, rr_ref, high_ref, low_ref, out_ref):
    peers, two_proj, tokens = rr_ref.shape
    layers, _, kl = high_ref.shape
    proj = two_proj // layers
    half = proj // 2
    owned = kl // peers
    examples = seq_ref.shape[0]
    seq = tokens // examples
    span = GROUP * seq
    width = 2 * 128
    total = rr_ref[0].astype(F32)
    for p in range(1, peers):
        total = total + rr_ref[p].astype(F32)
    first = total[:proj]
    second = total[proj:]
    lane = lax.broadcasted_iota(jnp.int32, (proj, width), 1)
    out_lane = lax.broadcasted_iota(jnp.int32, (GROUP * half, 128), 1)
    for g in range(examples // GROUP):
        x0 = first if g == 0 else pltpu.roll(first, (tokens - g * span) % tokens, 1)
        x1 = pltpu.roll(second, (tokens + span - g * span) % tokens, 1)
        x0, x1 = x0[:, :width], x1[:, :width]
        blocks = []
        for i in range(GROUP):
            start = i * seq
            stop = start + seq_ref[g * GROUP + i]
            mask0 = (lane >= start) & (lane < stop)
            mask1 = (lane >= start + span) & (lane < stop + span)
            blocks.append(jnp.where(mask0, x0, jnp.where(mask1, x1, 0.0)))
        spread = jnp.concatenate(blocks, axis=0)
        high, low = split(spread)
        both = jnp.concatenate([high, low], axis=0)[:, :layers * span]
        high = high[:, :layers * span]
        t = g * span
        left_high = jnp.concatenate([high_ref[l, t:t + span, :] for l in range(layers)], axis=0)
        left_low = jnp.concatenate([low_ref[l, t:t + span, :] for l in range(layers)], axis=0)
        rows = GROUP * proj
        part = dot(both, left_high, NN)
        part = part[:rows] + part[rows:] + dot(high, left_low, NN)
        part = part.reshape(GROUP, 2, half, kl)
        even = part[:, 0].reshape(GROUP * half, kl)
        odd = part[:, 1].reshape(GROUP * half, kl)
        for p in range(peers):
            tile = (p * owned) // 128 * 128
            e = even[:, tile:tile + 128]
            o = odd[:, tile:tile + 128]
            if (p * owned) % 128 == 0:
                o = pltpu.roll(o, 64, 1)
            else:
                e = pltpu.roll(e, 64, 1)
            both_k = jnp.where(out_lane < 64, e, o)
            r = g * GROUP * half
            out_ref[p, r:r + GROUP * half, :] = both_k.astype(BF16)


def spread_kernel(own_ref, far_ref, out_ref):
    for n in range(out_ref.shape[0]):
        out_ref[n, 0] = own_ref[...]
        out_ref[n, 1] = far_ref[...]


def valid_kernel(own_ref, half_ref, other_ref, out_ref, squares_ref):
    count = half_ref.shape[0]
    place = lax.broadcasted_iota(jnp.int32, (8, 2 * count), 1)
    core = ((place >> 8) ^ own_ref[0]) & 1
    far = ((place >> 3) ^ (own_ref[0] >> 2)) & 1
    index = (((place >> 5) & 7) << 5) | (far << 4) | (((place >> 4) & 1) << 3) | (core << 2) | ((place >> 1) & 3)
    row = lax.broadcasted_iota(jnp.int32, (count, 2 * count), 0)
    squares = jnp.zeros((count, 128), F32)
    for h in range(2):
        source = jnp.where((place & 1) == h, index, -1)
        order = (row == jnp.broadcast_to(source[:1], row.shape)).astype(F32).astype(BF16)
        for q in range(4):
            lanes = slice(q * 128, (q + 1) * 128)
            rows = dot(order[:, :count], half_ref[:, lanes], NN) + dot(order[:, count:], other_ref[:, lanes], NN)
            squares = squares + rows * rows
            b = h * 4 + q
            out_ref[:, b * 128:(b + 1) * 128] = rows.astype(BF16)
    squares_ref[...] = jnp.sum(squares.T, axis=0, keepdims=True)


def product_kernel(part_ref, valid_ref, squares_ref, out_ref, sum_ref):
    peers, rows, _ = part_ref.shape
    valid_count = valid_ref.shape[0]
    examples = rows // 8
    total = part_ref[0].astype(F32)
    for p in range(1, peers):
        total = total + part_ref[p].astype(F32)
    sum_ref[...] = total
    squares = jnp.sum((total * total).reshape(examples, 8, 128), axis=1)
    squares = jnp.sum(squares, axis=1, keepdims=True)
    row = lax.broadcasted_iota(jnp.int32, (examples, valid_count), 0)
    column = lax.broadcasted_iota(jnp.int32, (examples, valid_count), 1)
    train = jnp.sum(jnp.where(row == column, squares, 0.0), axis=0, keepdims=True)
    acc = jnp.zeros((2 * examples, valid_count), F32)
    for b in range(8):
        block = sum_ref[pl.ds(b, examples, stride=8), :]
        high, low = split(block)
        both = jnp.concatenate([high, low], axis=0)
        acc = acc + dot(both, valid_ref[:, b * 128:(b + 1) * 128], NT)
    products = acc[:examples] + acc[examples:]
    tail_row = lax.broadcasted_iota(jnp.int32, (8, valid_count), 0)
    tail = jnp.where(tail_row == 0, squares_ref[...], jnp.where(tail_row == 1, train, 0.0))
    for p in range(peers):
        out_ref[p, :examples, :] = products
        out_ref[p, examples:, :] = tail


def score_kernel(scaling, part_ref, out_ref):
    peers = part_ref.shape[0]
    examples, valid_count = out_ref.shape
    total = part_ref[0]
    for p in range(1, peers):
        total = total + part_ref[p]
    products = total[:examples]
    valid = jnp.sqrt(total[examples:examples + 1] + 1e-06)
    row = lax.broadcasted_iota(jnp.int32, (examples, valid_count), 0)
    column = lax.broadcasted_iota(jnp.int32, (examples, valid_count), 1)
    train = jnp.where(row == column, total[examples + 1:examples + 2], 0.0)
    train = jnp.sqrt(jnp.sum(train, axis=1, keepdims=True) + 1e-06)
    out_ref[...] = scaling * products / (train * valid)


def scores_of(proj_inputs, out_cotangent, seq_lengths, frozen_adapter, left_factor, right_factor, valid_grads):
    layers, examples, seq, inputs = proj_inputs.shape
    width = out_cotangent.shape[3]
    peers = lax.axis_size("feat")
    groups = lax.axis_size("ex")
    proj = right_factor.shape[2]
    kl = left_factor.shape[1]
    tokens = examples * seq
    owned = kl // peers
    valid_count = valid_grads.shape[0] * groups
    scaling = math.sqrt(kl * proj)

    own_valid = valid_grads.reshape(-1, owned, 2, 8).transpose(0, 3, 2, 1).reshape(-1, owned * proj // 2)
    far_valid = lax.ppermute(own_valid, "ex", [(i, i ^ 4) for i in range(groups)])
    count = groups // 4
    spread = call(
        spread_kernel,
        jax.ShapeDtypeStruct((count, 2) + own_valid.shape, BF16),
        0,
        valid_grads.size * 2 * count,
        args=(on_chip(own_valid), on_chip(far_valid)),
    )
    members = [[y * 8 + z * 4 + i * 2 + c for y in range(groups // 8) for i in range(2)] for z in range(2) for c in range(2)]
    half = lax.all_to_all(spread, "ex", 0, 0, tiled=True, axis_index_groups=members)
    half = half.reshape(valid_count, owned * proj // 2)
    other = lax.ppermute(half, "ex", [(i, i ^ 1) for i in range(groups)])
    own_group = jnp.full((1,), lax.axis_index("ex"), jnp.int32)
    valid, valid_squares = call(
        valid_kernel,
        (
            pltpu.VMEM((valid_count, owned * proj), BF16),
            pltpu.VMEM((1, valid_count), F32),
        ),
        2 * valid_count * valid_count * owned * proj,
        2 * valid_count * owned * proj * 2,
        smem=1,
        args=(own_group, on_chip(half), on_chip(other)),
    )

    right_in = (proj_inputs.reshape(layers, tokens, inputs), frozen_adapter, right_factor.swapaxes(1, 2))
    right_parts = call(
        right_kernel,
        pltpu.VMEM((peers, layers * proj, tokens), BF16),
        2 * layers * tokens * inputs * 256,
        proj_inputs.size * 2,
        scratch=(*staged(right_in), pltpu.SemaphoreType.DMA((2 + layers,))),
        args=tuple(off_chip(x) for x in right_in),
        hbm=True,
    )
    right_parts = lax.all_to_all(right_parts, "feat", 0, 0, tiled=True)

    left_shape = pltpu.VMEM((layers, tokens, kl), BF16)
    left_in = (out_cotangent.reshape(layers, tokens, width), left_factor)
    left_high, left_low = call(
        left_kernel,
        (left_shape, left_shape),
        2 * layers * tokens * width * kl,
        (out_cotangent.size + left_factor.size) * 2 + layers * tokens * kl * 4,
        scratch=(*staged(left_in), pltpu.SemaphoreType.DMA((layers + layers * tokens // LEFT_STEP,))),
        args=tuple(off_chip(x) for x in left_in),
        hbm=True,
    )
    parts = call(
        project_kernel,
        pltpu.VMEM((peers, examples * 8, 128), BF16),
        2 * layers * tokens * kl * 256,
        layers * tokens * kl * 4,
        smem=1,
        args=(seq_lengths, on_chip(right_parts), on_chip(left_high), on_chip(left_low)),
    )
    parts = lax.all_to_all(parts, "feat", 0, 0, tiled=True)
    products = call(
        product_kernel,
        pltpu.VMEM((peers, examples + 8, valid_count), F32),
        4 * examples * valid_count * owned * proj,
        parts.size * 2 + valid.size * 2,
        scratch=(pltpu.VMEM((examples * 8, 128), F32),),
        args=(on_chip(parts), on_chip(valid), on_chip(valid_squares)),
    )
    products = lax.all_to_all(products, "feat", 0, 0, tiled=True)

    def score(part_ref, out_ref):
        score_kernel(scaling, part_ref, out_ref)

    return call(
        score,
        jax.ShapeDtypeStruct((examples, valid_count), F32),
        examples * valid_count * 16,
        products.size * 4,
        args=(on_chip(products),),
    )


def solution(mesh):
    return jax.shard_map(
        scores_of,
        mesh=mesh,
        in_specs=(
            P(None, "ex", None, "feat"),
            P(None, "ex", None, "feat"),
            P("ex"),
            P(None, None, "feat"),
            P(None, None, "feat"),
            P(),
            P("ex", "feat"),
        ),
        out_specs=P("ex", None),
        check_vma=False,
    )
```

```python
import math

import jax
import jax.numpy as jnp
from jax import lax
from jax.experimental import pallas as pl
from jax.experimental.pallas import tpu as pltpu
from jax.sharding import PartitionSpec as P


F32 = jnp.float32
BF16 = jnp.bfloat16
VMEM_LIMIT = 24 << 20
LEFT_STEP = 256
GROUP = 4
NT = (((1,), (1,)), ((), ()))
NN = (((1,), (0,)), ((), ()))


def dot(a, b, dims):
    return lax.dot_general(a, b, dims, preferred_element_type=F32)


def split(x):
    high = x.astype(BF16)
    return high, (x - high.astype(F32)).astype(BF16)


def on_chip(x):
    return pltpu.with_memory_space_constraint(x, pltpu.VMEM)


def off_chip(x):
    return pltpu.with_memory_space_constraint(x, pltpu.HBM)


def staged(arrays):
    return tuple(pltpu.VMEM(x.shape, x.dtype) for x in arrays)


def call(kernel, out_shape, flops, bytes_accessed, scratch=(), smem=0, args=(), hbm=False):
    specs = [pl.BlockSpec(memory_space=pltpu.SMEM)] * smem
    specs += [pl.BlockSpec(memory_space=pltpu.HBM if hbm else pltpu.VMEM)] * (len(args) - smem)
    return pl.pallas_call(
        kernel,
        out_shape=out_shape,
        in_specs=specs,
        out_specs=jax.tree.map(
            lambda _: pl.BlockSpec(memory_space=pltpu.VMEM), out_shape, is_leaf=lambda x: hasattr(x, "shape")
        ),
        scratch_shapes=list(scratch),
        cost_estimate=pl.CostEstimate(flops=flops, bytes_accessed=bytes_accessed, transcendentals=0),
        compiler_params=pltpu.CompilerParams(vmem_limit_bytes=VMEM_LIMIT),
    )(*args)


def right_kernel(x_hbm, a_hbm, r_hbm, out_ref, x_ref, a_ref, r_ref, sems):
    peers = out_ref.shape[0]
    layers = x_ref.shape[0]
    proj = r_ref.shape[1]
    small = [
        pltpu.make_async_copy(r_hbm, r_ref, sems.at[0]),
        pltpu.make_async_copy(a_hbm, a_ref, sems.at[1]),
    ]
    inputs = [pltpu.make_async_copy(x_hbm.at[l], x_ref.at[l], sems.at[2 + l]) for l in range(layers)]
    for copy in small + inputs:
        copy.start()
    for copy in small:
        copy.wait()
    mixes = []
    for l in range(layers):
        high, low = split(dot(r_ref[l], a_ref[l], NN))
        mixes.append(jnp.concatenate([high, low], axis=0))
    for l in range(layers):
        inputs[l].wait()
        rows = dot(mixes[l], x_ref[l], NT)
        rows = (rows[:proj] + rows[proj:]).astype(BF16)
        for p in range(peers):
            out_ref[p, l * proj:(l + 1) * proj, :] = rows


def left_kernel(c_hbm, l_hbm, high_ref, low_ref, c_ref, l_ref, sems):
    layers, tokens, _ = c_ref.shape
    step = LEFT_STEP
    factors, pieces = [], []
    for l in range(layers):
        factors.append(pltpu.make_async_copy(l_hbm.at[l], l_ref.at[l], sems.at[l]))
        factors[-1].start()
        for t in range(0, tokens, step):
            rows = pl.ds(t, step)
            copy = pltpu.make_async_copy(c_hbm.at[l, rows], c_ref.at[l, rows], sems.at[layers + len(pieces)])
            copy.start()
            pieces.append((l, t, copy))
    for l, t, copy in pieces:
        if t == 0:
            factors[l].wait()
        copy.wait()
        high, low = split(dot(c_ref[l, t:t + step, :], l_ref[l], NT))
        high_ref[l, t:t + step, :] = high
        low_ref[l, t:t + step, :] = low


def project_kernel(seq_ref, rr_ref, high_ref, low_ref, out_ref):
    peers, two_proj, tokens = rr_ref.shape
    layers, _, kl = high_ref.shape
    proj = two_proj // layers
    half = proj // 2
    owned = kl // peers
    examples = seq_ref.shape[0]
    seq = tokens // examples
    span = GROUP * seq
    width = 2 * 128
    total = rr_ref[0].astype(F32)
    for p in range(1, peers):
        total = total + rr_ref[p].astype(F32)
    first = total[:proj]
    second = total[proj:]
    lane = lax.broadcasted_iota(jnp.int32, (proj, width), 1)
    out_lane = lax.broadcasted_iota(jnp.int32, (GROUP * half, 128), 1)
    for g in range(examples // GROUP):
        x0 = first if g == 0 else pltpu.roll(first, (tokens - g * span) % tokens, 1)
        x1 = pltpu.roll(second, (tokens + span - g * span) % tokens, 1)
        x0, x1 = x0[:, :width], x1[:, :width]
        blocks = []
        for i in range(GROUP):
            start = i * seq
            stop = start + seq_ref[g * GROUP + i]
            mask0 = (lane >= start) & (lane < stop)
            mask1 = (lane >= start + span) & (lane < stop + span)
            blocks.append(jnp.where(mask0, x0, jnp.where(mask1, x1, 0.0)))
        spread = jnp.concatenate(blocks, axis=0)
        high, low = split(spread)
        both = jnp.concatenate([high, low], axis=0)[:, :layers * span]
        high = high[:, :layers * span]
        t = g * span
        left_high = jnp.concatenate([high_ref[l, t:t + span, :] for l in range(layers)], axis=0)
        left_low = jnp.concatenate([low_ref[l, t:t + span, :] for l in range(layers)], axis=0)
        rows = GROUP * proj
        part = dot(both, left_high, NN)
        part = part[:rows] + part[rows:] + dot(high, left_low, NN)
        part = part.reshape(GROUP, 2, half, kl)
        even = part[:, 0].reshape(GROUP * half, kl)
        odd = part[:, 1].reshape(GROUP * half, kl)
        for p in range(peers):
            tile = (p * owned) // 128 * 128
            e = even[:, tile:tile + 128]
            o = odd[:, tile:tile + 128]
            if (p * owned) % 128 == 0:
                o = pltpu.roll(o, 64, 1)
            else:
                e = pltpu.roll(e, 64, 1)
            both_k = jnp.where(out_lane < 64, e, o)
            r = g * GROUP * half
            out_ref[p, r:r + GROUP * half, :] = both_k.astype(BF16)


def join_kernel(near_ref, far_ref, out_ref):
    rows = near_ref.shape[0]
    out_ref[:rows] = near_ref[...]
    out_ref[rows:] = far_ref[...]


def valid_kernel(own_ref, half_ref, other_ref, out_ref, squares_ref):
    count = half_ref.shape[0]
    place = lax.broadcasted_iota(jnp.int32, (8, 2 * count), 1)
    core = ((place >> 8) ^ own_ref[0]) & 1
    far = ((place >> 7) ^ (own_ref[0] >> 2)) & 1
    index = (((place >> 4) & 7) << 5) | (far << 4) | (((place >> 3) & 1) << 3) | (core << 2) | ((place >> 1) & 3)
    row = lax.broadcasted_iota(jnp.int32, (count, 2 * count), 0)
    squares = jnp.zeros((count, 128), F32)
    for h in range(2):
        source = jnp.where((place & 1) == h, index, -1)
        order = (row == jnp.broadcast_to(source[:1], row.shape)).astype(F32).astype(BF16)
        for q in range(4):
            lanes = slice(q * 128, (q + 1) * 128)
            rows = dot(order[:, :count], half_ref[:, lanes], NN) + dot(order[:, count:], other_ref[:, lanes], NN)
            squares = squares + rows * rows
            b = h * 4 + q
            out_ref[:, b * 128:(b + 1) * 128] = rows.astype(BF16)
    squares_ref[...] = jnp.sum(squares.T, axis=0, keepdims=True)


def product_kernel(part_ref, valid_ref, squares_ref, out_ref, sum_ref):
    peers, rows, _ = part_ref.shape
    valid_count = valid_ref.shape[0]
    examples = rows // 8
    total = part_ref[0].astype(F32)
    for p in range(1, peers):
        total = total + part_ref[p].astype(F32)
    sum_ref[...] = total
    squares = jnp.sum((total * total).reshape(examples, 8, 128), axis=1)
    squares = jnp.sum(squares, axis=1, keepdims=True)
    row = lax.broadcasted_iota(jnp.int32, (examples, valid_count), 0)
    column = lax.broadcasted_iota(jnp.int32, (examples, valid_count), 1)
    train = jnp.sum(jnp.where(row == column, squares, 0.0), axis=0, keepdims=True)
    acc = jnp.zeros((2 * examples, valid_count), F32)
    for b in range(8):
        block = sum_ref[pl.ds(b, examples, stride=8), :]
        high, low = split(block)
        both = jnp.concatenate([high, low], axis=0)
        acc = acc + dot(both, valid_ref[:, b * 128:(b + 1) * 128], NT)
    products = acc[:examples] + acc[examples:]
    tail_row = lax.broadcasted_iota(jnp.int32, (8, valid_count), 0)
    tail = jnp.where(tail_row == 0, squares_ref[...], jnp.where(tail_row == 1, train, 0.0))
    for p in range(peers):
        out_ref[p, :examples, :] = products
        out_ref[p, examples:, :] = tail


def score_kernel(scaling, part_ref, out_ref):
    peers = part_ref.shape[0]
    examples, valid_count = out_ref.shape
    total = part_ref[0]
    for p in range(1, peers):
        total = total + part_ref[p]
    products = total[:examples]
    valid = jnp.sqrt(total[examples:examples + 1] + 1e-06)
    row = lax.broadcasted_iota(jnp.int32, (examples, valid_count), 0)
    column = lax.broadcasted_iota(jnp.int32, (examples, valid_count), 1)
    train = jnp.where(row == column, total[examples + 1:examples + 2], 0.0)
    train = jnp.sqrt(jnp.sum(train, axis=1, keepdims=True) + 1e-06)
    out_ref[...] = scaling * products / (train * valid)


def scores_of(proj_inputs, out_cotangent, seq_lengths, frozen_adapter, left_factor, right_factor, valid_grads):
    layers, examples, seq, inputs = proj_inputs.shape
    width = out_cotangent.shape[3]
    peers = lax.axis_size("feat")
    groups = lax.axis_size("ex")
    proj = right_factor.shape[2]
    kl = left_factor.shape[1]
    tokens = examples * seq
    owned = kl // peers
    valid_count = valid_grads.shape[0] * groups
    scaling = math.sqrt(kl * proj)

    own_valid = valid_grads.reshape(-1, owned, 2, 8).transpose(0, 3, 2, 1).reshape(1, -1, owned * proj // 2)
    own_valid = jnp.broadcast_to(own_valid, (groups // 4,) + own_valid.shape[1:])
    members = [[y * 8 + z * 4 + i * 2 + c for y in range(groups // 8) for i in range(2)] for z in range(2) for c in range(2)]
    near = lax.all_to_all(own_valid, "ex", 0, 0, tiled=True, axis_index_groups=members)
    near = near.reshape(valid_count // 2, owned * proj // 2)
    far = lax.ppermute(near, "ex", [(i, i ^ 4) for i in range(groups)])
    half = call(
        join_kernel,
        jax.ShapeDtypeStruct((valid_count, owned * proj // 2), BF16),
        0,
        2 * valid_count * owned * proj,
        args=(on_chip(near), on_chip(far)),
    )
    other = lax.ppermute(half, "ex", [(i, i ^ 1) for i in range(groups)])
    own_group = jnp.full((1,), lax.axis_index("ex"), jnp.int32)
    valid, valid_squares = call(
        valid_kernel,
        (
            pltpu.VMEM((valid_count, owned * proj), BF16),
            pltpu.VMEM((1, valid_count), F32),
        ),
        2 * valid_count * valid_count * owned * proj,
        2 * valid_count * owned * proj * 2,
        smem=1,
        args=(own_group, on_chip(half), on_chip(other)),
    )

    right_in = (proj_inputs.reshape(layers, tokens, inputs), frozen_adapter, right_factor.swapaxes(1, 2))
    right_parts = call(
        right_kernel,
        pltpu.VMEM((peers, layers * proj, tokens), BF16),
        2 * layers * tokens * inputs * 256,
        proj_inputs.size * 2,
        scratch=(*staged(right_in), pltpu.SemaphoreType.DMA((2 + layers,))),
        args=tuple(off_chip(x) for x in right_in),
        hbm=True,
    )
    right_parts = lax.all_to_all(right_parts, "feat", 0, 0, tiled=True)

    left_shape = pltpu.VMEM((layers, tokens, kl), BF16)
    left_in = (out_cotangent.reshape(layers, tokens, width), left_factor)
    left_high, left_low = call(
        left_kernel,
        (left_shape, left_shape),
        2 * layers * tokens * width * kl,
        (out_cotangent.size + left_factor.size) * 2 + layers * tokens * kl * 4,
        scratch=(*staged(left_in), pltpu.SemaphoreType.DMA((layers + layers * tokens // LEFT_STEP,))),
        args=tuple(off_chip(x) for x in left_in),
        hbm=True,
    )
    parts = call(
        project_kernel,
        pltpu.VMEM((peers, examples * 8, 128), BF16),
        2 * layers * tokens * kl * 256,
        layers * tokens * kl * 4,
        smem=1,
        args=(seq_lengths, on_chip(right_parts), on_chip(left_high), on_chip(left_low)),
    )
    parts = lax.all_to_all(parts, "feat", 0, 0, tiled=True)
    products = call(
        product_kernel,
        pltpu.VMEM((peers, examples + 8, valid_count), F32),
        4 * examples * valid_count * owned * proj,
        parts.size * 2 + valid.size * 2,
        scratch=(pltpu.VMEM((examples * 8, 128), F32),),
        args=(on_chip(parts), on_chip(valid), on_chip(valid_squares)),
    )
    products = lax.all_to_all(products, "feat", 0, 0, tiled=True)

    def score(part_ref, out_ref):
        score_kernel(scaling, part_ref, out_ref)

    return call(
        score,
        jax.ShapeDtypeStruct((examples, valid_count), F32),
        examples * valid_count * 16,
        products.size * 4,
        args=(on_chip(products),),
    )


def solution(mesh):
    return jax.shard_map(
        scores_of,
        mesh=mesh,
        in_specs=(
            P(None, "ex", None, "feat"),
            P(None, "ex", None, "feat"),
            P("ex"),
            P(None, None, "feat"),
            P(None, None, "feat"),
            P(),
            P("ex", "feat"),
        ),
        out_specs=P("ex", None),
        check_vma=False,
    )
```

```python
import math

import jax
import jax.numpy as jnp
from jax import lax
from jax.experimental import pallas as pl
from jax.experimental.pallas import tpu as pltpu
from jax.sharding import PartitionSpec as P


F32 = jnp.float32
BF16 = jnp.bfloat16
VMEM_LIMIT = 24 << 20
LEFT_STEP = 256
GROUP = 4
NT = (((1,), (1,)), ((), ()))
NN = (((1,), (0,)), ((), ()))


def dot(a, b, dims):
    return lax.dot_general(a, b, dims, preferred_element_type=F32)


def split(x):
    high = x.astype(BF16)
    return high, (x - high.astype(F32)).astype(BF16)


def on_chip(x):
    return pltpu.with_memory_space_constraint(x, pltpu.VMEM)


def off_chip(x):
    return pltpu.with_memory_space_constraint(x, pltpu.HBM)


def staged(arrays):
    return tuple(pltpu.VMEM(x.shape, x.dtype) for x in arrays)


def call(kernel, out_shape, flops, bytes_accessed, scratch=(), smem=0, args=(), hbm=(), hbm_out=()):
    specs = [pl.BlockSpec(memory_space=pltpu.SMEM)] * smem
    specs += [pl.BlockSpec(memory_space=pltpu.HBM if n in hbm else pltpu.VMEM) for n in range(smem, len(args))]
    if isinstance(out_shape, tuple):
        out_specs = tuple(
            pl.BlockSpec(memory_space=pltpu.HBM if n in hbm_out else pltpu.VMEM) for n in range(len(out_shape))
        )
    else:
        out_specs = pl.BlockSpec(memory_space=pltpu.VMEM)
    return pl.pallas_call(
        kernel,
        out_shape=out_shape,
        in_specs=specs,
        out_specs=out_specs,
        scratch_shapes=list(scratch),
        cost_estimate=pl.CostEstimate(flops=flops, bytes_accessed=bytes_accessed, transcendentals=0),
        compiler_params=pltpu.CompilerParams(vmem_limit_bytes=VMEM_LIMIT),
    )(*args)


def right_kernel(x_hbm, a_hbm, r_hbm, out_ref, x_ref, a_ref, r_ref, sems):
    peers = out_ref.shape[0]
    layers = x_ref.shape[0]
    proj = r_ref.shape[1]
    small = [
        pltpu.make_async_copy(r_hbm, r_ref, sems.at[0]),
        pltpu.make_async_copy(a_hbm, a_ref, sems.at[1]),
    ]
    inputs = [pltpu.make_async_copy(x_hbm.at[l], x_ref.at[l], sems.at[2 + l]) for l in range(layers)]
    for copy in small + inputs:
        copy.start()
    for copy in small:
        copy.wait()
    mixes = []
    for l in range(layers):
        high, low = split(dot(r_ref[l], a_ref[l], NN))
        mixes.append(jnp.concatenate([high, low], axis=0))
    for l in range(layers):
        inputs[l].wait()
        rows = dot(mixes[l], x_ref[l], NT)
        rows = (rows[:proj] + rows[proj:]).astype(BF16)
        for p in range(peers):
            out_ref[p, l * proj:(l + 1) * proj, :] = rows


def left_kernel(c_hbm, l_hbm, high_ref, low_hbm, c_ref, l_ref, low_ref, sems):
    layers, tokens, _ = c_ref.shape
    step = LEFT_STEP
    factors, pieces = [], []
    for l in range(layers):
        factors.append(pltpu.make_async_copy(l_hbm.at[l], l_ref.at[l], sems.at[l]))
        factors[-1].start()
        for t in range(0, tokens, step):
            rows = pl.ds(t, step)
            copy = pltpu.make_async_copy(c_hbm.at[l, rows], c_ref.at[l, rows], sems.at[layers + len(pieces)])
            copy.start()
            pieces.append((l, t, copy))
    stores = []
    for l, t, copy in pieces:
        if t == 0:
            factors[l].wait()
        copy.wait()
        rows = pl.ds(t, step)
        high, low = split(dot(c_ref[l, t:t + step, :], l_ref[l], NT))
        high_ref[l, t:t + step, :] = high
        low_ref[l, t:t + step, :] = low
        sem = sems.at[layers + len(pieces) + len(stores)]
        stores.append(pltpu.make_async_copy(low_ref.at[l, rows], low_hbm.at[l, rows], sem))
        stores[-1].start()
    for store in stores:
        store.wait()


def project_kernel(seq_ref, rr_ref, high_ref, low_hbm, out_ref, low_ref, sems):
    peers, two_proj, tokens = rr_ref.shape
    layers, _, kl = high_ref.shape
    proj = two_proj // layers
    half = proj // 2
    owned = kl // peers
    examples = seq_ref.shape[0]
    seq = tokens // examples
    span = GROUP * seq
    width = 2 * 128
    chunk = 2 * span
    loads = []
    for t in range(0, tokens, chunk):
        rows = pl.ds(t, chunk)
        for l in range(layers):
            load = pltpu.make_async_copy(low_hbm.at[l, rows], low_ref.at[l, rows], sems.at[len(loads)])
            load.start()
            loads.append(load)
    total = rr_ref[0].astype(F32)
    for p in range(1, peers):
        total = total + rr_ref[p].astype(F32)
    first = total[:proj]
    second = total[proj:]
    lane = lax.broadcasted_iota(jnp.int32, (proj, width), 1)
    out_lane = lax.broadcasted_iota(jnp.int32, (GROUP * half, 128), 1)
    for g in range(examples // GROUP):
        x0 = first if g == 0 else pltpu.roll(first, (tokens - g * span) % tokens, 1)
        x1 = pltpu.roll(second, (tokens + span - g * span) % tokens, 1)
        x0, x1 = x0[:, :width], x1[:, :width]
        blocks = []
        for i in range(GROUP):
            start = i * seq
            stop = start + seq_ref[g * GROUP + i]
            mask0 = (lane >= start) & (lane < stop)
            mask1 = (lane >= start + span) & (lane < stop + span)
            blocks.append(jnp.where(mask0, x0, jnp.where(mask1, x1, 0.0)))
        spread = jnp.concatenate(blocks, axis=0)
        high, low = split(spread)
        both = jnp.concatenate([high, low], axis=0)[:, :layers * span]
        high = high[:, :layers * span]
        t = g * span
        if t % chunk == 0:
            for l in range(layers):
                loads[t // chunk * layers + l].wait()
        left_high = jnp.concatenate([high_ref[l, t:t + span, :] for l in range(layers)], axis=0)
        left_low = jnp.concatenate([low_ref[l, t:t + span, :] for l in range(layers)], axis=0)
        rows = GROUP * proj
        part = dot(both, left_high, NN)
        part = part[:rows] + part[rows:] + dot(high, left_low, NN)
        part = part.reshape(GROUP, 2, half, kl)
        even = part[:, 0].reshape(GROUP * half, kl)
        odd = part[:, 1].reshape(GROUP * half, kl)
        for p in range(peers):
            tile = (p * owned) // 128 * 128
            e = even[:, tile:tile + 128]
            o = odd[:, tile:tile + 128]
            if (p * owned) % 128 == 0:
                o = pltpu.roll(o, 64, 1)
            else:
                e = pltpu.roll(e, 64, 1)
            both_k = jnp.where(out_lane < 64, e, o)
            r = g * GROUP * half
            out_ref[p, r:r + GROUP * half, :] = both_k.astype(BF16)


def join_kernel(near_ref, far_ref, out_ref):
    rows = near_ref.shape[0]
    out_ref[:rows] = near_ref[...]
    out_ref[rows:] = far_ref[...]


def valid_kernel(own_ref, half_ref, other_ref, out_ref, squares_ref):
    count = half_ref.shape[0]
    place = lax.broadcasted_iota(jnp.int32, (8, 2 * count), 1)
    core = ((place >> 8) ^ own_ref[0]) & 1
    far = ((place >> 7) ^ (own_ref[0] >> 2)) & 1
    index = (((place >> 4) & 7) << 5) | (far << 4) | (((place >> 3) & 1) << 3) | (core << 2) | ((place >> 1) & 3)
    row = lax.broadcasted_iota(jnp.int32, (count, 2 * count), 0)
    squares = jnp.zeros((count, 128), F32)
    for h in range(2):
        source = jnp.where((place & 1) == h, index, -1)
        order = (row == jnp.broadcast_to(source[:1], row.shape)).astype(F32).astype(BF16)
        for q in range(4):
            lanes = slice(q * 128, (q + 1) * 128)
            rows = dot(order[:, :count], half_ref[:, lanes], NN) + dot(order[:, count:], other_ref[:, lanes], NN)
            squares = squares + rows * rows
            b = h * 4 + q
            out_ref[:, b * 128:(b + 1) * 128] = rows.astype(BF16)
    squares_ref[...] = jnp.sum(squares.T, axis=0, keepdims=True)


def product_kernel(part_ref, valid_ref, squares_ref, out_ref, sum_ref):
    peers, rows, _ = part_ref.shape
    valid_count = valid_ref.shape[0]
    examples = rows // 8
    total = part_ref[0].astype(F32)
    for p in range(1, peers):
        total = total + part_ref[p].astype(F32)
    sum_ref[...] = total
    squares = jnp.sum((total * total).reshape(examples, 8, 128), axis=1)
    squares = jnp.sum(squares, axis=1, keepdims=True)
    row = lax.broadcasted_iota(jnp.int32, (examples, valid_count), 0)
    column = lax.broadcasted_iota(jnp.int32, (examples, valid_count), 1)
    train = jnp.sum(jnp.where(row == column, squares, 0.0), axis=0, keepdims=True)
    acc = jnp.zeros((2 * examples, valid_count), F32)
    for b in range(8):
        block = sum_ref[pl.ds(b, examples, stride=8), :]
        high, low = split(block)
        both = jnp.concatenate([high, low], axis=0)
        acc = acc + dot(both, valid_ref[:, b * 128:(b + 1) * 128], NT)
    products = acc[:examples] + acc[examples:]
    tail_row = lax.broadcasted_iota(jnp.int32, (8, valid_count), 0)
    tail = jnp.where(tail_row == 0, squares_ref[...], jnp.where(tail_row == 1, train, 0.0))
    for p in range(peers):
        out_ref[p, :examples, :] = products
        out_ref[p, examples:, :] = tail


def score_kernel(scaling, part_ref, out_ref):
    peers = part_ref.shape[0]
    examples, valid_count = out_ref.shape
    total = part_ref[0]
    for p in range(1, peers):
        total = total + part_ref[p]
    products = total[:examples]
    valid = jnp.sqrt(total[examples:examples + 1] + 1e-06)
    row = lax.broadcasted_iota(jnp.int32, (examples, valid_count), 0)
    column = lax.broadcasted_iota(jnp.int32, (examples, valid_count), 1)
    train = jnp.where(row == column, total[examples + 1:examples + 2], 0.0)
    train = jnp.sqrt(jnp.sum(train, axis=1, keepdims=True) + 1e-06)
    out_ref[...] = scaling * products / (train * valid)


def scores_of(proj_inputs, out_cotangent, seq_lengths, frozen_adapter, left_factor, right_factor, valid_grads):
    layers, examples, seq, inputs = proj_inputs.shape
    width = out_cotangent.shape[3]
    peers = lax.axis_size("feat")
    groups = lax.axis_size("ex")
    proj = right_factor.shape[2]
    kl = left_factor.shape[1]
    tokens = examples * seq
    owned = kl // peers
    valid_count = valid_grads.shape[0] * groups
    scaling = math.sqrt(kl * proj)

    own_valid = valid_grads.reshape(-1, owned, 2, 8).transpose(0, 3, 2, 1).reshape(1, -1, owned * proj // 2)
    own_valid = jnp.broadcast_to(own_valid, (groups // 4,) + own_valid.shape[1:])
    members = [[y * 8 + z * 4 + i * 2 + c for y in range(groups // 8) for i in range(2)] for z in range(2) for c in range(2)]
    near = lax.all_to_all(own_valid, "ex", 0, 0, tiled=True, axis_index_groups=members)
    near = near.reshape(valid_count // 2, owned * proj // 2)
    far = lax.ppermute(near, "ex", [(i, i ^ 4) for i in range(groups)])
    half = call(
        join_kernel,
        jax.ShapeDtypeStruct((valid_count, owned * proj // 2), BF16),
        0,
        2 * valid_count * owned * proj,
        args=(on_chip(near), on_chip(far)),
    )
    other = lax.ppermute(half, "ex", [(i, i ^ 1) for i in range(groups)])
    own_group = jnp.full((1,), lax.axis_index("ex"), jnp.int32)
    valid, valid_squares = call(
        valid_kernel,
        (
            pltpu.VMEM((valid_count, owned * proj), BF16),
            pltpu.VMEM((1, valid_count), F32),
        ),
        2 * valid_count * valid_count * owned * proj,
        2 * valid_count * owned * proj * 2,
        smem=1,
        args=(own_group, on_chip(half), on_chip(other)),
    )

    right_in = (proj_inputs.reshape(layers, tokens, inputs), frozen_adapter, right_factor.swapaxes(1, 2))
    right_parts = call(
        right_kernel,
        pltpu.VMEM((peers, layers * proj, tokens), BF16),
        2 * layers * tokens * inputs * 256,
        proj_inputs.size * 2,
        scratch=(*staged(right_in), pltpu.SemaphoreType.DMA((2 + layers,))),
        args=tuple(off_chip(x) for x in right_in),
        hbm=(0, 1, 2),
    )
    right_parts = lax.all_to_all(right_parts, "feat", 0, 0, tiled=True)

    left_shape = (layers, tokens, kl)
    left_copies = layers * tokens // LEFT_STEP
    left_in = (out_cotangent.reshape(layers, tokens, width), left_factor)
    left_high, left_low = call(
        left_kernel,
        (pltpu.VMEM(left_shape, BF16), pltpu.HBM(left_shape, BF16)),
        2 * layers * tokens * width * kl,
        (out_cotangent.size + left_factor.size) * 2 + layers * tokens * kl * 4,
        scratch=(*staged(left_in), pltpu.VMEM(left_shape, BF16), pltpu.SemaphoreType.DMA((layers + 2 * left_copies,))),
        args=tuple(off_chip(x) for x in left_in),
        hbm=(0, 1),
        hbm_out=(1,),
    )
    parts = call(
        project_kernel,
        pltpu.VMEM((peers, examples * 8, 128), BF16),
        2 * layers * tokens * kl * 256,
        layers * tokens * kl * 4,
        scratch=(
            pltpu.VMEM(left_shape, BF16),
            pltpu.SemaphoreType.DMA((layers * examples // (2 * GROUP),)),
        ),
        smem=1,
        args=(seq_lengths, on_chip(right_parts), on_chip(left_high), off_chip(left_low)),
        hbm=(3,),
    )
    parts = lax.all_to_all(parts, "feat", 0, 0, tiled=True)
    products = call(
        product_kernel,
        pltpu.VMEM((peers, examples + 8, valid_count), F32),
        4 * examples * valid_count * owned * proj,
        parts.size * 2 + valid.size * 2,
        scratch=(pltpu.VMEM((examples * 8, 128), F32),),
        args=(on_chip(parts), on_chip(valid), on_chip(valid_squares)),
    )
    products = lax.all_to_all(products, "feat", 0, 0, tiled=True)

    def score(part_ref, out_ref):
        score_kernel(scaling, part_ref, out_ref)

    return call(
        score,
        jax.ShapeDtypeStruct((examples, valid_count), F32),
        examples * valid_count * 16,
        products.size * 4,
        args=(on_chip(products),),
    )


def solution(mesh):
    return jax.shard_map(
        scores_of,
        mesh=mesh,
        in_specs=(
            P(None, "ex", None, "feat"),
            P(None, "ex", None, "feat"),
            P("ex"),
            P(None, None, "feat"),
            P(None, None, "feat"),
            P(),
            P("ex", "feat"),
        ),
        out_specs=P("ex", None),
        check_vma=False,
    )
```

```python
import math

import jax
import jax.numpy as jnp
from jax import lax
from jax.experimental import pallas as pl
from jax.experimental.pallas import tpu as pltpu
from jax.sharding import PartitionSpec as P


F32 = jnp.float32
BF16 = jnp.bfloat16
VMEM_LIMIT = 24 << 20
LEFT_STEP = 192
LOW_KEPT = 576
GROUP = 4
NT = (((1,), (1,)), ((), ()))
NN = (((1,), (0,)), ((), ()))


def dot(a, b, dims):
    return lax.dot_general(a, b, dims, preferred_element_type=F32)


def split(x):
    high = x.astype(BF16)
    return high, (x - high.astype(F32)).astype(BF16)


def on_chip(x):
    return pltpu.with_memory_space_constraint(x, pltpu.VMEM)


def off_chip(x):
    return pltpu.with_memory_space_constraint(x, pltpu.HBM)


def staged(arrays):
    return tuple(pltpu.VMEM(x.shape, x.dtype) for x in arrays)


def call(kernel, out_shape, flops, bytes_accessed, scratch=(), smem=0, args=(), hbm=(), hbm_out=()):
    specs = [pl.BlockSpec(memory_space=pltpu.SMEM)] * smem
    specs += [pl.BlockSpec(memory_space=pltpu.HBM if n in hbm else pltpu.VMEM) for n in range(smem, len(args))]
    if isinstance(out_shape, tuple):
        out_specs = tuple(
            pl.BlockSpec(memory_space=pltpu.HBM if n in hbm_out else pltpu.VMEM) for n in range(len(out_shape))
        )
    else:
        out_specs = pl.BlockSpec(memory_space=pltpu.VMEM)
    return pl.pallas_call(
        kernel,
        out_shape=out_shape,
        in_specs=specs,
        out_specs=out_specs,
        scratch_shapes=list(scratch),
        cost_estimate=pl.CostEstimate(flops=flops, bytes_accessed=bytes_accessed, transcendentals=0),
        compiler_params=pltpu.CompilerParams(vmem_limit_bytes=VMEM_LIMIT),
    )(*args)


def right_kernel(x_hbm, a_hbm, r_hbm, out_ref, x_ref, a_ref, r_ref, sems):
    peers = out_ref.shape[0]
    layers = x_ref.shape[0]
    proj = r_ref.shape[1]
    small = [
        pltpu.make_async_copy(r_hbm, r_ref, sems.at[0]),
        pltpu.make_async_copy(a_hbm, a_ref, sems.at[1]),
    ]
    inputs = [pltpu.make_async_copy(x_hbm.at[l], x_ref.at[l], sems.at[2 + l]) for l in range(layers)]
    for copy in small + inputs:
        copy.start()
    for copy in small:
        copy.wait()
    mixes = []
    for l in range(layers):
        high, low = split(dot(r_ref[l], a_ref[l], NN))
        mixes.append(jnp.concatenate([high, low], axis=0))
    for l in range(layers):
        inputs[l].wait()
        rows = dot(mixes[l], x_ref[l], NT)
        rows = (rows[:proj] + rows[proj:]).astype(BF16)
        for p in range(peers):
            out_ref[p, l * proj:(l + 1) * proj, :] = rows


def left_kernel(c_hbm, l_hbm, high_ref, kept_ref, low_hbm, c_ref, l_ref, low_ref, sems):
    layers, tokens, _ = c_ref.shape
    kept = kept_ref.shape[1]
    step = LEFT_STEP
    factors, pieces = [], []
    for l in range(layers):
        factors.append(pltpu.make_async_copy(l_hbm.at[l], l_ref.at[l], sems.at[l]))
        factors[-1].start()
        for t in range(0, tokens, step):
            rows = pl.ds(t, step)
            copy = pltpu.make_async_copy(c_hbm.at[l, rows], c_ref.at[l, rows], sems.at[layers + len(pieces)])
            copy.start()
            pieces.append((l, t, copy))
    stores = []
    for l, t, copy in pieces:
        if t == 0:
            factors[l].wait()
        copy.wait()
        high, low = split(dot(c_ref[l, t:t + step, :], l_ref[l], NT))
        high_ref[l, t:t + step, :] = high
        if t < kept:
            kept_ref[l, t:t + step, :] = low
            continue
        low_ref[l, t - kept:t - kept + step, :] = low
        rows = pl.ds(t - kept, step)
        sem = sems.at[layers + len(pieces) + len(stores)]
        stores.append(pltpu.make_async_copy(low_ref.at[l, rows], low_hbm.at[l, rows], sem))
        stores[-1].start()
    for store in stores:
        store.wait()


def project_kernel(seq_ref, rr_ref, high_ref, kept_ref, low_hbm, out_ref, low_ref, sems):
    peers, two_proj, tokens = rr_ref.shape
    layers, _, kl = high_ref.shape
    proj = two_proj // layers
    half = proj // 2
    owned = kl // peers
    examples = seq_ref.shape[0]
    seq = tokens // examples
    span = GROUP * seq
    width = 2 * 128
    kept = kept_ref.shape[1]
    chunk = 2 * span
    loads = []
    for t in range(0, tokens - kept, chunk):
        rows = pl.ds(t, chunk)
        for l in range(layers):
            load = pltpu.make_async_copy(low_hbm.at[l, rows], low_ref.at[l, rows], sems.at[len(loads)])
            load.start()
            loads.append(load)
    total = rr_ref[0].astype(F32)
    for p in range(1, peers):
        total = total + rr_ref[p].astype(F32)
    first = total[:proj]
    second = total[proj:]
    lane = lax.broadcasted_iota(jnp.int32, (proj, width), 1)
    out_lane = lax.broadcasted_iota(jnp.int32, (GROUP * half, 128), 1)
    for g in range(examples // GROUP):
        x0 = first if g == 0 else pltpu.roll(first, (tokens - g * span) % tokens, 1)
        x1 = pltpu.roll(second, (tokens + span - g * span) % tokens, 1)
        x0, x1 = x0[:, :width], x1[:, :width]
        blocks = []
        for i in range(GROUP):
            start = i * seq
            stop = start + seq_ref[g * GROUP + i]
            mask0 = (lane >= start) & (lane < stop)
            mask1 = (lane >= start + span) & (lane < stop + span)
            blocks.append(jnp.where(mask0, x0, jnp.where(mask1, x1, 0.0)))
        spread = jnp.concatenate(blocks, axis=0)
        high, low = split(spread)
        both = jnp.concatenate([high, low], axis=0)[:, :layers * span]
        high = high[:, :layers * span]
        t = g * span
        if t >= kept and (t - kept) % chunk == 0:
            for l in range(layers):
                loads[(t - kept) // chunk * layers + l].wait()
        source, first_row = (kept_ref, t) if t < kept else (low_ref, t - kept)
        left_high = jnp.concatenate([high_ref[l, t:t + span, :] for l in range(layers)], axis=0)
        left_low = jnp.concatenate([source[l, first_row:first_row + span, :] for l in range(layers)], axis=0)
        rows = GROUP * proj
        part = dot(both, left_high, NN)
        part = part[:rows] + part[rows:] + dot(high, left_low, NN)
        part = part.reshape(GROUP, 2, half, kl)
        even = part[:, 0].reshape(GROUP * half, kl)
        odd = part[:, 1].reshape(GROUP * half, kl)
        for p in range(peers):
            tile = (p * owned) // 128 * 128
            e = even[:, tile:tile + 128]
            o = odd[:, tile:tile + 128]
            if (p * owned) % 128 == 0:
                o = pltpu.roll(o, 64, 1)
            else:
                e = pltpu.roll(e, 64, 1)
            both_k = jnp.where(out_lane < 64, e, o)
            r = g * GROUP * half
            out_ref[p, r:r + GROUP * half, :] = both_k.astype(BF16)


def join_kernel(near_ref, far_ref, out_ref):
    rows = near_ref.shape[0]
    out_ref[:rows] = near_ref[...]
    out_ref[rows:] = far_ref[...]


def valid_kernel(own_ref, half_ref, other_ref, out_ref, squares_ref):
    count = half_ref.shape[0]
    place = lax.broadcasted_iota(jnp.int32, (8, 2 * count), 1)
    core = ((place >> 8) ^ own_ref[0]) & 1
    far = ((place >> 7) ^ (own_ref[0] >> 2)) & 1
    index = (((place >> 4) & 7) << 5) | (far << 4) | (((place >> 3) & 1) << 3) | (core << 2) | ((place >> 1) & 3)
    row = lax.broadcasted_iota(jnp.int32, (count, 2 * count), 0)
    squares = jnp.zeros((count, 128), F32)
    for h in range(2):
        source = jnp.where((place & 1) == h, index, -1)
        order = (row == jnp.broadcast_to(source[:1], row.shape)).astype(F32).astype(BF16)
        for q in range(4):
            lanes = slice(q * 128, (q + 1) * 128)
            rows = dot(order[:, :count], half_ref[:, lanes], NN) + dot(order[:, count:], other_ref[:, lanes], NN)
            squares = squares + rows * rows
            b = h * 4 + q
            out_ref[:, b * 128:(b + 1) * 128] = rows.astype(BF16)
    squares_ref[...] = jnp.sum(squares.T, axis=0, keepdims=True)


def product_kernel(part_ref, valid_ref, squares_ref, out_ref, sum_ref):
    peers, rows, _ = part_ref.shape
    valid_count = valid_ref.shape[0]
    examples = rows // 8
    total = part_ref[0].astype(F32)
    for p in range(1, peers):
        total = total + part_ref[p].astype(F32)
    sum_ref[...] = total
    squares = jnp.sum((total * total).reshape(examples, 8, 128), axis=1)
    squares = jnp.sum(squares, axis=1, keepdims=True)
    row = lax.broadcasted_iota(jnp.int32, (examples, valid_count), 0)
    column = lax.broadcasted_iota(jnp.int32, (examples, valid_count), 1)
    train = jnp.sum(jnp.where(row == column, squares, 0.0), axis=0, keepdims=True)
    acc = jnp.zeros((2 * examples, valid_count), F32)
    for b in range(8):
        block = sum_ref[pl.ds(b, examples, stride=8), :]
        high, low = split(block)
        both = jnp.concatenate([high, low], axis=0)
        acc = acc + dot(both, valid_ref[:, b * 128:(b + 1) * 128], NT)
    products = acc[:examples] + acc[examples:]
    tail_row = lax.broadcasted_iota(jnp.int32, (8, valid_count), 0)
    tail = jnp.where(tail_row == 0, squares_ref[...], jnp.where(tail_row == 1, train, 0.0))
    for p in range(peers):
        out_ref[p, :examples, :] = products
        out_ref[p, examples:, :] = tail


def score_kernel(scaling, part_ref, out_ref):
    peers = part_ref.shape[0]
    examples, valid_count = out_ref.shape
    total = part_ref[0]
    for p in range(1, peers):
        total = total + part_ref[p]
    products = total[:examples]
    valid = jnp.sqrt(total[examples:examples + 1] + 1e-06)
    row = lax.broadcasted_iota(jnp.int32, (examples, valid_count), 0)
    column = lax.broadcasted_iota(jnp.int32, (examples, valid_count), 1)
    train = jnp.where(row == column, total[examples + 1:examples + 2], 0.0)
    train = jnp.sqrt(jnp.sum(train, axis=1, keepdims=True) + 1e-06)
    out_ref[...] = scaling * products / (train * valid)


def scores_of(proj_inputs, out_cotangent, seq_lengths, frozen_adapter, left_factor, right_factor, valid_grads):
    layers, examples, seq, inputs = proj_inputs.shape
    width = out_cotangent.shape[3]
    peers = lax.axis_size("feat")
    groups = lax.axis_size("ex")
    proj = right_factor.shape[2]
    kl = left_factor.shape[1]
    tokens = examples * seq
    owned = kl // peers
    valid_count = valid_grads.shape[0] * groups
    scaling = math.sqrt(kl * proj)

    own_valid = valid_grads.reshape(-1, owned, 2, 8).transpose(0, 3, 2, 1).reshape(1, -1, owned * proj // 2)
    own_valid = jnp.broadcast_to(own_valid, (groups // 4,) + own_valid.shape[1:])
    members = [[y * 8 + z * 4 + i * 2 + c for y in range(groups // 8) for i in range(2)] for z in range(2) for c in range(2)]
    near = lax.all_to_all(own_valid, "ex", 0, 0, tiled=True, axis_index_groups=members)
    near = near.reshape(valid_count // 2, owned * proj // 2)
    far = lax.ppermute(near, "ex", [(i, i ^ 4) for i in range(groups)])
    half = call(
        join_kernel,
        jax.ShapeDtypeStruct((valid_count, owned * proj // 2), BF16),
        0,
        2 * valid_count * owned * proj,
        args=(on_chip(near), on_chip(far)),
    )
    other = lax.ppermute(half, "ex", [(i, i ^ 1) for i in range(groups)])
    own_group = jnp.full((1,), lax.axis_index("ex"), jnp.int32)
    valid, valid_squares = call(
        valid_kernel,
        (
            pltpu.VMEM((valid_count, owned * proj), BF16),
            pltpu.VMEM((1, valid_count), F32),
        ),
        2 * valid_count * valid_count * owned * proj,
        2 * valid_count * owned * proj * 2,
        smem=1,
        args=(own_group, on_chip(half), on_chip(other)),
    )

    right_in = (proj_inputs.reshape(layers, tokens, inputs), frozen_adapter, right_factor.swapaxes(1, 2))
    right_parts = call(
        right_kernel,
        pltpu.VMEM((peers, layers * proj, tokens), BF16),
        2 * layers * tokens * inputs * 256,
        proj_inputs.size * 2,
        scratch=(*staged(right_in), pltpu.SemaphoreType.DMA((2 + layers,))),
        args=tuple(off_chip(x) for x in right_in),
        hbm=(0, 1, 2),
    )
    right_parts = lax.all_to_all(right_parts, "feat", 0, 0, tiled=True)

    left_shape = (layers, tokens, kl)
    low_shape = (layers, tokens - LOW_KEPT, kl)
    left_copies = layers * tokens // LEFT_STEP
    left_in = (out_cotangent.reshape(layers, tokens, width), left_factor)
    left_high, left_kept, left_low = call(
        left_kernel,
        (
            pltpu.VMEM(left_shape, BF16),
            pltpu.VMEM((layers, LOW_KEPT, kl), BF16),
            pltpu.HBM(low_shape, BF16),
        ),
        2 * layers * tokens * width * kl,
        (out_cotangent.size + left_factor.size) * 2 + layers * tokens * kl * 4,
        scratch=(*staged(left_in), pltpu.VMEM(low_shape, BF16), pltpu.SemaphoreType.DMA((layers + 2 * left_copies,))),
        args=tuple(off_chip(x) for x in left_in),
        hbm=(0, 1),
        hbm_out=(2,),
    )
    parts = call(
        project_kernel,
        pltpu.VMEM((peers, examples * 8, 128), BF16),
        2 * layers * tokens * kl * 256,
        layers * tokens * kl * 4,
        scratch=(
            pltpu.VMEM(low_shape, BF16),
            pltpu.SemaphoreType.DMA((layers * examples // (2 * GROUP),)),
        ),
        smem=1,
        args=(seq_lengths, on_chip(right_parts), on_chip(left_high), on_chip(left_kept), off_chip(left_low)),
        hbm=(4,),
    )
    parts = lax.all_to_all(parts, "feat", 0, 0, tiled=True)
    products = call(
        product_kernel,
        pltpu.VMEM((peers, examples + 8, valid_count), F32),
        4 * examples * valid_count * owned * proj,
        parts.size * 2 + valid.size * 2,
        scratch=(pltpu.VMEM((examples * 8, 128), F32),),
        args=(on_chip(parts), on_chip(valid), on_chip(valid_squares)),
    )
    products = lax.all_to_all(products, "feat", 0, 0, tiled=True)

    def score(part_ref, out_ref):
        score_kernel(scaling, part_ref, out_ref)

    return call(
        score,
        jax.ShapeDtypeStruct((examples, valid_count), F32),
        examples * valid_count * 16,
        products.size * 4,
        args=(on_chip(products),),
    )


def solution(mesh):
    return jax.shard_map(
        scores_of,
        mesh=mesh,
        in_specs=(
            P(None, "ex", None, "feat"),
            P(None, "ex", None, "feat"),
            P("ex"),
            P(None, None, "feat"),
            P(None, None, "feat"),
            P(),
            P("ex", "feat"),
        ),
        out_specs=P("ex", None),
        check_vma=False,
    )
```

```python
import math

import jax
import jax.numpy as jnp
from jax import lax
from jax.experimental import pallas as pl
from jax.experimental.pallas import tpu as pltpu
from jax.sharding import PartitionSpec as P


F32 = jnp.float32
BF16 = jnp.bfloat16
VMEM_LIMIT = 24 << 20
LEFT_STEP = 96
LOW_KEPT = 672
GROUP = 4
NT = (((1,), (1,)), ((), ()))
NN = (((1,), (0,)), ((), ()))


def dot(a, b, dims):
    return lax.dot_general(a, b, dims, preferred_element_type=F32)


def split(x):
    high = x.astype(BF16)
    return high, (x - high.astype(F32)).astype(BF16)


def on_chip(x):
    return pltpu.with_memory_space_constraint(x, pltpu.VMEM)


def off_chip(x):
    return pltpu.with_memory_space_constraint(x, pltpu.HBM)


def staged(arrays):
    return tuple(pltpu.VMEM(x.shape, x.dtype) for x in arrays)


def call(kernel, out_shape, flops, bytes_accessed, scratch=(), smem=0, args=(), hbm=(), hbm_out=()):
    specs = [pl.BlockSpec(memory_space=pltpu.SMEM)] * smem
    specs += [pl.BlockSpec(memory_space=pltpu.HBM if n in hbm else pltpu.VMEM) for n in range(smem, len(args))]
    if isinstance(out_shape, tuple):
        out_specs = tuple(
            pl.BlockSpec(memory_space=pltpu.HBM if n in hbm_out else pltpu.VMEM) for n in range(len(out_shape))
        )
    else:
        out_specs = pl.BlockSpec(memory_space=pltpu.VMEM)
    return pl.pallas_call(
        kernel,
        out_shape=out_shape,
        in_specs=specs,
        out_specs=out_specs,
        scratch_shapes=list(scratch),
        cost_estimate=pl.CostEstimate(flops=flops, bytes_accessed=bytes_accessed, transcendentals=0),
        compiler_params=pltpu.CompilerParams(vmem_limit_bytes=VMEM_LIMIT),
    )(*args)


def right_kernel(x_hbm, a_hbm, r_hbm, out_ref, x_ref, a_ref, r_ref, sems):
    peers = out_ref.shape[0]
    layers = x_ref.shape[0]
    proj = r_ref.shape[1]
    small = [
        pltpu.make_async_copy(r_hbm, r_ref, sems.at[0]),
        pltpu.make_async_copy(a_hbm, a_ref, sems.at[1]),
    ]
    inputs = [pltpu.make_async_copy(x_hbm.at[l], x_ref.at[l], sems.at[2 + l]) for l in range(layers)]
    for copy in small + inputs:
        copy.start()
    for copy in small:
        copy.wait()
    mixes = []
    for l in range(layers):
        high, low = split(dot(r_ref[l], a_ref[l], NN))
        mixes.append(jnp.concatenate([high, low], axis=0))
    for l in range(layers):
        inputs[l].wait()
        rows = dot(mixes[l], x_ref[l], NT)
        rows = (rows[:proj] + rows[proj:]).astype(BF16)
        for p in range(peers):
            out_ref[p, l * proj:(l + 1) * proj, :] = rows


def left_kernel(c_hbm, l_hbm, high_ref, kept_ref, low_hbm, c_ref, l_ref, low_ref, sems):
    layers, tokens, _ = c_ref.shape
    kept = kept_ref.shape[1]
    step = LEFT_STEP
    factors, pieces = [], []
    for l in range(layers):
        factors.append(pltpu.make_async_copy(l_hbm.at[l], l_ref.at[l], sems.at[l]))
        factors[-1].start()
        for t in range(0, tokens, step):
            rows = pl.ds(t, step)
            copy = pltpu.make_async_copy(c_hbm.at[l, rows], c_ref.at[l, rows], sems.at[layers + len(pieces)])
            copy.start()
            pieces.append((l, t, copy))
    stores = []
    for l, t, copy in pieces:
        if t == 0:
            factors[l].wait()
        copy.wait()
        high, low = split(dot(c_ref[l, t:t + step, :], l_ref[l], NT))
        high_ref[l, t:t + step, :] = high
        if t < kept:
            kept_ref[l, t:t + step, :] = low
            continue
        low_ref[l, t - kept:t - kept + step, :] = low
        rows = pl.ds(t - kept, step)
        sem = sems.at[layers + len(pieces) + len(stores)]
        stores.append(pltpu.make_async_copy(low_ref.at[l, rows], low_hbm.at[l, rows], sem))
        stores[-1].start()
    for store in stores:
        store.wait()


def project_kernel(seq_ref, rr_ref, high_ref, kept_ref, low_hbm, out_hbm, out_ref, low_ref, sems, out_sems):
    peers, two_proj, tokens = rr_ref.shape
    layers, _, kl = high_ref.shape
    proj = two_proj // layers
    half = proj // 2
    owned = kl // peers
    examples = seq_ref.shape[0]
    seq = tokens // examples
    span = GROUP * seq
    width = 2 * 128
    kept = kept_ref.shape[1]
    chunk = span
    loads = []
    for t in range(0, tokens - kept, chunk):
        rows = pl.ds(t, chunk)
        for l in range(layers):
            load = pltpu.make_async_copy(low_hbm.at[l, rows], low_ref.at[l, rows], sems.at[len(loads)])
            load.start()
            loads.append(load)
    total = rr_ref[0].astype(F32)
    for p in range(1, peers):
        total = total + rr_ref[p].astype(F32)
    first = total[:proj]
    second = total[proj:]
    lane = lax.broadcasted_iota(jnp.int32, (proj, width), 1)
    out_lane = lax.broadcasted_iota(jnp.int32, (GROUP * half, 128), 1)
    stores = []
    for g in range(examples // GROUP):
        x0 = first if g == 0 else pltpu.roll(first, (tokens - g * span) % tokens, 1)
        x1 = pltpu.roll(second, (tokens + span - g * span) % tokens, 1)
        x0, x1 = x0[:, :width], x1[:, :width]
        blocks = []
        for i in range(GROUP):
            start = i * seq
            stop = start + seq_ref[g * GROUP + i]
            mask0 = (lane >= start) & (lane < stop)
            mask1 = (lane >= start + span) & (lane < stop + span)
            blocks.append(jnp.where(mask0, x0, jnp.where(mask1, x1, 0.0)))
        spread = jnp.concatenate(blocks, axis=0)
        high, low = split(spread)
        both = jnp.concatenate([high, low], axis=0)[:, :layers * span]
        high = high[:, :layers * span]
        t = g * span
        if t >= kept and (t - kept) % chunk == 0:
            for l in range(layers):
                loads[(t - kept) // chunk * layers + l].wait()
        source, first_row = (kept_ref, t) if t < kept else (low_ref, t - kept)
        left_high = jnp.concatenate([high_ref[l, t:t + span, :] for l in range(layers)], axis=0)
        left_low = jnp.concatenate([source[l, first_row:first_row + span, :] for l in range(layers)], axis=0)
        rows = GROUP * proj
        part = dot(both, left_high, NN)
        part = part[:rows] + part[rows:] + dot(high, left_low, NN)
        part = part.reshape(GROUP, 2, half, kl)
        even = part[:, 0].reshape(GROUP * half, kl)
        odd = part[:, 1].reshape(GROUP * half, kl)
        for p in range(peers):
            tile = (p * owned) // 128 * 128
            e = even[:, tile:tile + 128]
            o = odd[:, tile:tile + 128]
            if (p * owned) % 128 == 0:
                o = pltpu.roll(o, 64, 1)
            else:
                e = pltpu.roll(e, 64, 1)
            both_k = jnp.where(out_lane < 64, e, o)
            r = g * GROUP * half
            out_ref[p, r:r + GROUP * half, :] = both_k.astype(BF16)
        rows = pl.ds(g * GROUP * half, GROUP * half)
        stores.append(pltpu.make_async_copy(out_ref.at[:, rows], out_hbm.at[:, rows], out_sems.at[g]))
        stores[-1].start()
    for store in stores:
        store.wait()


def join_kernel(near_ref, far_ref, out_ref):
    rows = near_ref.shape[0]
    out_ref[:rows] = near_ref[...]
    out_ref[rows:] = far_ref[...]


def valid_kernel(own_ref, half_ref, other_ref, out_ref, squares_ref):
    count = half_ref.shape[0]
    place = lax.broadcasted_iota(jnp.int32, (8, 2 * count), 1)
    core = ((place >> 8) ^ own_ref[0]) & 1
    far = ((place >> 7) ^ (own_ref[0] >> 2)) & 1
    index = (((place >> 4) & 7) << 5) | (far << 4) | (((place >> 3) & 1) << 3) | (core << 2) | ((place >> 1) & 3)
    row = lax.broadcasted_iota(jnp.int32, (count, 2 * count), 0)
    squares = jnp.zeros((count, 128), F32)
    for h in range(2):
        source = jnp.where((place & 1) == h, index, -1)
        order = (row == jnp.broadcast_to(source[:1], row.shape)).astype(F32).astype(BF16)
        for q in range(4):
            lanes = slice(q * 128, (q + 1) * 128)
            rows = dot(order[:, :count], half_ref[:, lanes], NN) + dot(order[:, count:], other_ref[:, lanes], NN)
            squares = squares + rows * rows
            b = h * 4 + q
            out_ref[:, b * 128:(b + 1) * 128] = rows.astype(BF16)
    squares_ref[...] = jnp.sum(squares.T, axis=0, keepdims=True)


def product_kernel(part_ref, valid_ref, squares_ref, out_ref, sum_ref):
    peers, rows, _ = part_ref.shape
    valid_count = valid_ref.shape[0]
    examples = rows // 8
    total = part_ref[0].astype(F32)
    for p in range(1, peers):
        total = total + part_ref[p].astype(F32)
    sum_ref[...] = total
    squares = jnp.sum((total * total).reshape(examples, 8, 128), axis=1)
    squares = jnp.sum(squares, axis=1, keepdims=True)
    row = lax.broadcasted_iota(jnp.int32, (examples, valid_count), 0)
    column = lax.broadcasted_iota(jnp.int32, (examples, valid_count), 1)
    train = jnp.sum(jnp.where(row == column, squares, 0.0), axis=0, keepdims=True)
    acc = jnp.zeros((2 * examples, valid_count), F32)
    for b in range(8):
        block = sum_ref[pl.ds(b, examples, stride=8), :]
        high, low = split(block)
        both = jnp.concatenate([high, low], axis=0)
        acc = acc + dot(both, valid_ref[:, b * 128:(b + 1) * 128], NT)
    products = acc[:examples] + acc[examples:]
    tail_row = lax.broadcasted_iota(jnp.int32, (8, valid_count), 0)
    tail = jnp.where(tail_row == 0, squares_ref[...], jnp.where(tail_row == 1, train, 0.0))
    for p in range(peers):
        out_ref[p, :examples, :] = products
        out_ref[p, examples:, :] = tail


def score_kernel(scaling, part_ref, out_ref):
    peers = part_ref.shape[0]
    examples, valid_count = out_ref.shape
    total = part_ref[0]
    for p in range(1, peers):
        total = total + part_ref[p]
    products = total[:examples]
    valid = jnp.sqrt(total[examples:examples + 1] + 1e-06)
    row = lax.broadcasted_iota(jnp.int32, (examples, valid_count), 0)
    column = lax.broadcasted_iota(jnp.int32, (examples, valid_count), 1)
    train = jnp.where(row == column, total[examples + 1:examples + 2], 0.0)
    train = jnp.sqrt(jnp.sum(train, axis=1, keepdims=True) + 1e-06)
    out_ref[...] = scaling * products / (train * valid)


def scores_of(proj_inputs, out_cotangent, seq_lengths, frozen_adapter, left_factor, right_factor, valid_grads):
    layers, examples, seq, inputs = proj_inputs.shape
    width = out_cotangent.shape[3]
    peers = lax.axis_size("feat")
    groups = lax.axis_size("ex")
    proj = right_factor.shape[2]
    kl = left_factor.shape[1]
    tokens = examples * seq
    owned = kl // peers
    valid_count = valid_grads.shape[0] * groups
    scaling = math.sqrt(kl * proj)

    own_valid = valid_grads.reshape(-1, owned, 2, 8).transpose(0, 3, 2, 1).reshape(1, -1, owned * proj // 2)
    own_valid = jnp.broadcast_to(own_valid, (groups // 4,) + own_valid.shape[1:])
    members = [[y * 8 + z * 4 + i * 2 + c for y in range(groups // 8) for i in range(2)] for z in range(2) for c in range(2)]
    near = lax.all_to_all(own_valid, "ex", 0, 0, tiled=True, axis_index_groups=members)
    near = near.reshape(valid_count // 2, owned * proj // 2)
    far = lax.ppermute(near, "ex", [(i, i ^ 4) for i in range(groups)])
    half = call(
        join_kernel,
        jax.ShapeDtypeStruct((valid_count, owned * proj // 2), BF16),
        0,
        2 * valid_count * owned * proj,
        args=(on_chip(near), on_chip(far)),
    )
    other = lax.ppermute(half, "ex", [(i, i ^ 1) for i in range(groups)])
    own_group = jnp.full((1,), lax.axis_index("ex"), jnp.int32)
    valid, valid_squares = call(
        valid_kernel,
        (
            pltpu.VMEM((valid_count, owned * proj), BF16),
            pltpu.VMEM((1, valid_count), F32),
        ),
        2 * valid_count * valid_count * owned * proj,
        2 * valid_count * owned * proj * 2,
        smem=1,
        args=(own_group, on_chip(half), on_chip(other)),
    )

    right_in = (proj_inputs.reshape(layers, tokens, inputs), frozen_adapter, right_factor.swapaxes(1, 2))
    right_parts = call(
        right_kernel,
        pltpu.VMEM((peers, layers * proj, tokens), BF16),
        2 * layers * tokens * inputs * 256,
        proj_inputs.size * 2,
        scratch=(*staged(right_in), pltpu.SemaphoreType.DMA((2 + layers,))),
        args=tuple(off_chip(x) for x in right_in),
        hbm=(0, 1, 2),
    )
    right_parts = lax.all_to_all(right_parts, "feat", 0, 0, tiled=True)

    left_shape = (layers, tokens, kl)
    low_shape = (layers, tokens - LOW_KEPT, kl)
    left_copies = layers * tokens // LEFT_STEP
    left_in = (out_cotangent.reshape(layers, tokens, width), left_factor)
    left_high, left_kept, left_low = call(
        left_kernel,
        (
            pltpu.VMEM(left_shape, BF16),
            pltpu.VMEM((layers, LOW_KEPT, kl), BF16),
            pltpu.HBM(low_shape, BF16),
        ),
        2 * layers * tokens * width * kl,
        (out_cotangent.size + left_factor.size) * 2 + layers * tokens * kl * 4,
        scratch=(*staged(left_in), pltpu.VMEM(low_shape, BF16), pltpu.SemaphoreType.DMA((layers + 2 * left_copies,))),
        args=tuple(off_chip(x) for x in left_in),
        hbm=(0, 1),
        hbm_out=(2,),
    )
    parts_shape = (peers, examples * 8, 128)
    (parts,) = call(
        project_kernel,
        (pltpu.HBM(parts_shape, BF16),),
        2 * layers * tokens * kl * 256,
        layers * tokens * kl * 4,
        scratch=(
            pltpu.VMEM(parts_shape, BF16),
            pltpu.VMEM(low_shape, BF16),
            pltpu.SemaphoreType.DMA((layers * examples // GROUP,)),
            pltpu.SemaphoreType.DMA((examples // GROUP,)),
        ),
        smem=1,
        args=(seq_lengths, on_chip(right_parts), on_chip(left_high), on_chip(left_kept), off_chip(left_low)),
        hbm=(4,),
        hbm_out=(0,),
    )
    parts = lax.all_to_all(parts, "feat", 0, 0, tiled=True)
    products = call(
        product_kernel,
        pltpu.VMEM((peers, examples + 8, valid_count), F32),
        4 * examples * valid_count * owned * proj,
        parts.size * 2 + valid.size * 2,
        scratch=(pltpu.VMEM((examples * 8, 128), F32),),
        args=(on_chip(parts), on_chip(valid), on_chip(valid_squares)),
    )
    products = lax.all_to_all(products, "feat", 0, 0, tiled=True)

    def score(part_ref, out_ref):
        score_kernel(scaling, part_ref, out_ref)

    return call(
        score,
        jax.ShapeDtypeStruct((examples, valid_count), F32),
        examples * valid_count * 16,
        products.size * 4,
        args=(on_chip(products),),
    )


def solution(mesh):
    return jax.shard_map(
        scores_of,
        mesh=mesh,
        in_specs=(
            P(None, "ex", None, "feat"),
            P(None, "ex", None, "feat"),
            P("ex"),
            P(None, None, "feat"),
            P(None, None, "feat"),
            P(),
            P("ex", "feat"),
        ),
        out_specs=P("ex", None),
        check_vma=False,
    )
```

```python
import math

import jax
import jax.numpy as jnp
from jax import lax
from jax.experimental import pallas as pl
from jax.experimental.pallas import tpu as pltpu
from jax.sharding import PartitionSpec as P


F32 = jnp.float32
BF16 = jnp.bfloat16
VMEM_LIMIT = 24 << 20
LEFT_STEP = 256
LOW_ROWS = 672
GROUP = 4
NT = (((1,), (1,)), ((), ()))
NN = (((1,), (0,)), ((), ()))


def dot(a, b, dims):
    return lax.dot_general(a, b, dims, preferred_element_type=F32)


def split(x):
    high = x.astype(BF16)
    return high, (x - high.astype(F32)).astype(BF16)


def on_chip(x):
    return pltpu.with_memory_space_constraint(x, pltpu.VMEM)


def off_chip(x):
    return pltpu.with_memory_space_constraint(x, pltpu.HBM)


def staged(arrays):
    return tuple(pltpu.VMEM(x.shape, x.dtype) for x in arrays)


def call(kernel, out_shape, flops, bytes_accessed, scratch=(), smem=0, args=(), hbm=(), hbm_out=()):
    specs = [pl.BlockSpec(memory_space=pltpu.SMEM)] * smem
    specs += [pl.BlockSpec(memory_space=pltpu.HBM if n in hbm else pltpu.VMEM) for n in range(smem, len(args))]
    if isinstance(out_shape, tuple):
        out_specs = tuple(
            pl.BlockSpec(memory_space=pltpu.HBM if n in hbm_out else pltpu.VMEM) for n in range(len(out_shape))
        )
    else:
        out_specs = pl.BlockSpec(memory_space=pltpu.VMEM)
    return pl.pallas_call(
        kernel,
        out_shape=out_shape,
        in_specs=specs,
        out_specs=out_specs,
        scratch_shapes=list(scratch),
        cost_estimate=pl.CostEstimate(flops=flops, bytes_accessed=bytes_accessed, transcendentals=0),
        compiler_params=pltpu.CompilerParams(vmem_limit_bytes=VMEM_LIMIT),
    )(*args)


def right_kernel(x_hbm, a_hbm, r_hbm, out_ref, x_ref, a_ref, r_ref, sems):
    peers = out_ref.shape[0]
    layers = x_ref.shape[0]
    proj = r_ref.shape[1]
    small = [
        pltpu.make_async_copy(r_hbm, r_ref, sems.at[0]),
        pltpu.make_async_copy(a_hbm, a_ref, sems.at[1]),
    ]
    inputs = [pltpu.make_async_copy(x_hbm.at[l], x_ref.at[l], sems.at[2 + l]) for l in range(layers)]
    for copy in small + inputs:
        copy.start()
    for copy in small:
        copy.wait()
    mixes = []
    for l in range(layers):
        high, low = split(dot(r_ref[l], a_ref[l], NN))
        mixes.append(jnp.concatenate([high, low], axis=0))
    for l in range(layers):
        inputs[l].wait()
        rows = dot(mixes[l], x_ref[l], NT)
        rows = (rows[:proj] + rows[proj:]).astype(BF16)
        for p in range(peers):
            out_ref[p, l * proj:(l + 1) * proj, :] = rows


def left_kernel(c_hbm, l_hbm, high_ref, low_ref, c_ref, l_ref, sems):
    layers, tokens, _ = c_ref.shape
    step = LEFT_STEP
    factors, pieces = [], []
    for l in range(layers):
        factors.append(pltpu.make_async_copy(l_hbm.at[l], l_ref.at[l], sems.at[l]))
        factors[-1].start()
        for t in range(0, tokens, step):
            rows = pl.ds(t, step)
            copy = pltpu.make_async_copy(c_hbm.at[l, rows], c_ref.at[l, rows], sems.at[layers + len(pieces)])
            copy.start()
            pieces.append((l, t, copy))
    for l, t, copy in pieces:
        if t == 0:
            factors[l].wait()
        copy.wait()
        high, low = split(dot(c_ref[l, t:t + step, :], l_ref[l], NT))
        high_ref[l, t:t + step, :] = high
        stop = min(t + step, low_ref.shape[1])
        if t < stop:
            low_ref[l, t:stop, :] = low[:stop - t]


def project_kernel(seq_ref, rr_ref, high_ref, low_ref, out_hbm, out_ref, out_sems):
    peers, two_proj, tokens = rr_ref.shape
    layers, _, kl = high_ref.shape
    proj = two_proj // layers
    half = proj // 2
    owned = kl // peers
    examples = seq_ref.shape[0]
    seq = tokens // examples
    span = GROUP * seq
    width = 2 * 128
    total = rr_ref[0].astype(F32)
    for p in range(1, peers):
        total = total + rr_ref[p].astype(F32)
    first = total[:proj]
    second = total[proj:]
    lane = lax.broadcasted_iota(jnp.int32, (proj, width), 1)
    out_lane = lax.broadcasted_iota(jnp.int32, (GROUP * half, 128), 1)
    stores = []
    for g in range(examples // GROUP):
        x0 = first if g == 0 else pltpu.roll(first, (tokens - g * span) % tokens, 1)
        x1 = pltpu.roll(second, (tokens + span - g * span) % tokens, 1)
        x0, x1 = x0[:, :width], x1[:, :width]
        blocks = []
        for i in range(GROUP):
            start = i * seq
            stop = start + seq_ref[g * GROUP + i]
            mask0 = (lane >= start) & (lane < stop)
            mask1 = (lane >= start + span) & (lane < stop + span)
            blocks.append(jnp.where(mask0, x0, jnp.where(mask1, x1, 0.0)))
        spread = jnp.concatenate(blocks, axis=0)
        high, low = split(spread)
        both = jnp.concatenate([high, low], axis=0)[:, :layers * span]
        high = high[:, :layers * span]
        t = g * span
        left_high = jnp.concatenate([high_ref[l, t:t + span, :] for l in range(layers)], axis=0)
        rows = GROUP * proj
        part = dot(both, left_high, NN)
        part = part[:rows] + part[rows:]
        if t < low_ref.shape[1]:
            left_low = jnp.concatenate([low_ref[l, t:t + span, :] for l in range(layers)], axis=0)
            part = part + dot(high, left_low, NN)
        part = part.reshape(GROUP, 2, half, kl)
        even = part[:, 0].reshape(GROUP * half, kl)
        odd = part[:, 1].reshape(GROUP * half, kl)
        for p in range(peers):
            tile = (p * owned) // 128 * 128
            e = even[:, tile:tile + 128]
            o = odd[:, tile:tile + 128]
            if (p * owned) % 128 == 0:
                o = pltpu.roll(o, 64, 1)
            else:
                e = pltpu.roll(e, 64, 1)
            both_k = jnp.where(out_lane < 64, e, o)
            r = g * GROUP * half
            out_ref[p, r:r + GROUP * half, :] = both_k.astype(BF16)
        rows = pl.ds(g * GROUP * half, GROUP * half)
        stores.append(pltpu.make_async_copy(out_ref.at[:, rows], out_hbm.at[:, rows], out_sems.at[g]))
        stores[-1].start()
    for store in stores:
        store.wait()


def join_kernel(near_ref, far_ref, out_ref):
    rows = near_ref.shape[0]
    out_ref[:rows] = near_ref[...]
    out_ref[rows:] = far_ref[...]


def valid_kernel(own_ref, half_ref, other_ref, out_ref, squares_ref):
    count = half_ref.shape[0]
    place = lax.broadcasted_iota(jnp.int32, (8, 2 * count), 1)
    core = ((place >> 8) ^ own_ref[0]) & 1
    far = ((place >> 7) ^ (own_ref[0] >> 2)) & 1
    index = (((place >> 4) & 7) << 5) | (far << 4) | (((place >> 3) & 1) << 3) | (core << 2) | ((place >> 1) & 3)
    row = lax.broadcasted_iota(jnp.int32, (count, 2 * count), 0)
    squares = jnp.zeros((count, 128), F32)
    for h in range(2):
        source = jnp.where((place & 1) == h, index, -1)
        order = (row == jnp.broadcast_to(source[:1], row.shape)).astype(F32).astype(BF16)
        for q in range(4):
            lanes = slice(q * 128, (q + 1) * 128)
            rows = dot(order[:, :count], half_ref[:, lanes], NN) + dot(order[:, count:], other_ref[:, lanes], NN)
            squares = squares + rows * rows
            b = h * 4 + q
            out_ref[:, b * 128:(b + 1) * 128] = rows.astype(BF16)
    squares_ref[...] = jnp.sum(squares.T, axis=0, keepdims=True)


def product_kernel(part_ref, valid_ref, squares_ref, out_ref, sum_ref):
    peers, rows, _ = part_ref.shape
    valid_count = valid_ref.shape[0]
    examples = rows // 8
    total = part_ref[0].astype(F32)
    for p in range(1, peers):
        total = total + part_ref[p].astype(F32)
    sum_ref[...] = total
    squares = jnp.sum((total * total).reshape(examples, 8, 128), axis=1)
    squares = jnp.sum(squares, axis=1, keepdims=True)
    row = lax.broadcasted_iota(jnp.int32, (examples, valid_count), 0)
    column = lax.broadcasted_iota(jnp.int32, (examples, valid_count), 1)
    train = jnp.sum(jnp.where(row == column, squares, 0.0), axis=0, keepdims=True)
    acc = jnp.zeros((2 * examples, valid_count), F32)
    for b in range(8):
        block = sum_ref[pl.ds(b, examples, stride=8), :]
        high, low = split(block)
        both = jnp.concatenate([high, low], axis=0)
        acc = acc + dot(both, valid_ref[:, b * 128:(b + 1) * 128], NT)
    products = acc[:examples] + acc[examples:]
    tail_row = lax.broadcasted_iota(jnp.int32, (8, valid_count), 0)
    tail = jnp.where(tail_row == 0, squares_ref[...], jnp.where(tail_row == 1, train, 0.0))
    for p in range(peers):
        out_ref[p, :examples, :] = products
        out_ref[p, examples:, :] = tail


def score_kernel(scaling, part_ref, out_ref):
    peers = part_ref.shape[0]
    examples, valid_count = out_ref.shape
    total = part_ref[0]
    for p in range(1, peers):
        total = total + part_ref[p]
    products = total[:examples]
    valid = jnp.sqrt(total[examples:examples + 1] + 1e-06)
    row = lax.broadcasted_iota(jnp.int32, (examples, valid_count), 0)
    column = lax.broadcasted_iota(jnp.int32, (examples, valid_count), 1)
    train = jnp.where(row == column, total[examples + 1:examples + 2], 0.0)
    train = jnp.sqrt(jnp.sum(train, axis=1, keepdims=True) + 1e-06)
    out_ref[...] = scaling * products / (train * valid)


def scores_of(proj_inputs, out_cotangent, seq_lengths, frozen_adapter, left_factor, right_factor, valid_grads):
    layers, examples, seq, inputs = proj_inputs.shape
    width = out_cotangent.shape[3]
    peers = lax.axis_size("feat")
    groups = lax.axis_size("ex")
    proj = right_factor.shape[2]
    kl = left_factor.shape[1]
    tokens = examples * seq
    owned = kl // peers
    valid_count = valid_grads.shape[0] * groups
    scaling = math.sqrt(kl * proj)

    own_valid = valid_grads.reshape(-1, owned, 2, 8).transpose(0, 3, 2, 1).reshape(1, -1, owned * proj // 2)
    own_valid = jnp.broadcast_to(own_valid, (groups // 4,) + own_valid.shape[1:])
    members = [[y * 8 + z * 4 + i * 2 + c for y in range(groups // 8) for i in range(2)] for z in range(2) for c in range(2)]
    near = lax.all_to_all(own_valid, "ex", 0, 0, tiled=True, axis_index_groups=members)
    near = near.reshape(valid_count // 2, owned * proj // 2)
    far = lax.ppermute(near, "ex", [(i, i ^ 4) for i in range(groups)])
    half = call(
        join_kernel,
        jax.ShapeDtypeStruct((valid_count, owned * proj // 2), BF16),
        0,
        2 * valid_count * owned * proj,
        args=(on_chip(near), on_chip(far)),
    )
    other = lax.ppermute(half, "ex", [(i, i ^ 1) for i in range(groups)])
    own_group = jnp.full((1,), lax.axis_index("ex"), jnp.int32)
    valid, valid_squares = call(
        valid_kernel,
        (
            pltpu.VMEM((valid_count, owned * proj), BF16),
            pltpu.VMEM((1, valid_count), F32),
        ),
        2 * valid_count * valid_count * owned * proj,
        2 * valid_count * owned * proj * 2,
        smem=1,
        args=(own_group, on_chip(half), on_chip(other)),
    )

    right_in = (proj_inputs.reshape(layers, tokens, inputs), frozen_adapter, right_factor.swapaxes(1, 2))
    right_parts = call(
        right_kernel,
        pltpu.VMEM((peers, layers * proj, tokens), BF16),
        2 * layers * tokens * inputs * 256,
        proj_inputs.size * 2,
        scratch=(*staged(right_in), pltpu.SemaphoreType.DMA((2 + layers,))),
        args=tuple(off_chip(x) for x in right_in),
        hbm=(0, 1, 2),
    )
    right_parts = lax.all_to_all(right_parts, "feat", 0, 0, tiled=True)

    left_shape = (layers, tokens, kl)
    left_copies = layers * tokens // LEFT_STEP
    left_in = (out_cotangent.reshape(layers, tokens, width), left_factor)
    left_high, left_low = call(
        left_kernel,
        (
            pltpu.VMEM(left_shape, BF16),
            pltpu.VMEM((layers, LOW_ROWS, kl), BF16),
        ),
        2 * layers * tokens * width * kl,
        (out_cotangent.size + left_factor.size) * 2 + layers * tokens * kl * 4,
        scratch=(*staged(left_in), pltpu.SemaphoreType.DMA((layers + left_copies,))),
        args=tuple(off_chip(x) for x in left_in),
        hbm=(0, 1),
    )
    parts_shape = (peers, examples * 8, 128)
    (parts,) = call(
        project_kernel,
        (pltpu.HBM(parts_shape, BF16),),
        2 * layers * tokens * kl * 256,
        layers * tokens * kl * 4,
        scratch=(pltpu.VMEM(parts_shape, BF16), pltpu.SemaphoreType.DMA((examples // GROUP,))),
        hbm_out=(0,),
        smem=1,
        args=(seq_lengths, on_chip(right_parts), on_chip(left_high), on_chip(left_low)),
    )
    parts = lax.all_to_all(parts, "feat", 0, 0, tiled=True)
    products = call(
        product_kernel,
        pltpu.VMEM((peers, examples + 8, valid_count), F32),
        4 * examples * valid_count * owned * proj,
        parts.size * 2 + valid.size * 2,
        scratch=(pltpu.VMEM((examples * 8, 128), F32),),
        args=(on_chip(parts), on_chip(valid), on_chip(valid_squares)),
    )
    products = lax.all_to_all(products, "feat", 0, 0, tiled=True)

    def score(part_ref, out_ref):
        score_kernel(scaling, part_ref, out_ref)

    return call(
        score,
        jax.ShapeDtypeStruct((examples, valid_count), F32),
        examples * valid_count * 16,
        products.size * 4,
        args=(on_chip(products),),
    )


def solution(mesh):
    return jax.shard_map(
        scores_of,
        mesh=mesh,
        in_specs=(
            P(None, "ex", None, "feat"),
            P(None, "ex", None, "feat"),
            P("ex"),
            P(None, None, "feat"),
            P(None, None, "feat"),
            P(),
            P("ex", "feat"),
        ),
        out_specs=P("ex", None),
        check_vma=False,
    )
```

```python
import math

import jax
import jax.numpy as jnp
from jax import lax
from jax.experimental import pallas as pl
from jax.experimental.pallas import tpu as pltpu
from jax.sharding import PartitionSpec as P


F32 = jnp.float32
BF16 = jnp.bfloat16
VMEM_LIMIT = 24 << 20
LEFT_STEP = 256
GROUP = 4
NT = (((1,), (1,)), ((), ()))
NN = (((1,), (0,)), ((), ()))


def dot(a, b, dims):
    return lax.dot_general(a, b, dims, preferred_element_type=F32)


def split(x):
    high = x.astype(BF16)
    return high, (x - high.astype(F32)).astype(BF16)


def on_chip(x):
    return pltpu.with_memory_space_constraint(x, pltpu.VMEM)


def off_chip(x):
    return pltpu.with_memory_space_constraint(x, pltpu.HBM)


def staged(arrays):
    return tuple(pltpu.VMEM(x.shape, x.dtype) for x in arrays)


def call(kernel, out_shape, flops, bytes_accessed, scratch=(), smem=0, args=(), hbm=(), hbm_out=()):
    specs = [pl.BlockSpec(memory_space=pltpu.SMEM)] * smem
    specs += [pl.BlockSpec(memory_space=pltpu.HBM if n in hbm else pltpu.VMEM) for n in range(smem, len(args))]
    if isinstance(out_shape, tuple):
        out_specs = tuple(
            pl.BlockSpec(memory_space=pltpu.HBM if n in hbm_out else pltpu.VMEM) for n in range(len(out_shape))
        )
    else:
        out_specs = pl.BlockSpec(memory_space=pltpu.VMEM)
    return pl.pallas_call(
        kernel,
        out_shape=out_shape,
        in_specs=specs,
        out_specs=out_specs,
        scratch_shapes=list(scratch),
        cost_estimate=pl.CostEstimate(flops=flops, bytes_accessed=bytes_accessed, transcendentals=0),
        compiler_params=pltpu.CompilerParams(vmem_limit_bytes=VMEM_LIMIT),
    )(*args)


def right_kernel(x_hbm, a_hbm, r_hbm, out_ref, x_ref, a_ref, r_ref, sems):
    layers = x_ref.shape[0]
    proj = r_ref.shape[1]
    small = [
        pltpu.make_async_copy(r_hbm, r_ref, sems.at[0]),
        pltpu.make_async_copy(a_hbm, a_ref, sems.at[1]),
    ]
    inputs = [pltpu.make_async_copy(x_hbm.at[l], x_ref.at[l], sems.at[2 + l]) for l in range(layers)]
    for copy in small + inputs:
        copy.start()
    for copy in small:
        copy.wait()
    mixes = []
    for l in range(layers):
        high, low = split(dot(r_ref[l], a_ref[l], NN))
        mixes.append(jnp.concatenate([high, low], axis=0))
    for l in range(layers):
        inputs[l].wait()
        rows = dot(mixes[l], x_ref[l], NT)
        out_ref[l * proj:(l + 1) * proj, :] = rows[:proj] + rows[proj:]


def pair_kernel(own_ref, other_ref, out_ref):
    total = own_ref[...] + other_ref[...]
    for p in range(out_ref.shape[0]):
        out_ref[p] = total


def left_kernel(c_hbm, l_hbm, out_ref, c_ref, l_ref, sems):
    layers, tokens, _ = c_ref.shape
    step = LEFT_STEP
    factors, pieces = [], []
    for l in range(layers):
        factors.append(pltpu.make_async_copy(l_hbm.at[l], l_ref.at[l], sems.at[l]))
        factors[-1].start()
        for t in range(0, tokens, step):
            rows = pl.ds(t, step)
            copy = pltpu.make_async_copy(c_hbm.at[l, rows], c_ref.at[l, rows], sems.at[layers + len(pieces)])
            copy.start()
            pieces.append((l, t, copy))
    for l, t, copy in pieces:
        if t == 0:
            factors[l].wait()
        copy.wait()
        out_ref[l, t:t + step, :] = dot(c_ref[l, t:t + step, :], l_ref[l], NT).astype(BF16)


def project_kernel(seq_ref, rr_ref, left_ref, out_hbm, out_ref, out_sems):
    parts, two_proj, tokens = rr_ref.shape
    layers, _, kl = left_ref.shape
    peers = out_ref.shape[0]
    proj = two_proj // layers
    half = proj // 2
    owned = kl // peers
    examples = seq_ref.shape[0]
    seq = tokens // examples
    span = GROUP * seq
    width = 2 * 128
    total = rr_ref[0]
    for p in range(1, parts):
        total = total + rr_ref[p]
    first = total[:proj]
    second = total[proj:]
    lane = lax.broadcasted_iota(jnp.int32, (proj, width), 1)
    out_lane = lax.broadcasted_iota(jnp.int32, (GROUP * half, 128), 1)
    stores = []
    for g in range(examples // GROUP):
        x0 = first if g == 0 else pltpu.roll(first, (tokens - g * span) % tokens, 1)
        x1 = pltpu.roll(second, (tokens + span - g * span) % tokens, 1)
        x0, x1 = x0[:, :width], x1[:, :width]
        blocks = []
        for i in range(GROUP):
            start = i * seq
            stop = start + seq_ref[g * GROUP + i]
            mask0 = (lane >= start) & (lane < stop)
            mask1 = (lane >= start + span) & (lane < stop + span)
            blocks.append(jnp.where(mask0, x0, jnp.where(mask1, x1, 0.0)))
        spread = jnp.concatenate(blocks, axis=0).astype(BF16)[:, :layers * span]
        t = g * span
        left = jnp.concatenate([left_ref[l, t:t + span, :] for l in range(layers)], axis=0)
        part = dot(spread, left, NN)
        part = part.reshape(GROUP, 2, half, kl)
        even = part[:, 0].reshape(GROUP * half, kl)
        odd = part[:, 1].reshape(GROUP * half, kl)
        for p in range(peers):
            tile = (p * owned) // 128 * 128
            e = even[:, tile:tile + 128]
            o = odd[:, tile:tile + 128]
            if (p * owned) % 128 == 0:
                o = pltpu.roll(o, 64, 1)
            else:
                e = pltpu.roll(e, 64, 1)
            both_k = jnp.where(out_lane < 64, e, o)
            r = g * GROUP * half
            out_ref[p, r:r + GROUP * half, :] = both_k.astype(BF16)
        rows = pl.ds(g * GROUP * half, GROUP * half)
        stores.append(pltpu.make_async_copy(out_ref.at[:, rows], out_hbm.at[:, rows], out_sems.at[g]))
        stores[-1].start()
    for store in stores:
        store.wait()


def join_kernel(near_ref, far_ref, out_ref):
    rows = near_ref.shape[0]
    out_ref[:rows] = near_ref[...]
    out_ref[rows:] = far_ref[...]


def valid_kernel(own_ref, half_ref, other_ref, out_ref, squares_ref):
    count = half_ref.shape[0]
    place = lax.broadcasted_iota(jnp.int32, (8, 2 * count), 1)
    core = ((place >> 8) ^ own_ref[0]) & 1
    far = ((place >> 7) ^ (own_ref[0] >> 2)) & 1
    index = (((place >> 4) & 7) << 5) | (far << 4) | (((place >> 3) & 1) << 3) | (core << 2) | ((place >> 1) & 3)
    row = lax.broadcasted_iota(jnp.int32, (count, 2 * count), 0)
    squares = jnp.zeros((count, 128), F32)
    for h in range(2):
        source = jnp.where((place & 1) == h, index, -1)
        order = (row == jnp.broadcast_to(source[:1], row.shape)).astype(F32).astype(BF16)
        for q in range(4):
            lanes = slice(q * 128, (q + 1) * 128)
            rows = dot(order[:, :count], half_ref[:, lanes], NN) + dot(order[:, count:], other_ref[:, lanes], NN)
            squares = squares + rows * rows
            b = h * 4 + q
            out_ref[:, b * 128:(b + 1) * 128] = rows.astype(BF16)
    squares_ref[...] = jnp.sum(squares.T, axis=0, keepdims=True)


def product_kernel(part_ref, valid_ref, squares_ref, out_ref, sum_ref):
    peers, rows, _ = part_ref.shape
    valid_count = valid_ref.shape[0]
    examples = rows // 8
    total = part_ref[0].astype(F32)
    for p in range(1, peers):
        total = total + part_ref[p].astype(F32)
    sum_ref[...] = total
    squares = jnp.sum((total * total).reshape(examples, 8, 128), axis=1)
    squares = jnp.sum(squares, axis=1, keepdims=True)
    row = lax.broadcasted_iota(jnp.int32, (examples, valid_count), 0)
    column = lax.broadcasted_iota(jnp.int32, (examples, valid_count), 1)
    train = jnp.sum(jnp.where(row == column, squares, 0.0), axis=0, keepdims=True)
    acc = jnp.zeros((2 * examples, valid_count), F32)
    for b in range(8):
        block = sum_ref[pl.ds(b, examples, stride=8), :]
        high, low = split(block)
        both = jnp.concatenate([high, low], axis=0)
        acc = acc + dot(both, valid_ref[:, b * 128:(b + 1) * 128], NT)
    products = acc[:examples] + acc[examples:]
    tail_row = lax.broadcasted_iota(jnp.int32, (8, valid_count), 0)
    tail = jnp.where(tail_row == 0, squares_ref[...], jnp.where(tail_row == 1, train, 0.0))
    for p in range(peers):
        out_ref[p, :examples, :] = products
        out_ref[p, examples:, :] = tail


def score_kernel(scaling, part_ref, out_ref):
    peers = part_ref.shape[0]
    examples, valid_count = out_ref.shape
    total = part_ref[0]
    for p in range(1, peers):
        total = total + part_ref[p]
    products = total[:examples]
    valid = jnp.sqrt(total[examples:examples + 1] + 1e-06)
    row = lax.broadcasted_iota(jnp.int32, (examples, valid_count), 0)
    column = lax.broadcasted_iota(jnp.int32, (examples, valid_count), 1)
    train = jnp.where(row == column, total[examples + 1:examples + 2], 0.0)
    train = jnp.sqrt(jnp.sum(train, axis=1, keepdims=True) + 1e-06)
    out_ref[...] = scaling * products / (train * valid)


def scores_of(proj_inputs, out_cotangent, seq_lengths, frozen_adapter, left_factor, right_factor, valid_grads):
    layers, examples, seq, inputs = proj_inputs.shape
    width = out_cotangent.shape[3]
    peers = lax.axis_size("feat")
    groups = lax.axis_size("ex")
    proj = right_factor.shape[2]
    kl = left_factor.shape[1]
    tokens = examples * seq
    owned = kl // peers
    valid_count = valid_grads.shape[0] * groups
    scaling = math.sqrt(kl * proj)

    own_valid = valid_grads.reshape(-1, owned, 2, 8).transpose(0, 3, 2, 1).reshape(1, -1, owned * proj // 2)
    own_valid = jnp.broadcast_to(own_valid, (groups // 4,) + own_valid.shape[1:])
    members = [[y * 8 + z * 4 + i * 2 + c for y in range(groups // 8) for i in range(2)] for z in range(2) for c in range(2)]
    near = lax.all_to_all(own_valid, "ex", 0, 0, tiled=True, axis_index_groups=members)
    near = near.reshape(valid_count // 2, owned * proj // 2)
    far = lax.ppermute(near, "ex", [(i, i ^ 4) for i in range(groups)])
    half = call(
        join_kernel,
        jax.ShapeDtypeStruct((valid_count, owned * proj // 2), BF16),
        0,
        2 * valid_count * owned * proj,
        args=(on_chip(near), on_chip(far)),
    )
    other = lax.ppermute(half, "ex", [(i, i ^ 1) for i in range(groups)])
    own_group = jnp.full((1,), lax.axis_index("ex"), jnp.int32)
    valid, valid_squares = call(
        valid_kernel,
        (
            pltpu.VMEM((valid_count, owned * proj), BF16),
            pltpu.VMEM((1, valid_count), F32),
        ),
        2 * valid_count * valid_count * owned * proj,
        2 * valid_count * owned * proj * 2,
        smem=1,
        args=(own_group, on_chip(half), on_chip(other)),
    )

    right_in = (proj_inputs.reshape(layers, tokens, inputs), frozen_adapter, right_factor.swapaxes(1, 2))
    right_parts = call(
        right_kernel,
        jax.ShapeDtypeStruct((layers * proj, tokens), F32),
        2 * layers * tokens * inputs * 256,
        proj_inputs.size * 2,
        scratch=(*staged(right_in), pltpu.SemaphoreType.DMA((2 + layers,))),
        args=tuple(off_chip(x) for x in right_in),
        hbm=(0, 1, 2),
    )
    right_other = lax.ppermute(right_parts, "feat", [(i, i ^ 1) for i in range(peers)])
    right_parts = call(
        pair_kernel,
        jax.ShapeDtypeStruct((peers // 2, layers * proj, tokens), F32),
        layers * proj * tokens,
        4 * peers * layers * proj * tokens,
        args=(right_parts, right_other),
    )
    along_x = [[i * 2 + z for i in range(peers // 2)] for z in range(2)]
    right_parts = lax.all_to_all(right_parts, "feat", 0, 0, tiled=True, axis_index_groups=along_x)
    left_shape = (layers, tokens, kl)
    left_copies = layers * tokens // LEFT_STEP
    left_in = (out_cotangent.reshape(layers, tokens, width), left_factor)
    left_rows = call(
        left_kernel,
        pltpu.VMEM(left_shape, BF16),
        2 * layers * tokens * width * kl,
        (out_cotangent.size + left_factor.size) * 2 + layers * tokens * kl * 2,
        scratch=(*staged(left_in), pltpu.SemaphoreType.DMA((layers + left_copies,))),
        args=tuple(off_chip(x) for x in left_in),
        hbm=(0, 1),
    )
    parts_shape = (peers, examples * 8, 128)
    (parts,) = call(
        project_kernel,
        (pltpu.HBM(parts_shape, BF16),),
        2 * layers * tokens * kl * 256,
        layers * tokens * kl * 4,
        scratch=(pltpu.VMEM(parts_shape, BF16), pltpu.SemaphoreType.DMA((examples // GROUP,))),
        hbm_out=(0,),
        smem=1,
        args=(seq_lengths, on_chip(right_parts), on_chip(left_rows)),
    )
    parts = lax.all_to_all(parts, "feat", 0, 0, tiled=True)
    products = call(
        product_kernel,
        pltpu.VMEM((peers, examples + 8, valid_count), F32),
        4 * examples * valid_count * owned * proj,
        parts.size * 2 + valid.size * 2,
        scratch=(pltpu.VMEM((examples * 8, 128), F32),),
        args=(on_chip(parts), on_chip(valid), on_chip(valid_squares)),
    )
    products = lax.all_to_all(products, "feat", 0, 0, tiled=True)

    def score(part_ref, out_ref):
        score_kernel(scaling, part_ref, out_ref)

    return call(
        score,
        jax.ShapeDtypeStruct((examples, valid_count), F32),
        examples * valid_count * 16,
        products.size * 4,
        args=(on_chip(products),),
    )


def solution(mesh):
    return jax.shard_map(
        scores_of,
        mesh=mesh,
        in_specs=(
            P(None, "ex", None, "feat"),
            P(None, "ex", None, "feat"),
            P("ex"),
            P(None, None, "feat"),
            P(None, None, "feat"),
            P(),
            P("ex", "feat"),
        ),
        out_specs=P("ex", None),
        check_vma=False,
    )
```

```python
import math

import jax
import jax.numpy as jnp
from jax import lax
from jax.experimental import pallas as pl
from jax.experimental.pallas import tpu as pltpu
from jax.sharding import PartitionSpec as P


F32 = jnp.float32
BF16 = jnp.bfloat16
VMEM_LIMIT = 24 << 20
LEFT_STEP = 256
GROUP = 4
NT = (((1,), (1,)), ((), ()))
NN = (((1,), (0,)), ((), ()))


def dot(a, b, dims):
    return lax.dot_general(a, b, dims, preferred_element_type=F32)


def split(x):
    high = x.astype(BF16)
    return high, (x - high.astype(F32)).astype(BF16)


def on_chip(x):
    return pltpu.with_memory_space_constraint(x, pltpu.VMEM)


def off_chip(x):
    return pltpu.with_memory_space_constraint(x, pltpu.HBM)


def staged(arrays):
    return tuple(pltpu.VMEM(x.shape, x.dtype) for x in arrays)


def call(kernel, out_shape, flops, bytes_accessed, scratch=(), smem=0, args=(), hbm=(), hbm_out=()):
    specs = [pl.BlockSpec(memory_space=pltpu.SMEM)] * smem
    specs += [pl.BlockSpec(memory_space=pltpu.HBM if n in hbm else pltpu.VMEM) for n in range(smem, len(args))]
    if isinstance(out_shape, tuple):
        out_specs = tuple(
            pl.BlockSpec(memory_space=pltpu.HBM if n in hbm_out else pltpu.VMEM) for n in range(len(out_shape))
        )
    else:
        out_specs = pl.BlockSpec(memory_space=pltpu.VMEM)
    return pl.pallas_call(
        kernel,
        out_shape=out_shape,
        in_specs=specs,
        out_specs=out_specs,
        scratch_shapes=list(scratch),
        cost_estimate=pl.CostEstimate(flops=flops, bytes_accessed=bytes_accessed, transcendentals=0),
        compiler_params=pltpu.CompilerParams(vmem_limit_bytes=VMEM_LIMIT),
    )(*args)


def right_kernel(x_hbm, a_hbm, r_hbm, out_ref, x_ref, a_ref, r_ref, sems):
    layers = x_ref.shape[0]
    proj = r_ref.shape[1]
    small = [
        pltpu.make_async_copy(r_hbm, r_ref, sems.at[0]),
        pltpu.make_async_copy(a_hbm, a_ref, sems.at[1]),
    ]
    inputs = [pltpu.make_async_copy(x_hbm.at[l], x_ref.at[l], sems.at[2 + l]) for l in range(layers)]
    for copy in small + inputs:
        copy.start()
    for copy in small:
        copy.wait()
    mixes = []
    for l in range(layers):
        high, low = split(dot(r_ref[l], a_ref[l], NN))
        mixes.append(jnp.concatenate([high, low], axis=0))
    for l in range(layers):
        inputs[l].wait()
        rows = dot(mixes[l], x_ref[l], NT)
        out_ref[l * proj:(l + 1) * proj, :] = rows[:proj] + rows[proj:]


def pair_kernel(own_ref, other_ref, out_ref):
    total = own_ref[...] + other_ref[...]
    for p in range(out_ref.shape[0]):
        out_ref[p] = total


def left_kernel(c_hbm, l_hbm, out_ref, c_ref, l_ref, sems):
    layers, tokens, _ = c_ref.shape
    step = LEFT_STEP
    factors, pieces = [], []
    for l in range(layers):
        factors.append(pltpu.make_async_copy(l_hbm.at[l], l_ref.at[l], sems.at[l]))
        factors[-1].start()
        for t in range(0, tokens, step):
            rows = pl.ds(t, step)
            copy = pltpu.make_async_copy(c_hbm.at[l, rows], c_ref.at[l, rows], sems.at[layers + len(pieces)])
            copy.start()
            pieces.append((l, t, copy))
    for l, t, copy in pieces:
        if t == 0:
            factors[l].wait()
        copy.wait()
        out_ref[l, t:t + step, :] = dot(c_ref[l, t:t + step, :], l_ref[l], NT).astype(BF16)


def project_kernel(seq_ref, rr_ref, left_ref, out_hbm, out_ref, out_sems):
    parts, two_proj, tokens = rr_ref.shape
    layers, _, kl = left_ref.shape
    peers = out_ref.shape[0]
    proj = two_proj // layers
    half = proj // 2
    owned = kl // peers
    examples = seq_ref.shape[0]
    seq = tokens // examples
    span = GROUP * seq
    width = 2 * 128
    total = rr_ref[0]
    for p in range(1, parts):
        total = total + rr_ref[p]
    first = total[:proj]
    second = total[proj:]
    lane = lax.broadcasted_iota(jnp.int32, (proj, width), 1)
    out_lane = lax.broadcasted_iota(jnp.int32, (GROUP * half, 128), 1)
    stores = []
    for g in range(examples // GROUP):
        base = min(g * span // 128 * 128, tokens - width)
        offset = g * span - base
        x0 = first[:, base:base + width]
        x1 = second[:, base:base + width]
        if offset:
            x0 = pltpu.roll(x0, width - offset, 1)
        if offset != span:
            x1 = pltpu.roll(x1, (width + span - offset) % width, 1)
        blocks = []
        for i in range(GROUP):
            start = i * seq
            stop = start + seq_ref[g * GROUP + i]
            mask0 = (lane >= start) & (lane < stop)
            mask1 = (lane >= start + span) & (lane < stop + span)
            blocks.append(jnp.where(mask0, x0, jnp.where(mask1, x1, 0.0)))
        spread = jnp.concatenate(blocks, axis=0).astype(BF16)[:, :layers * span]
        t = g * span
        left = jnp.concatenate([left_ref[l, t:t + span, :] for l in range(layers)], axis=0)
        part = dot(spread, left, NN)
        part = part.reshape(GROUP, 2, half, kl)
        even = part[:, 0].reshape(GROUP * half, kl)
        odd = part[:, 1].reshape(GROUP * half, kl)
        r = g * GROUP * half
        for tile in range(kl // 128):
            e = even[:, tile * 128:(tile + 1) * 128]
            o = odd[:, tile * 128:(tile + 1) * 128]
            kept = jnp.where(out_lane < owned, e, o)
            moved = pltpu.roll(jnp.where(out_lane < owned, o, e), owned, 1)
            out_ref[2 * tile, r:r + GROUP * half, :] = jnp.where(out_lane < owned, kept, moved).astype(BF16)
            out_ref[2 * tile + 1, r:r + GROUP * half, :] = jnp.where(out_lane < owned, moved, kept).astype(BF16)
        rows = pl.ds(g * GROUP * half, GROUP * half)
        stores.append(pltpu.make_async_copy(out_ref.at[:, rows], out_hbm.at[:, rows], out_sems.at[g]))
        stores[-1].start()
    for store in stores:
        store.wait()


def join_kernel(near_ref, far_ref, out_ref):
    rows = near_ref.shape[0]
    out_ref[:rows] = near_ref[...]
    out_ref[rows:] = far_ref[...]


def valid_kernel(own_ref, half_ref, other_ref, out_ref, squares_ref):
    count = half_ref.shape[0]
    place = lax.broadcasted_iota(jnp.int32, (8, 2 * count), 1)
    core = ((place >> 8) ^ own_ref[0]) & 1
    far = ((place >> 7) ^ (own_ref[0] >> 2)) & 1
    index = (((place >> 4) & 7) << 5) | (far << 4) | (((place >> 3) & 1) << 3) | (core << 2) | ((place >> 1) & 3)
    row = lax.broadcasted_iota(jnp.int32, (count, 2 * count), 0)
    squares = jnp.zeros((count, 128), F32)
    for h in range(2):
        source = jnp.where((place & 1) == h, index, -1)
        order = (row == jnp.broadcast_to(source[:1], row.shape)).astype(F32).astype(BF16)
        for q in range(4):
            lanes = slice(q * 128, (q + 1) * 128)
            rows = dot(order[:, :count], half_ref[:, lanes], NN) + dot(order[:, count:], other_ref[:, lanes], NN)
            squares = squares + rows * rows
            b = h * 4 + q
            out_ref[:, b * 128:(b + 1) * 128] = rows.astype(BF16)
    squares_ref[...] = jnp.sum(squares.T, axis=0, keepdims=True)


def product_kernel(part_ref, valid_ref, squares_ref, out_ref, sum_ref):
    peers, rows, _ = part_ref.shape
    valid_count = valid_ref.shape[0]
    examples = rows // 8
    total = part_ref[0].astype(F32)
    for p in range(1, peers):
        total = total + part_ref[p].astype(F32)
    sum_ref[...] = total
    squares = jnp.sum((total * total).reshape(examples, 8, 128), axis=1)
    squares = jnp.sum(squares, axis=1, keepdims=True)
    row = lax.broadcasted_iota(jnp.int32, (examples, valid_count), 0)
    column = lax.broadcasted_iota(jnp.int32, (examples, valid_count), 1)
    train = jnp.sum(jnp.where(row == column, squares, 0.0), axis=0, keepdims=True)
    acc = jnp.zeros((2 * examples, valid_count), F32)
    for b in range(8):
        block = sum_ref[pl.ds(b, examples, stride=8), :]
        high, low = split(block)
        both = jnp.concatenate([high, low], axis=0)
        acc = acc + dot(both, valid_ref[:, b * 128:(b + 1) * 128], NT)
    products = acc[:examples] + acc[examples:]
    tail_row = lax.broadcasted_iota(jnp.int32, (8, valid_count), 0)
    tail = jnp.where(tail_row == 0, squares_ref[...], jnp.where(tail_row == 1, train, 0.0))
    for p in range(peers):
        out_ref[p, :examples, :] = products
        out_ref[p, examples:, :] = tail


def score_kernel(scaling, part_ref, out_ref):
    peers = part_ref.shape[0]
    examples, valid_count = out_ref.shape
    total = part_ref[0]
    for p in range(1, peers):
        total = total + part_ref[p]
    products = total[:examples]
    valid = jnp.sqrt(total[examples:examples + 1] + 1e-06)
    row = lax.broadcasted_iota(jnp.int32, (examples, valid_count), 0)
    column = lax.broadcasted_iota(jnp.int32, (examples, valid_count), 1)
    train = jnp.where(row == column, total[examples + 1:examples + 2], 0.0)
    train = jnp.sqrt(jnp.sum(train, axis=1, keepdims=True) + 1e-06)
    out_ref[...] = scaling * products / (train * valid)


def scores_of(proj_inputs, out_cotangent, seq_lengths, frozen_adapter, left_factor, right_factor, valid_grads):
    layers, examples, seq, inputs = proj_inputs.shape
    width = out_cotangent.shape[3]
    peers = lax.axis_size("feat")
    groups = lax.axis_size("ex")
    proj = right_factor.shape[2]
    kl = left_factor.shape[1]
    tokens = examples * seq
    owned = kl // peers
    valid_count = valid_grads.shape[0] * groups
    scaling = math.sqrt(kl * proj)

    own_valid = valid_grads.reshape(-1, owned, 2, 8).transpose(0, 3, 2, 1).reshape(1, -1, owned * proj // 2)
    own_valid = jnp.broadcast_to(own_valid, (groups // 4,) + own_valid.shape[1:])
    members = [[y * 8 + z * 4 + i * 2 + c for y in range(groups // 8) for i in range(2)] for z in range(2) for c in range(2)]
    near = lax.all_to_all(own_valid, "ex", 0, 0, tiled=True, axis_index_groups=members)
    near = near.reshape(valid_count // 2, owned * proj // 2)
    far = lax.ppermute(near, "ex", [(i, i ^ 4) for i in range(groups)])
    half = call(
        join_kernel,
        jax.ShapeDtypeStruct((valid_count, owned * proj // 2), BF16),
        0,
        2 * valid_count * owned * proj,
        args=(on_chip(near), on_chip(far)),
    )
    other = lax.ppermute(half, "ex", [(i, i ^ 1) for i in range(groups)])
    own_group = jnp.full((1,), lax.axis_index("ex"), jnp.int32)
    valid, valid_squares = call(
        valid_kernel,
        (
            pltpu.VMEM((valid_count, owned * proj), BF16),
            pltpu.VMEM((1, valid_count), F32),
        ),
        2 * valid_count * valid_count * owned * proj,
        2 * valid_count * owned * proj * 2,
        smem=1,
        args=(own_group, on_chip(half), on_chip(other)),
    )

    right_in = (proj_inputs.reshape(layers, tokens, inputs), frozen_adapter, right_factor.swapaxes(1, 2))
    right_parts = call(
        right_kernel,
        jax.ShapeDtypeStruct((layers * proj, tokens), F32),
        2 * layers * tokens * inputs * 256,
        proj_inputs.size * 2,
        scratch=(*staged(right_in), pltpu.SemaphoreType.DMA((2 + layers,))),
        args=tuple(off_chip(x) for x in right_in),
        hbm=(0, 1, 2),
    )
    right_other = lax.ppermute(right_parts, "feat", [(i, i ^ 1) for i in range(peers)])
    right_parts = call(
        pair_kernel,
        jax.ShapeDtypeStruct((peers // 2, layers * proj, tokens), F32),
        layers * proj * tokens,
        4 * peers * layers * proj * tokens,
        args=(right_parts, right_other),
    )
    along_x = [[i * 2 + z for i in range(peers // 2)] for z in range(2)]
    right_parts = lax.all_to_all(right_parts, "feat", 0, 0, tiled=True, axis_index_groups=along_x)
    left_shape = (layers, tokens, kl)
    left_copies = layers * tokens // LEFT_STEP
    left_in = (out_cotangent.reshape(layers, tokens, width), left_factor)
    left_rows = call(
        left_kernel,
        pltpu.VMEM(left_shape, BF16),
        2 * layers * tokens * width * kl,
        (out_cotangent.size + left_factor.size) * 2 + layers * tokens * kl * 2,
        scratch=(*staged(left_in), pltpu.SemaphoreType.DMA((layers + left_copies,))),
        args=tuple(off_chip(x) for x in left_in),
        hbm=(0, 1),
    )
    parts_shape = (peers, examples * 8, 128)
    (parts,) = call(
        project_kernel,
        (pltpu.HBM(parts_shape, BF16),),
        2 * layers * tokens * kl * 256,
        layers * tokens * kl * 4,
        scratch=(pltpu.VMEM(parts_shape, BF16), pltpu.SemaphoreType.DMA((examples // GROUP,))),
        hbm_out=(0,),
        smem=1,
        args=(seq_lengths, on_chip(right_parts), on_chip(left_rows)),
    )
    parts = lax.all_to_all(parts, "feat", 0, 0, tiled=True)
    products = call(
        product_kernel,
        pltpu.VMEM((peers, examples + 8, valid_count), F32),
        4 * examples * valid_count * owned * proj,
        parts.size * 2 + valid.size * 2,
        scratch=(pltpu.VMEM((examples * 8, 128), F32),),
        args=(on_chip(parts), on_chip(valid), on_chip(valid_squares)),
    )
    products = lax.all_to_all(products, "feat", 0, 0, tiled=True)

    def score(part_ref, out_ref):
        score_kernel(scaling, part_ref, out_ref)

    return call(
        score,
        jax.ShapeDtypeStruct((examples, valid_count), F32),
        examples * valid_count * 16,
        products.size * 4,
        args=(on_chip(products),),
    )


def solution(mesh):
    return jax.shard_map(
        scores_of,
        mesh=mesh,
        in_specs=(
            P(None, "ex", None, "feat"),
            P(None, "ex", None, "feat"),
            P("ex"),
            P(None, None, "feat"),
            P(None, None, "feat"),
            P(),
            P("ex", "feat"),
        ),
        out_specs=P("ex", None),
        check_vma=False,
    )
```

```python
import math

import jax
import jax.numpy as jnp
from jax import lax
from jax.experimental import pallas as pl
from jax.experimental.pallas import tpu as pltpu
from jax.sharding import PartitionSpec as P


F32 = jnp.float32
BF16 = jnp.bfloat16
VMEM_LIMIT = 24 << 20
LEFT_STEP = 256
GROUP = 4
NT = (((1,), (1,)), ((), ()))
NN = (((1,), (0,)), ((), ()))


def dot(a, b, dims):
    return lax.dot_general(a, b, dims, preferred_element_type=F32)


def split(x):
    high = x.astype(BF16)
    return high, (x - high.astype(F32)).astype(BF16)


def on_chip(x):
    return pltpu.with_memory_space_constraint(x, pltpu.VMEM)


def off_chip(x):
    return pltpu.with_memory_space_constraint(x, pltpu.HBM)


def staged(arrays):
    return tuple(pltpu.VMEM(x.shape, x.dtype) for x in arrays)


def call(kernel, out_shape, flops, bytes_accessed, scratch=(), smem=0, args=(), hbm=(), hbm_out=()):
    specs = [pl.BlockSpec(memory_space=pltpu.SMEM)] * smem
    specs += [pl.BlockSpec(memory_space=pltpu.HBM if n in hbm else pltpu.VMEM) for n in range(smem, len(args))]
    if isinstance(out_shape, tuple):
        out_specs = tuple(
            pl.BlockSpec(memory_space=pltpu.HBM if n in hbm_out else pltpu.VMEM) for n in range(len(out_shape))
        )
    else:
        out_specs = pl.BlockSpec(memory_space=pltpu.VMEM)
    return pl.pallas_call(
        kernel,
        out_shape=out_shape,
        in_specs=specs,
        out_specs=out_specs,
        scratch_shapes=list(scratch),
        cost_estimate=pl.CostEstimate(flops=flops, bytes_accessed=bytes_accessed, transcendentals=0),
        compiler_params=pltpu.CompilerParams(vmem_limit_bytes=VMEM_LIMIT),
    )(*args)


def right_kernel(x_hbm, a_hbm, r_hbm, out_ref, x_ref, a_ref, r_ref, sems):
    layers = x_ref.shape[0]
    proj = r_ref.shape[1]
    small = [
        pltpu.make_async_copy(r_hbm, r_ref, sems.at[0]),
        pltpu.make_async_copy(a_hbm, a_ref, sems.at[1]),
    ]
    inputs = [pltpu.make_async_copy(x_hbm.at[l], x_ref.at[l], sems.at[2 + l]) for l in range(layers)]
    for copy in small + inputs:
        copy.start()
    for copy in small:
        copy.wait()
    mixes = []
    for l in range(layers):
        high, low = split(dot(r_ref[l], a_ref[l], NN))
        mixes.append(jnp.concatenate([high, low], axis=0))
    for l in range(layers):
        inputs[l].wait()
        rows = dot(mixes[l], x_ref[l], NT)
        out_ref[l * proj:(l + 1) * proj, :] = rows[:proj] + rows[proj:]


def pair_kernel(own_ref, other_ref, out_ref):
    total = own_ref[...] + other_ref[...]
    for p in range(out_ref.shape[0]):
        out_ref[p] = total


def left_kernel(c_hbm, l_hbm, out_ref, c_ref, l_ref, sems):
    layers, tokens, _ = c_ref.shape
    step = LEFT_STEP
    factors, pieces = [], []
    for l in range(layers):
        factors.append(pltpu.make_async_copy(l_hbm.at[l], l_ref.at[l], sems.at[l]))
        factors[-1].start()
        for t in range(0, tokens, step):
            rows = pl.ds(t, step)
            copy = pltpu.make_async_copy(c_hbm.at[l, rows], c_ref.at[l, rows], sems.at[layers + len(pieces)])
            copy.start()
            pieces.append((l, t, copy))
    for l, t, copy in pieces:
        if t == 0:
            factors[l].wait()
        copy.wait()
        out_ref[l, t:t + step, :] = dot(c_ref[l, t:t + step, :], l_ref[l], NT).astype(BF16)


def project_kernel(seq_ref, rr_ref, left_ref, out_hbm, out_ref, out_sems):
    parts, two_proj, tokens = rr_ref.shape
    layers, _, kl = left_ref.shape
    peers = out_ref.shape[0]
    proj = two_proj // layers
    half = proj // 2
    owned = kl // peers
    examples = seq_ref.shape[0]
    seq = tokens // examples
    span = GROUP * seq
    width = 2 * 128
    total = rr_ref[0]
    for p in range(1, parts):
        total = total + rr_ref[p]
    first = total[:proj]
    second = total[proj:]
    lane = lax.broadcasted_iota(jnp.int32, (proj, width), 1)
    out_lane = lax.broadcasted_iota(jnp.int32, (GROUP * half, 128), 1)
    stores = []
    for g in range(examples // GROUP):
        base = min(g * span // 128 * 128, tokens - width)
        offset = g * span - base
        x0 = first[:, base:base + width]
        x1 = second[:, base:base + width]
        if offset:
            x0 = pltpu.roll(x0, width - offset, 1)
        if offset != span:
            x1 = pltpu.roll(x1, (width + span - offset) % width, 1)
        blocks = []
        for i in range(GROUP):
            start = i * seq
            stop = start + seq_ref[g * GROUP + i]
            mask0 = (lane >= start) & (lane < stop)
            mask1 = (lane >= start + span) & (lane < stop + span)
            blocks.append(jnp.where(mask0, x0, jnp.where(mask1, x1, 0.0)))
        spread = jnp.concatenate(blocks, axis=0).astype(BF16)[:, :layers * span]
        t = g * span
        left = jnp.concatenate([left_ref[l, t:t + span, :] for l in range(layers)], axis=0)
        part = dot(spread, left, NN)
        part = part.reshape(GROUP, 2, half, kl)
        even = part[:, 0].reshape(GROUP * half, kl)
        odd = part[:, 1].reshape(GROUP * half, kl)
        r = g * GROUP * half
        for tile in range(kl // 128):
            e = even[:, tile * 128:(tile + 1) * 128]
            o = odd[:, tile * 128:(tile + 1) * 128]
            kept = jnp.where(out_lane < owned, e, o)
            moved = pltpu.roll(jnp.where(out_lane < owned, o, e), owned, 1)
            out_ref[2 * tile, r:r + GROUP * half, :] = jnp.where(out_lane < owned, kept, moved).astype(BF16)
            out_ref[2 * tile + 1, r:r + GROUP * half, :] = jnp.where(out_lane < owned, moved, kept).astype(BF16)
        rows = pl.ds(g * GROUP * half, GROUP * half)
        stores.append(pltpu.make_async_copy(out_ref.at[:, rows], out_hbm.at[:, rows], out_sems.at[g]))
        stores[-1].start()
    for store in stores:
        store.wait()


def join_kernel(near_ref, far_ref, out_ref):
    rows = near_ref.shape[0]
    out_ref[:rows] = near_ref[...]
    out_ref[rows:] = far_ref[...]


def valid_kernel(own_ref, half_ref, other_ref, out_ref, squares_ref):
    count = half_ref.shape[0]
    place = lax.broadcasted_iota(jnp.int32, (8, 2 * count), 1)
    core = ((place >> 8) ^ own_ref[0]) & 1
    far = ((place >> 7) ^ (own_ref[0] >> 5)) & 1
    index = (far << 7) | (((place >> 3) & 15) << 3) | (core << 2) | ((place >> 1) & 3)
    row = lax.broadcasted_iota(jnp.int32, (count, 2 * count), 0)
    squares = jnp.zeros((count, 128), F32)
    for h in range(2):
        source = jnp.where((place & 1) == h, index, -1)
        order = (row == jnp.broadcast_to(source[:1], row.shape)).astype(F32).astype(BF16)
        for q in range(4):
            lanes = slice(q * 128, (q + 1) * 128)
            rows = dot(order[:, :count], half_ref[:, lanes], NN) + dot(order[:, count:], other_ref[:, lanes], NN)
            squares = squares + rows * rows
            b = h * 4 + q
            out_ref[:, b * 128:(b + 1) * 128] = rows.astype(BF16)
    squares_ref[...] = jnp.sum(squares.T, axis=0, keepdims=True)


def product_kernel(part_ref, valid_ref, squares_ref, out_ref, sum_ref):
    peers, rows, _ = part_ref.shape
    valid_count = valid_ref.shape[0]
    examples = rows // 8
    total = part_ref[0].astype(F32)
    for p in range(1, peers):
        total = total + part_ref[p].astype(F32)
    sum_ref[...] = total
    squares = jnp.sum((total * total).reshape(examples, 8, 128), axis=1)
    squares = jnp.sum(squares, axis=1, keepdims=True)
    row = lax.broadcasted_iota(jnp.int32, (examples, valid_count), 0)
    column = lax.broadcasted_iota(jnp.int32, (examples, valid_count), 1)
    train = jnp.sum(jnp.where(row == column, squares, 0.0), axis=0, keepdims=True)
    acc = jnp.zeros((2 * examples, valid_count), F32)
    for b in range(8):
        block = sum_ref[pl.ds(b, examples, stride=8), :]
        high, low = split(block)
        both = jnp.concatenate([high, low], axis=0)
        acc = acc + dot(both, valid_ref[:, b * 128:(b + 1) * 128], NT)
    products = acc[:examples] + acc[examples:]
    tail_row = lax.broadcasted_iota(jnp.int32, (8, valid_count), 0)
    tail = jnp.where(tail_row == 0, squares_ref[...], jnp.where(tail_row == 1, train, 0.0))
    for p in range(peers):
        out_ref[p, :examples, :] = products
        out_ref[p, examples:, :] = tail


def score_kernel(scaling, part_ref, out_ref):
    peers = part_ref.shape[0]
    examples, valid_count = out_ref.shape
    total = part_ref[0]
    for p in range(1, peers):
        total = total + part_ref[p]
    products = total[:examples]
    valid = jnp.sqrt(total[examples:examples + 1] + 1e-06)
    row = lax.broadcasted_iota(jnp.int32, (examples, valid_count), 0)
    column = lax.broadcasted_iota(jnp.int32, (examples, valid_count), 1)
    train = jnp.where(row == column, total[examples + 1:examples + 2], 0.0)
    train = jnp.sqrt(jnp.sum(train, axis=1, keepdims=True) + 1e-06)
    out_ref[...] = scaling * products / (train * valid)


def scores_of(proj_inputs, out_cotangent, seq_lengths, frozen_adapter, left_factor, right_factor, valid_grads):
    layers, examples, seq, inputs = proj_inputs.shape
    width = out_cotangent.shape[3]
    peers = lax.axis_size("feat")
    groups = lax.axis_size("ex")
    proj = right_factor.shape[2]
    kl = left_factor.shape[1]
    tokens = examples * seq
    owned = kl // peers
    valid_count = valid_grads.shape[0] * groups
    scaling = math.sqrt(kl * proj)

    own_valid = valid_grads.reshape(-1, owned, 2, 8).transpose(0, 3, 2, 1).reshape(1, -1, owned * proj // 2)
    own_valid = jnp.broadcast_to(own_valid, (groups // 4,) + own_valid.shape[1:])
    far_bit = groups // 2
    members = [[y * far_bit + i * 2 + c for i in range(far_bit // 2)] for y in range(2) for c in range(2)]
    near = lax.all_to_all(own_valid, "ex", 0, 0, tiled=True, axis_index_groups=members)
    near = near.reshape(valid_count // 2, owned * proj // 2)
    far = lax.ppermute(near, "ex", [(i, i ^ far_bit) for i in range(groups)])
    half = call(
        join_kernel,
        jax.ShapeDtypeStruct((valid_count, owned * proj // 2), BF16),
        0,
        2 * valid_count * owned * proj,
        args=(on_chip(near), on_chip(far)),
    )
    other = lax.ppermute(half, "ex", [(i, i ^ 1) for i in range(groups)])
    own_group = jnp.full((1,), lax.axis_index("ex"), jnp.int32)
    valid, valid_squares = call(
        valid_kernel,
        (
            pltpu.VMEM((valid_count, owned * proj), BF16),
            pltpu.VMEM((1, valid_count), F32),
        ),
        2 * valid_count * valid_count * owned * proj,
        2 * valid_count * owned * proj * 2,
        smem=1,
        args=(own_group, on_chip(half), on_chip(other)),
    )

    right_in = (proj_inputs.reshape(layers, tokens, inputs), frozen_adapter, right_factor.swapaxes(1, 2))
    right_parts = call(
        right_kernel,
        jax.ShapeDtypeStruct((layers * proj, tokens), F32),
        2 * layers * tokens * inputs * 256,
        proj_inputs.size * 2,
        scratch=(*staged(right_in), pltpu.SemaphoreType.DMA((2 + layers,))),
        args=tuple(off_chip(x) for x in right_in),
        hbm=(0, 1, 2),
    )
    right_other = lax.ppermute(right_parts, "feat", [(i, i ^ 1) for i in range(peers)])
    right_parts = call(
        pair_kernel,
        jax.ShapeDtypeStruct((peers // 2, layers * proj, tokens), F32),
        layers * proj * tokens,
        4 * peers * layers * proj * tokens,
        args=(right_parts, right_other),
    )
    along_x = [[i * 2 + z for i in range(peers // 2)] for z in range(2)]
    right_parts = lax.all_to_all(right_parts, "feat", 0, 0, tiled=True, axis_index_groups=along_x)
    left_shape = (layers, tokens, kl)
    left_copies = layers * tokens // LEFT_STEP
    left_in = (out_cotangent.reshape(layers, tokens, width), left_factor)
    left_rows = call(
        left_kernel,
        pltpu.VMEM(left_shape, BF16),
        2 * layers * tokens * width * kl,
        (out_cotangent.size + left_factor.size) * 2 + layers * tokens * kl * 2,
        scratch=(*staged(left_in), pltpu.SemaphoreType.DMA((layers + left_copies,))),
        args=tuple(off_chip(x) for x in left_in),
        hbm=(0, 1),
    )
    parts_shape = (peers, examples * 8, 128)
    (parts,) = call(
        project_kernel,
        (pltpu.HBM(parts_shape, BF16),),
        2 * layers * tokens * kl * 256,
        layers * tokens * kl * 4,
        scratch=(pltpu.VMEM(parts_shape, BF16), pltpu.SemaphoreType.DMA((examples // GROUP,))),
        hbm_out=(0,),
        smem=1,
        args=(seq_lengths, on_chip(right_parts), on_chip(left_rows)),
    )
    parts = lax.all_to_all(parts, "feat", 0, 0, tiled=True)
    products = call(
        product_kernel,
        pltpu.VMEM((peers, examples + 8, valid_count), F32),
        4 * examples * valid_count * owned * proj,
        parts.size * 2 + valid.size * 2,
        scratch=(pltpu.VMEM((examples * 8, 128), F32),),
        args=(on_chip(parts), on_chip(valid), on_chip(valid_squares)),
    )
    products = lax.all_to_all(products, "feat", 0, 0, tiled=True)

    def score(part_ref, out_ref):
        score_kernel(scaling, part_ref, out_ref)

    return call(
        score,
        jax.ShapeDtypeStruct((examples, valid_count), F32),
        examples * valid_count * 16,
        products.size * 4,
        args=(on_chip(products),),
    )


def solution(mesh):
    return jax.shard_map(
        scores_of,
        mesh=mesh,
        in_specs=(
            P(None, "ex", None, "feat"),
            P(None, "ex", None, "feat"),
            P("ex"),
            P(None, None, "feat"),
            P(None, None, "feat"),
            P(),
            P("ex", "feat"),
        ),
        out_specs=P("ex", None),
        check_vma=False,
    )
```

```python
import math

import jax
import jax.numpy as jnp
from jax import lax
from jax.experimental import pallas as pl
from jax.experimental.pallas import tpu as pltpu
from jax.sharding import PartitionSpec as P


F32 = jnp.float32
BF16 = jnp.bfloat16
VMEM_LIMIT = 24 << 20
LEFT_STEP = 256
GROUP = 4
NT = (((1,), (1,)), ((), ()))
NN = (((1,), (0,)), ((), ()))


def dot(a, b, dims):
    return lax.dot_general(a, b, dims, preferred_element_type=F32)


def split(x):
    high = x.astype(BF16)
    return high, (x - high.astype(F32)).astype(BF16)


def on_chip(x):
    return pltpu.with_memory_space_constraint(x, pltpu.VMEM)


def off_chip(x):
    return pltpu.with_memory_space_constraint(x, pltpu.HBM)


def staged(arrays):
    return tuple(pltpu.VMEM(x.shape, x.dtype) for x in arrays)


def call(kernel, out_shape, flops, bytes_accessed, scratch=(), smem=0, args=(), hbm=(), hbm_out=()):
    specs = [pl.BlockSpec(memory_space=pltpu.SMEM)] * smem
    specs += [pl.BlockSpec(memory_space=pltpu.HBM if n in hbm else pltpu.VMEM) for n in range(smem, len(args))]
    if isinstance(out_shape, tuple):
        out_specs = tuple(
            pl.BlockSpec(memory_space=pltpu.HBM if n in hbm_out else pltpu.VMEM) for n in range(len(out_shape))
        )
    else:
        out_specs = pl.BlockSpec(memory_space=pltpu.VMEM)
    return pl.pallas_call(
        kernel,
        out_shape=out_shape,
        in_specs=specs,
        out_specs=out_specs,
        scratch_shapes=list(scratch),
        cost_estimate=pl.CostEstimate(flops=flops, bytes_accessed=bytes_accessed, transcendentals=0),
        compiler_params=pltpu.CompilerParams(vmem_limit_bytes=VMEM_LIMIT),
    )(*args)


def right_kernel(x_hbm, a_hbm, r_hbm, out_ref, x_ref, a_ref, r_ref, sems):
    layers = x_ref.shape[0]
    proj = r_ref.shape[1]
    small = [
        pltpu.make_async_copy(r_hbm, r_ref, sems.at[0]),
        pltpu.make_async_copy(a_hbm, a_ref, sems.at[1]),
    ]
    inputs = [pltpu.make_async_copy(x_hbm.at[l], x_ref.at[l], sems.at[2 + l]) for l in range(layers)]
    for copy in small + inputs:
        copy.start()
    for copy in small:
        copy.wait()
    mixes = []
    for l in range(layers):
        high, low = split(dot(r_ref[l], a_ref[l], NN))
        mixes.append(jnp.concatenate([high, low], axis=0))
    for l in range(layers):
        inputs[l].wait()
        rows = dot(mixes[l], x_ref[l], NT)
        out_ref[l * proj:(l + 1) * proj, :] = rows[:proj] + rows[proj:]


def pair_kernel(own_ref, other_ref, out_ref):
    total = own_ref[...] + other_ref[...]
    for p in range(out_ref.shape[0]):
        out_ref[p] = total


def left_kernel(c_hbm, l_hbm, out_ref, c_ref, l_ref, sems):
    layers, tokens, _ = c_ref.shape
    step = LEFT_STEP
    factors, pieces = [], []
    for l in range(layers):
        factors.append(pltpu.make_async_copy(l_hbm.at[l], l_ref.at[l], sems.at[l]))
        factors[-1].start()
        for t in range(0, tokens, step):
            rows = pl.ds(t, step)
            copy = pltpu.make_async_copy(c_hbm.at[l, rows], c_ref.at[l, rows], sems.at[layers + len(pieces)])
            copy.start()
            pieces.append((l, t, copy))
    for l, t, copy in pieces:
        if t == 0:
            factors[l].wait()
        copy.wait()
        out_ref[l, t:t + step, :] = dot(c_ref[l, t:t + step, :], l_ref[l], NT).astype(BF16)


def project_kernel(seq_ref, rr_ref, left_ref, out_hbm, out_ref, out_sems):
    parts, two_proj, tokens = rr_ref.shape
    layers, _, kl = left_ref.shape
    peers = out_ref.shape[0]
    proj = two_proj // layers
    half = proj // 2
    owned = kl // peers
    examples = seq_ref.shape[0]
    seq = tokens // examples
    span = GROUP * seq
    width = 2 * 128
    total = rr_ref[0]
    for p in range(1, parts):
        total = total + rr_ref[p]
    first = total[:proj]
    second = total[proj:]
    lane = lax.broadcasted_iota(jnp.int32, (proj, width), 1)
    out_lane = lax.broadcasted_iota(jnp.int32, (GROUP * half, 128), 1)
    stores = []
    for g in range(examples // GROUP):
        base = min(g * span // 128 * 128, tokens - width)
        offset = g * span - base
        x0 = first[:, base:base + width]
        x1 = second[:, base:base + width]
        if offset:
            x0 = pltpu.roll(x0, width - offset, 1)
        if offset != span:
            x1 = pltpu.roll(x1, (width + span - offset) % width, 1)
        blocks = []
        for i in range(GROUP):
            start = i * seq
            stop = start + seq_ref[g * GROUP + i]
            mask0 = (lane >= start) & (lane < stop)
            mask1 = (lane >= start + span) & (lane < stop + span)
            blocks.append(jnp.where(mask0, x0, jnp.where(mask1, x1, 0.0)))
        spread = jnp.concatenate(blocks, axis=0).astype(BF16)[:, :layers * span]
        t = g * span
        left = jnp.concatenate([left_ref[l, t:t + span, :] for l in range(layers)], axis=0)
        part = dot(spread, left, NN)
        part = part.reshape(GROUP, 2, half, kl)
        even = part[:, 0].reshape(GROUP * half, kl)
        odd = part[:, 1].reshape(GROUP * half, kl)
        r = g * GROUP * half
        for tile in range(kl // 128):
            e = even[:, tile * 128:(tile + 1) * 128]
            o = odd[:, tile * 128:(tile + 1) * 128]
            kept = jnp.where(out_lane < owned, e, o)
            moved = pltpu.roll(jnp.where(out_lane < owned, o, e), owned, 1)
            out_ref[2 * tile, r:r + GROUP * half, :] = jnp.where(out_lane < owned, kept, moved).astype(BF16)
            out_ref[2 * tile + 1, r:r + GROUP * half, :] = jnp.where(out_lane < owned, moved, kept).astype(BF16)
        rows = pl.ds(g * GROUP * half, GROUP * half)
        stores.append(pltpu.make_async_copy(out_ref.at[:, rows], out_hbm.at[:, rows], out_sems.at[g]))
        stores[-1].start()
    for store in stores:
        store.wait()


def valid_kernel(own_ref, half_ref, other_ref, out_ref, squares_ref):
    count = half_ref.shape[0]
    place = lax.broadcasted_iota(jnp.int32, (8, 2 * count), 1)
    far = ((place >> 8) ^ (own_ref[0] >> 5)) & 1
    index = (far << 7) | (((place >> 3) & 31) << 2) | ((place >> 1) & 3)
    row = lax.broadcasted_iota(jnp.int32, (count, 2 * count), 0)
    squares = jnp.zeros((count, 128), F32)
    for h in range(2):
        source = jnp.where((place & 1) == h, index, -1)
        order = (row == jnp.broadcast_to(source[:1], row.shape)).astype(F32).astype(BF16)
        for q in range(4):
            lanes = slice(q * 128, (q + 1) * 128)
            rows = dot(order[:, :count], half_ref[:, lanes], NN) + dot(order[:, count:], other_ref[:, lanes], NN)
            squares = squares + rows * rows
            b = h * 4 + q
            out_ref[:, b * 128:(b + 1) * 128] = rows.astype(BF16)
    squares_ref[...] = jnp.sum(squares.T, axis=0, keepdims=True)


def product_kernel(part_ref, valid_ref, squares_ref, out_ref, sum_ref):
    peers, rows, _ = part_ref.shape
    valid_count = valid_ref.shape[0]
    examples = rows // 8
    total = part_ref[0].astype(F32)
    for p in range(1, peers):
        total = total + part_ref[p].astype(F32)
    sum_ref[...] = total
    squares = jnp.sum((total * total).reshape(examples, 8, 128), axis=1)
    squares = jnp.sum(squares, axis=1, keepdims=True)
    row = lax.broadcasted_iota(jnp.int32, (examples, valid_count), 0)
    column = lax.broadcasted_iota(jnp.int32, (examples, valid_count), 1)
    train = jnp.sum(jnp.where(row == column, squares, 0.0), axis=0, keepdims=True)
    acc = jnp.zeros((2 * examples, valid_count), F32)
    for b in range(8):
        block = sum_ref[pl.ds(b, examples, stride=8), :]
        high, low = split(block)
        both = jnp.concatenate([high, low], axis=0)
        acc = acc + dot(both, valid_ref[:, b * 128:(b + 1) * 128], NT)
    products = acc[:examples] + acc[examples:]
    tail_row = lax.broadcasted_iota(jnp.int32, (8, valid_count), 0)
    tail = jnp.where(tail_row == 0, squares_ref[...], jnp.where(tail_row == 1, train, 0.0))
    for p in range(peers):
        out_ref[p, :examples, :] = products
        out_ref[p, examples:, :] = tail


def score_kernel(scaling, part_ref, out_ref):
    peers = part_ref.shape[0]
    examples, valid_count = out_ref.shape
    total = part_ref[0]
    for p in range(1, peers):
        total = total + part_ref[p]
    products = total[:examples]
    valid = jnp.sqrt(total[examples:examples + 1] + 1e-06)
    row = lax.broadcasted_iota(jnp.int32, (examples, valid_count), 0)
    column = lax.broadcasted_iota(jnp.int32, (examples, valid_count), 1)
    train = jnp.where(row == column, total[examples + 1:examples + 2], 0.0)
    train = jnp.sqrt(jnp.sum(train, axis=1, keepdims=True) + 1e-06)
    out_ref[...] = scaling * products / (train * valid)


def scores_of(proj_inputs, out_cotangent, seq_lengths, frozen_adapter, left_factor, right_factor, valid_grads):
    layers, examples, seq, inputs = proj_inputs.shape
    width = out_cotangent.shape[3]
    peers = lax.axis_size("feat")
    groups = lax.axis_size("ex")
    proj = right_factor.shape[2]
    kl = left_factor.shape[1]
    tokens = examples * seq
    owned = kl // peers
    valid_count = valid_grads.shape[0] * groups
    scaling = math.sqrt(kl * proj)

    far_bit = groups // 2
    own_valid = valid_grads.reshape(-1, owned, 2, 8).transpose(0, 3, 2, 1).reshape(1, -1, owned * proj // 2)
    own_valid = jnp.broadcast_to(own_valid, (far_bit,) + own_valid.shape[1:])
    members = [[y * far_bit + i for i in range(far_bit)] for y in range(2)]
    near = lax.all_to_all(own_valid, "ex", 0, 0, tiled=True, axis_index_groups=members)
    near = near.reshape(valid_count, owned * proj // 2)
    far = lax.ppermute(near, "ex", [(i, i ^ far_bit) for i in range(groups)])
    own_group = jnp.full((1,), lax.axis_index("ex"), jnp.int32)
    valid, valid_squares = call(
        valid_kernel,
        (
            pltpu.VMEM((valid_count, owned * proj), BF16),
            pltpu.VMEM((1, valid_count), F32),
        ),
        2 * valid_count * valid_count * owned * proj,
        2 * valid_count * owned * proj * 2,
        smem=1,
        args=(own_group, on_chip(near), on_chip(far)),
    )

    right_in = (proj_inputs.reshape(layers, tokens, inputs), frozen_adapter, right_factor.swapaxes(1, 2))
    right_parts = call(
        right_kernel,
        jax.ShapeDtypeStruct((layers * proj, tokens), F32),
        2 * layers * tokens * inputs * 256,
        proj_inputs.size * 2,
        scratch=(*staged(right_in), pltpu.SemaphoreType.DMA((2 + layers,))),
        args=tuple(off_chip(x) for x in right_in),
        hbm=(0, 1, 2),
    )
    right_other = lax.ppermute(right_parts, "feat", [(i, i ^ 1) for i in range(peers)])
    right_parts = call(
        pair_kernel,
        jax.ShapeDtypeStruct((peers // 2, layers * proj, tokens), F32),
        layers * proj * tokens,
        4 * peers * layers * proj * tokens,
        args=(right_parts, right_other),
    )
    along_x = [[i * 2 + z for i in range(peers // 2)] for z in range(2)]
    right_parts = lax.all_to_all(right_parts, "feat", 0, 0, tiled=True, axis_index_groups=along_x)
    left_shape = (layers, tokens, kl)
    left_copies = layers * tokens // LEFT_STEP
    left_in = (out_cotangent.reshape(layers, tokens, width), left_factor)
    left_rows = call(
        left_kernel,
        pltpu.VMEM(left_shape, BF16),
        2 * layers * tokens * width * kl,
        (out_cotangent.size + left_factor.size) * 2 + layers * tokens * kl * 2,
        scratch=(*staged(left_in), pltpu.SemaphoreType.DMA((layers + left_copies,))),
        args=tuple(off_chip(x) for x in left_in),
        hbm=(0, 1),
    )
    parts_shape = (peers, examples * 8, 128)
    (parts,) = call(
        project_kernel,
        (pltpu.HBM(parts_shape, BF16),),
        2 * layers * tokens * kl * 256,
        layers * tokens * kl * 4,
        scratch=(pltpu.VMEM(parts_shape, BF16), pltpu.SemaphoreType.DMA((examples // GROUP,))),
        hbm_out=(0,),
        smem=1,
        args=(seq_lengths, on_chip(right_parts), on_chip(left_rows)),
    )
    parts = lax.all_to_all(parts, "feat", 0, 0, tiled=True)
    products = call(
        product_kernel,
        pltpu.VMEM((peers, examples + 8, valid_count), F32),
        4 * examples * valid_count * owned * proj,
        parts.size * 2 + valid.size * 2,
        scratch=(pltpu.VMEM((examples * 8, 128), F32),),
        args=(on_chip(parts), on_chip(valid), on_chip(valid_squares)),
    )
    products = lax.all_to_all(products, "feat", 0, 0, tiled=True)

    def score(part_ref, out_ref):
        score_kernel(scaling, part_ref, out_ref)

    return call(
        score,
        jax.ShapeDtypeStruct((examples, valid_count), F32),
        examples * valid_count * 16,
        products.size * 4,
        args=(on_chip(products),),
    )


def solution(mesh):
    return jax.shard_map(
        scores_of,
        mesh=mesh,
        in_specs=(
            P(None, "ex", None, "feat"),
            P(None, "ex", None, "feat"),
            P("ex"),
            P(None, None, "feat"),
            P(None, None, "feat"),
            P(),
            P("ex", "feat"),
        ),
        out_specs=P("ex", None),
        check_vma=False,
    )
```

```python
import math

import jax
import jax.numpy as jnp
from jax import lax
from jax.experimental import pallas as pl
from jax.experimental.pallas import tpu as pltpu
from jax.sharding import PartitionSpec as P


F32 = jnp.float32
BF16 = jnp.bfloat16
VMEM_LIMIT = 24 << 20
LEFT_STEP = 256
GROUP = 4
NT = (((1,), (1,)), ((), ()))
NN = (((1,), (0,)), ((), ()))


def dot(a, b, dims):
    return lax.dot_general(a, b, dims, preferred_element_type=F32)


def split(x):
    high = x.astype(BF16)
    return high, (x - high.astype(F32)).astype(BF16)


def on_chip(x):
    return pltpu.with_memory_space_constraint(x, pltpu.VMEM)


def off_chip(x):
    return pltpu.with_memory_space_constraint(x, pltpu.HBM)


def staged(arrays):
    return tuple(pltpu.VMEM(x.shape, x.dtype) for x in arrays)


def call(kernel, out_shape, flops, bytes_accessed, scratch=(), smem=0, args=(), hbm=(), hbm_out=()):
    specs = [pl.BlockSpec(memory_space=pltpu.SMEM)] * smem
    specs += [pl.BlockSpec(memory_space=pltpu.HBM if n in hbm else pltpu.VMEM) for n in range(smem, len(args))]
    if isinstance(out_shape, tuple):
        out_specs = tuple(
            pl.BlockSpec(memory_space=pltpu.HBM if n in hbm_out else pltpu.VMEM) for n in range(len(out_shape))
        )
    else:
        out_specs = pl.BlockSpec(memory_space=pltpu.VMEM)
    return pl.pallas_call(
        kernel,
        out_shape=out_shape,
        in_specs=specs,
        out_specs=out_specs,
        scratch_shapes=list(scratch),
        cost_estimate=pl.CostEstimate(flops=flops, bytes_accessed=bytes_accessed, transcendentals=0),
        compiler_params=pltpu.CompilerParams(vmem_limit_bytes=VMEM_LIMIT),
    )(*args)


def right_kernel(x_hbm, a_hbm, r_hbm, out_ref, x_ref, a_ref, r_ref, sems):
    layers = x_ref.shape[0]
    proj = r_ref.shape[1]
    small = [
        pltpu.make_async_copy(r_hbm, r_ref, sems.at[0]),
        pltpu.make_async_copy(a_hbm, a_ref, sems.at[1]),
    ]
    inputs = [pltpu.make_async_copy(x_hbm.at[l], x_ref.at[l], sems.at[2 + l]) for l in range(layers)]
    for copy in small + inputs:
        copy.start()
    for copy in small:
        copy.wait()
    mixes = []
    for l in range(layers):
        high, low = split(dot(r_ref[l], a_ref[l], NN))
        mixes.append(jnp.concatenate([high, low], axis=0))
    for l in range(layers):
        inputs[l].wait()
        rows = dot(mixes[l], x_ref[l], NT)
        out_ref[l * proj:(l + 1) * proj, :] = rows[:proj] + rows[proj:]


def pair_kernel(own_ref, other_ref, out_ref):
    total = own_ref[...] + other_ref[...]
    for p in range(out_ref.shape[0]):
        out_ref[p] = total


def left_kernel(c_hbm, l_hbm, out_ref, c_ref, l_ref, sems):
    layers, tokens, _ = c_ref.shape
    step = LEFT_STEP
    factors, pieces = [], []
    for l in range(layers):
        factors.append(pltpu.make_async_copy(l_hbm.at[l], l_ref.at[l], sems.at[l]))
        factors[-1].start()
        for t in range(0, tokens, step):
            rows = pl.ds(t, step)
            copy = pltpu.make_async_copy(c_hbm.at[l, rows], c_ref.at[l, rows], sems.at[layers + len(pieces)])
            copy.start()
            pieces.append((l, t, copy))
    for l, t, copy in pieces:
        if t == 0:
            factors[l].wait()
        copy.wait()
        out_ref[l, t:t + step, :] = dot(c_ref[l, t:t + step, :], l_ref[l], NT).astype(BF16)


def project_kernel(seq_ref, rr_ref, left_ref, out_hbm, out_ref, out_sems):
    parts, two_proj, tokens = rr_ref.shape
    layers, _, kl = left_ref.shape
    peers = out_ref.shape[0]
    proj = two_proj // layers
    half = proj // 2
    owned = kl // peers
    examples = seq_ref.shape[0]
    seq = tokens // examples
    span = GROUP * seq
    width = 2 * 128
    total = rr_ref[0]
    for p in range(1, parts):
        total = total + rr_ref[p]
    first = total[:proj]
    second = total[proj:]
    lane = lax.broadcasted_iota(jnp.int32, (proj, width), 1)
    out_lane = lax.broadcasted_iota(jnp.int32, (GROUP * half, 128), 1)
    stores = []
    for g in range(examples // GROUP):
        base = min(g * span // 128 * 128, tokens - width)
        offset = g * span - base
        x0 = first[:, base:base + width]
        x1 = second[:, base:base + width]
        if offset:
            x0 = pltpu.roll(x0, width - offset, 1)
        if offset != span:
            x1 = pltpu.roll(x1, (width + span - offset) % width, 1)
        blocks = []
        for i in range(GROUP):
            start = i * seq
            stop = start + seq_ref[g * GROUP + i]
            mask0 = (lane >= start) & (lane < stop)
            mask1 = (lane >= start + span) & (lane < stop + span)
            blocks.append(jnp.where(mask0, x0, jnp.where(mask1, x1, 0.0)))
        spread = jnp.concatenate(blocks, axis=0).astype(BF16)[:, :layers * span]
        t = g * span
        left = jnp.concatenate([left_ref[l, t:t + span, :] for l in range(layers)], axis=0)
        part = dot(spread, left, NN)
        part = part.reshape(GROUP, 2, half, kl)
        even = part[:, 0].reshape(GROUP * half, kl)
        odd = part[:, 1].reshape(GROUP * half, kl)
        r = g * GROUP * half
        for tile in range(kl // 128):
            e = even[:, tile * 128:(tile + 1) * 128]
            o = odd[:, tile * 128:(tile + 1) * 128]
            kept = jnp.where(out_lane < owned, e, o)
            moved = pltpu.roll(jnp.where(out_lane < owned, o, e), owned, 1)
            out_ref[2 * tile, r:r + GROUP * half, :] = jnp.where(out_lane < owned, kept, moved).astype(BF16)
            out_ref[2 * tile + 1, r:r + GROUP * half, :] = jnp.where(out_lane < owned, moved, kept).astype(BF16)
        rows = pl.ds(g * GROUP * half, GROUP * half)
        stores.append(pltpu.make_async_copy(out_ref.at[:, rows], out_hbm.at[:, rows], out_sems.at[g]))
        stores[-1].start()
    for store in stores:
        store.wait()


def spread_kernel(own_ref, out_hbm, sems):
    copies = [pltpu.make_async_copy(own_ref, out_hbm.at[n], sems.at[n]) for n in range(out_hbm.shape[0])]
    for copy in copies:
        copy.start()
    for copy in copies:
        copy.wait()


def join_kernel(near_ref, far_ref, out_ref):
    rows = near_ref.shape[0]
    out_ref[:rows] = near_ref[...]
    out_ref[rows:] = far_ref[...]


def valid_kernel(own_ref, half_ref, other_ref, out_ref, squares_ref):
    count = half_ref.shape[0]
    place = lax.broadcasted_iota(jnp.int32, (8, 2 * count), 1)
    core = ((place >> 8) ^ own_ref[0]) & 1
    far = ((place >> 7) ^ (own_ref[0] >> 5)) & 1
    index = (far << 7) | (((place >> 3) & 15) << 3) | (core << 2) | ((place >> 1) & 3)
    row = lax.broadcasted_iota(jnp.int32, (count, 2 * count), 0)
    squares = jnp.zeros((count, 128), F32)
    for h in range(2):
        source = jnp.where((place & 1) == h, index, -1)
        order = (row == jnp.broadcast_to(source[:1], row.shape)).astype(F32).astype(BF16)
        for q in range(4):
            lanes = slice(q * 128, (q + 1) * 128)
            rows = dot(order[:, :count], half_ref[:, lanes], NN) + dot(order[:, count:], other_ref[:, lanes], NN)
            squares = squares + rows * rows
            b = h * 4 + q
            out_ref[:, b * 128:(b + 1) * 128] = rows.astype(BF16)
    squares_ref[...] = jnp.sum(squares.T, axis=0, keepdims=True)


def product_kernel(part_ref, valid_ref, squares_ref, out_ref, sum_ref):
    peers, rows, _ = part_ref.shape
    valid_count = valid_ref.shape[0]
    examples = rows // 8
    total = part_ref[0].astype(F32)
    for p in range(1, peers):
        total = total + part_ref[p].astype(F32)
    sum_ref[...] = total
    squares = jnp.sum((total * total).reshape(examples, 8, 128), axis=1)
    squares = jnp.sum(squares, axis=1, keepdims=True)
    row = lax.broadcasted_iota(jnp.int32, (examples, valid_count), 0)
    column = lax.broadcasted_iota(jnp.int32, (examples, valid_count), 1)
    train = jnp.sum(jnp.where(row == column, squares, 0.0), axis=0, keepdims=True)
    acc = jnp.zeros((2 * examples, valid_count), F32)
    for b in range(8):
        block = sum_ref[pl.ds(b, examples, stride=8), :]
        high, low = split(block)
        both = jnp.concatenate([high, low], axis=0)
        acc = acc + dot(both, valid_ref[:, b * 128:(b + 1) * 128], NT)
    products = acc[:examples] + acc[examples:]
    tail_row = lax.broadcasted_iota(jnp.int32, (8, valid_count), 0)
    tail = jnp.where(tail_row == 0, squares_ref[...], jnp.where(tail_row == 1, train, 0.0))
    for p in range(peers):
        out_ref[p, :examples, :] = products
        out_ref[p, examples:, :] = tail


def score_kernel(scaling, part_ref, out_ref):
    peers = part_ref.shape[0]
    examples, valid_count = out_ref.shape
    total = part_ref[0]
    for p in range(1, peers):
        total = total + part_ref[p]
    products = total[:examples]
    valid = jnp.sqrt(total[examples:examples + 1] + 1e-06)
    row = lax.broadcasted_iota(jnp.int32, (examples, valid_count), 0)
    column = lax.broadcasted_iota(jnp.int32, (examples, valid_count), 1)
    train = jnp.where(row == column, total[examples + 1:examples + 2], 0.0)
    train = jnp.sqrt(jnp.sum(train, axis=1, keepdims=True) + 1e-06)
    out_ref[...] = scaling * products / (train * valid)


def scores_of(proj_inputs, out_cotangent, seq_lengths, frozen_adapter, left_factor, right_factor, valid_grads):
    layers, examples, seq, inputs = proj_inputs.shape
    width = out_cotangent.shape[3]
    peers = lax.axis_size("feat")
    groups = lax.axis_size("ex")
    proj = right_factor.shape[2]
    kl = left_factor.shape[1]
    tokens = examples * seq
    owned = kl // peers
    valid_count = valid_grads.shape[0] * groups
    scaling = math.sqrt(kl * proj)

    own_valid = valid_grads.reshape(-1, owned, 2, 8).transpose(0, 3, 2, 1).reshape(-1, owned * proj // 2)
    count = groups // 4
    (own_valid,) = call(
        spread_kernel,
        (pltpu.HBM((count,) + own_valid.shape, BF16),),
        0,
        valid_grads.size * 2 * count,
        scratch=(pltpu.SemaphoreType.DMA((count,)),),
        args=(on_chip(own_valid),),
        hbm_out=(0,),
    )
    far_bit = groups // 2
    members = [[y * far_bit + i * 2 + c for i in range(far_bit // 2)] for y in range(2) for c in range(2)]
    near = lax.all_to_all(own_valid, "ex", 0, 0, tiled=True, axis_index_groups=members)
    near = near.reshape(valid_count // 2, owned * proj // 2)
    far = lax.ppermute(near, "ex", [(i, i ^ far_bit) for i in range(groups)])
    half = call(
        join_kernel,
        jax.ShapeDtypeStruct((valid_count, owned * proj // 2), BF16),
        0,
        2 * valid_count * owned * proj,
        args=(on_chip(near), on_chip(far)),
    )
    other = lax.ppermute(half, "ex", [(i, i ^ 1) for i in range(groups)])
    own_group = jnp.full((1,), lax.axis_index("ex"), jnp.int32)
    valid, valid_squares = call(
        valid_kernel,
        (
            pltpu.VMEM((valid_count, owned * proj), BF16),
            pltpu.VMEM((1, valid_count), F32),
        ),
        2 * valid_count * valid_count * owned * proj,
        2 * valid_count * owned * proj * 2,
        smem=1,
        args=(own_group, on_chip(half), on_chip(other)),
    )

    right_in = (proj_inputs.reshape(layers, tokens, inputs), frozen_adapter, right_factor.swapaxes(1, 2))
    right_parts = call(
        right_kernel,
        jax.ShapeDtypeStruct((layers * proj, tokens), F32),
        2 * layers * tokens * inputs * 256,
        proj_inputs.size * 2,
        scratch=(*staged(right_in), pltpu.SemaphoreType.DMA((2 + layers,))),
        args=tuple(off_chip(x) for x in right_in),
        hbm=(0, 1, 2),
    )
    right_other = lax.ppermute(right_parts, "feat", [(i, i ^ 1) for i in range(peers)])
    right_parts = call(
        pair_kernel,
        jax.ShapeDtypeStruct((peers // 2, layers * proj, tokens), F32),
        layers * proj * tokens,
        4 * peers * layers * proj * tokens,
        args=(right_parts, right_other),
    )
    along_x = [[i * 2 + z for i in range(peers // 2)] for z in range(2)]
    right_parts = lax.all_to_all(right_parts, "feat", 0, 0, tiled=True, axis_index_groups=along_x)
    left_shape = (layers, tokens, kl)
    left_copies = layers * tokens // LEFT_STEP
    left_in = (out_cotangent.reshape(layers, tokens, width), left_factor)
    left_rows = call(
        left_kernel,
        pltpu.VMEM(left_shape, BF16),
        2 * layers * tokens * width * kl,
        (out_cotangent.size + left_factor.size) * 2 + layers * tokens * kl * 2,
        scratch=(*staged(left_in), pltpu.SemaphoreType.DMA((layers + left_copies,))),
        args=tuple(off_chip(x) for x in left_in),
        hbm=(0, 1),
    )
    parts_shape = (peers, examples * 8, 128)
    (parts,) = call(
        project_kernel,
        (pltpu.HBM(parts_shape, BF16),),
        2 * layers * tokens * kl * 256,
        layers * tokens * kl * 4,
        scratch=(pltpu.VMEM(parts_shape, BF16), pltpu.SemaphoreType.DMA((examples // GROUP,))),
        hbm_out=(0,),
        smem=1,
        args=(seq_lengths, on_chip(right_parts), on_chip(left_rows)),
    )
    parts = lax.all_to_all(parts, "feat", 0, 0, tiled=True)
    products = call(
        product_kernel,
        pltpu.VMEM((peers, examples + 8, valid_count), F32),
        4 * examples * valid_count * owned * proj,
        parts.size * 2 + valid.size * 2,
        scratch=(pltpu.VMEM((examples * 8, 128), F32),),
        args=(on_chip(parts), on_chip(valid), on_chip(valid_squares)),
    )
    products = lax.all_to_all(products, "feat", 0, 0, tiled=True)

    def score(part_ref, out_ref):
        score_kernel(scaling, part_ref, out_ref)

    return call(
        score,
        jax.ShapeDtypeStruct((examples, valid_count), F32),
        examples * valid_count * 16,
        products.size * 4,
        args=(on_chip(products),),
    )


def solution(mesh):
    return jax.shard_map(
        scores_of,
        mesh=mesh,
        in_specs=(
            P(None, "ex", None, "feat"),
            P(None, "ex", None, "feat"),
            P("ex"),
            P(None, None, "feat"),
            P(None, None, "feat"),
            P(),
            P("ex", "feat"),
        ),
        out_specs=P("ex", None),
        check_vma=False,
    )
```
